256 devices in a mesh: seq: 8 (over z), expert: 8 (over y, core), mp: 4 (over x).
Axes of the slice: x: 4, y: 4, z: 8, core: 2. Of those that a mesh axis runs over, the one named last changes fastest.
Arguments:
- tokens: bfloat16 [2048, 6144], P(('seq', 'expert', 'mp')), may hold values from -6 to 6
- out_grad: bfloat16 [2048, 6144], P(('seq', 'expert', 'mp')), may hold values from -3 to 3
- kept_mask: int32 [2048], P(('seq', 'expert', 'mp')), may hold values 0 or 1
- routes: int32 [2048, 2], P(('seq', 'expert', 'mp')), may hold values from 0 to 7, all different within a row; in each aligned block of 8 rows (0 to 7, 8 to 15, ...) at most 3 rows name the same one
- router: bfloat16 [6144, 8], replicated, may hold values from -0.078125 to 0.078125
- gate_weight: bfloat16 [8, 6144, 8192], P('expert', None, ('seq', 'mp')), may hold values from -0.078125 to 0.078125
- up_weight: bfloat16 [8, 6144, 8192], P('expert', None, ('seq', 'mp')), may hold values from -0.078125 to 0.078125
- down_weight: bfloat16 [8, 8192, 6144], P('expert', ('seq', 'mp')), may hold values from -0.0625 to 0.0625
Outputs:
- d_tokens: bfloat16 [2048, 6144], P(('seq', 'expert', 'mp'))
- gate_grad: float32 [2048, 2], P(('seq', 'expert', 'mp'))
The draws below stay inside these ranges and needn't reach their ends.
Inputs may be any that keep to these rules, and one draw needn't show every extreme that they name: `routes`: among the 8 rows of one device, at most 3 name any one expert, and in every draw some expert is named by exactly 3 rows of some device.
All inputs are finite; a program needn't handle non-finite values. No bound on the sum of `kept_mask` on one device may be relied on, other than what follows from the above.
Results may differ from the reference program's by a relative error of at most 0.02.
Values may be sent and summed in bfloat16 or wider, within the bound.
A program may use at most 128 MiB of HBM per device.

```python
import math
import jax
import jax.numpy as jnp
import numpy as np
from jax import lax

D = 6144
FF = 8192
TOK_DEV = 8
EXPERTS = 8
TOKENS = 2048
CAP = 3
N_SEQ = 8
N_MP = 4


def with_ends(result, key, smallest, high):
    spot = [jax.random.randint(jax.random.fold_in(key, axis), (), 0, length) for axis, length in enumerate(result.shape)]
    longest = result.shape.index(max(result.shape))
    next_to = spot[:longest] + [(spot[longest] + 1) % result.shape[longest]] + spot[longest + 1:]
    return result.at[tuple(spot)].set(smallest).at[tuple(next_to)].set(high)


def steps_of(own_key, dims, shards, smallest, largest):
    factor_of = 1.0
    for dim, shards_of in shards:
        steps = jax.random.uniform(jax.random.fold_in(jax.random.fold_in(own_key, 6), dim), (shards_of,), jnp.float32, smallest / len(shards), largest / len(shards))
        factor_of = factor_of * jnp.repeat(jnp.exp(steps), dims[dim] // shards_of).reshape((-1,) + (1,) * (len(dims) - 1 - dim))
    return factor_of


def deal_out(rng, own, number, rows, number_of, top, most, slope):
    ranking = jax.random.permutation(rng, number_of)
    crowded, usual = shares(number_of, rows * top, most, slope, True), shares(number_of, rows * top, most, slope, False)
    places = jnp.arange(number_of)

    def named(tallies, offset_by):
        used = int((tallies > 0).sum())
        fixed = max(1, used // 4)
        passed = fixed + (places - fixed + offset_by * (used - fixed)) % max(1, number_of - fixed)
        return jnp.zeros((number_of,), jnp.int32).at[ranking[jnp.where(places < fixed, places, passed)]].set(jnp.asarray(tallies, jnp.int32))

    tallies = jnp.where(number % 4 == 0, named(crowded, number // 4), named(usual, number - number // 4 - 1))
    mixed = jax.random.permutation(jax.random.fold_in(own, 3), number_of)
    giver, receiver = mixed[0:number_of // 2 * 2:2], mixed[1:number_of // 2 * 2:2]
    room = jnp.minimum(tallies[giver] - 1, most - tallies[receiver]) // 2
    room = jnp.where((giver == ranking[0]) | (receiver == ranking[0]) | (tallies[receiver] == 0), 0, jnp.maximum(room, 0))
    passed = jax.random.randint(jax.random.fold_in(own, 4), (number_of // 2,), 0, 1 << 20) % (room + 1)
    tallies = tallies.at[giver].add(-passed).at[receiver].add(passed)
    members = jnp.searchsorted(jnp.cumsum(tallies), jnp.arange(rows * top), side="right").astype(jnp.int32)
    table = members.reshape(top, rows).T
    table = table[jax.random.permutation(jax.random.fold_in(own, 1), rows)]
    offset_by = jax.random.randint(jax.random.fold_in(own, 2), (rows, 1), 0, top)
    return jnp.take_along_axis(table, (jnp.arange(top)[None, :] + offset_by) % top, axis=1)


def shares(amount, total, limit, slope, full):
    portions = [(1 << 20) // math.isqrt(standing ** slope) + 1 for standing in range(1, amount + 1)]
    largest = limit if full else min(limit, max(-(-total // amount), total * portions[0] // sum(portions)))
    least = 1 if total - largest >= amount - 1 else 0
    holding, surplus = [largest] + [least] * (amount - 1), total - largest - least * (amount - 1)
    while surplus > 0:
        free = [i for i in range(1, amount) if holding[i] < largest] or [i for i in range(1, amount) if holding[i] < limit]
        pool, remaining = sum([portions[i] for i in free]), surplus
        for i in free:
            addition = min(limit - holding[i], max(1, remaining * portions[i] // pool), surplus)
            holding[i] = holding[i] + addition
            surplus = surplus - addition
    return np.array(holding)


def noise(rng, dims, scale, bound, shards=(), kind=jnp.bfloat16):
    gain = steps_of(rng, dims, shards, -0.22, 0.18) if shards else 1.0
    entries = jax.random.normal(rng, dims, jnp.float32) * scale * gain
    return jnp.minimum(jnp.maximum(entries, -bound), bound).astype(kind)


def setup_inputs(seed: int = 0) -> dict:
    key_list = jax.random.split(jax.random.key(seed), 9)
    tokens = noise(key_list[0], (TOKENS, D), 1.0, 6.0, ((0, 256),))
    out_grad = noise(key_list[1], (TOKENS, D), 0.5, 3.0, ((0, 256),))
    kept_mask = with_ends((jax.random.randint(key_list[2], (TOKENS,), 0, 5) < 4).astype(jnp.int32), jax.random.fold_in(key_list[2], 1), 0, 1)
    routes_keys = jax.random.split(jax.random.fold_in(key_list[3], 1), TOKENS // TOK_DEV)
    routes_turns = jax.random.permutation(jax.random.fold_in(key_list[3], 3), TOKENS // TOK_DEV)
    routes = jax.vmap(lambda own, number: deal_out(jax.random.fold_in(key_list[3], 2), own, number, TOK_DEV, EXPERTS, 2, CAP, 1))(routes_keys, routes_turns).reshape((TOKENS, 2))
    router = noise(key_list[4], (D, EXPERTS), D ** -0.5, 0.078125)
    gate_weight = noise(key_list[5], (EXPERTS, D, FF), D ** -0.5, 0.078125, ((0, 8), (2, 32)))
    up_weight = noise(key_list[6], (EXPERTS, D, FF), D ** -0.5, 0.078125, ((0, 8), (2, 32)))
    down_weight = noise(key_list[7], (EXPERTS, FF, D), FF ** -0.5, 0.0625, ((0, 8), (1, 32)))
    return dict(tokens=tokens, out_grad=out_grad, kept_mask=kept_mask, routes=routes, router=router, gate_weight=gate_weight, up_weight=up_weight, down_weight=down_weight)


def expert_pass(token_rows, grad_rows, gate_rows, gate_mat, up_mat, down_mat):
    pre_gate = jnp.dot(token_rows, gate_mat, preferred_element_type=jnp.float32)
    pre_up = jnp.dot(token_rows, up_mat, preferred_element_type=jnp.float32)
    sigma = jax.nn.sigmoid(pre_gate)
    act = pre_gate * sigma
    hidden = act * pre_up
    grad_hidden = jnp.dot(grad_rows, down_mat.T, preferred_element_type=jnp.float32)
    gate_dot = jnp.sum(grad_hidden * hidden, axis=1)
    scaled = gate_rows.astype(jnp.float32)[:, None] * grad_hidden
    grad_gate = (scaled * pre_up * sigma * (1.0 + pre_gate * (1.0 - sigma))).astype(jnp.bfloat16)
    grad_up = (scaled * act).astype(jnp.bfloat16)
    blocks = N_SEQ * N_MP
    width = FF // blocks

    def add_block(total, block_index):
        start = (block_index * width).astype(jnp.int32)
        left_gate = lax.dynamic_slice_in_dim(grad_gate, start, width, 1)
        left_up = lax.dynamic_slice_in_dim(grad_up, start, width, 1)
        right_gate = lax.dynamic_slice_in_dim(gate_mat, start, width, 1)
        right_up = lax.dynamic_slice_in_dim(up_mat, start, width, 1)
        part = jnp.dot(left_gate, right_gate.T, preferred_element_type=jnp.float32)
        part = part + jnp.dot(left_up, right_up.T, preferred_element_type=jnp.float32)
        rounded = lax.optimization_barrier(part.astype(jnp.bfloat16))
        return total + rounded.astype(jnp.float32), None

    start_total = jnp.zeros((token_rows.shape[0], token_rows.shape[1]), jnp.float32)
    expert_grad, _ = lax.scan(add_block, start_total, jnp.arange(blocks, dtype=jnp.int32))
    return expert_grad, gate_dot


def reference(tokens, out_grad, kept_mask, routes, router, gate_weight, up_weight, down_weight):
    logits = jnp.dot(tokens, router, preferred_element_type=jnp.float32)
    first_id = routes[:, 0].astype(jnp.int32)
    second_id = routes[:, 1].astype(jnp.int32)
    first_logit = jnp.take_along_axis(logits, first_id[:, None], axis=1)[:, 0]
    second_logit = jnp.take_along_axis(logits, second_id[:, None], axis=1)[:, 0]
    gate_first = jax.nn.sigmoid(first_logit - second_logit)
    gate_second = jax.nn.sigmoid(second_logit - first_logit)
    keep_rows = kept_mask.astype(jnp.float32)
    most_rows = (TOKENS // TOK_DEV) * CAP

    def per_expert(carry, inputs):
        grad_total, dot_total = carry
        expert_id, gate_mat, up_mat, down_mat = inputs
        hit = (kept_mask == 1) & ((first_id == expert_id) | (second_id == expert_id))
        hit = hit.astype(jnp.int32)
        order = jnp.argsort(1 - hit, stable=True)[:most_rows].astype(jnp.int32)
        live = hit[order].astype(jnp.float32)
        gate_rows = jnp.where(first_id == expert_id, gate_first, gate_second).astype(jnp.bfloat16)[order]
        expert_grad, gate_dot = expert_pass(tokens[order], out_grad[order], gate_rows, gate_mat, up_mat, down_mat)
        grad_total = grad_total.at[order].add(expert_grad * live[:, None])
        dot_total = dot_total.at[order, expert_id].add(gate_dot * live)
        return (grad_total, dot_total), None

    start = (jnp.zeros((TOKENS, D), jnp.float32), jnp.zeros((TOKENS, EXPERTS), jnp.float32))
    (grad_total, dot_total), _ = lax.scan(per_expert, start, (jnp.arange(EXPERTS, dtype=jnp.int32), gate_weight, up_weight, down_weight))
    dot_first = jnp.take_along_axis(dot_total, first_id[:, None], axis=1)[:, 0]
    dot_second = jnp.take_along_axis(dot_total, second_id[:, None], axis=1)[:, 0]
    product = gate_first * gate_second * keep_rows
    grad_first = product * (dot_first - dot_second)
    grad_second = product * (dot_second - dot_first)
    columns = lax.broadcasted_iota(jnp.int32, (TOKENS, EXPERTS), 1)
    first_hot = (first_id[:, None] == columns).astype(jnp.float32)
    second_hot = (second_id[:, None] == columns).astype(jnp.float32)
    logit_grad = first_hot * grad_first[:, None] + second_hot * grad_second[:, None]
    router_term = jnp.dot(logit_grad, router.astype(jnp.float32).T, precision=lax.Precision.HIGHEST)
    d_tokens = ((grad_total + router_term) * keep_rows[:, None]).astype(jnp.bfloat16)
    gate_grad = jnp.stack([grad_first, grad_second], axis=1)
    return d_tokens, gate_grad
```

```python
import functools

import jax
import jax.numpy as jnp
from jax import lax
from jax.experimental import pallas as pl
from jax.experimental.pallas import tpu as pltpu
from jax.sharding import PartitionSpec as P

MESH = pl.DeviceIdType.MESH
BF = jnp.bfloat16
F32 = jnp.float32
RING = 32
GROUP = 4
SPAN = 8


def div(a, b):
    return a // b if isinstance(a, int) else lax.div(a, jnp.int32(b))


def rem(a, b):
    return a % b if isinstance(a, int) else lax.rem(a, jnp.int32(b))


def place(cycle, z, x):
    if cycle == 0:
        return 4 * z + rem(x + z, 4)
    turn = rem(z + 5 * x, 8)
    return 4 * x + 16 * div(turn, 4) + rem(turn, 4)


def coords(cycle, q):
    a, b = div(q, 4), rem(q, 4)
    if cycle == 0:
        return a, rem(b - a + 8, 4)
    return rem(3 * a + b, 8), rem(a, 4)


def peer(z, x):
    return {"seq": z, "mp": x}


def dispatch_kernel(count, send_ref, recv_ref, send_sem, recv_sem, own_sem):
    z, e, x = lax.axis_index("seq"), lax.axis_index("expert"), lax.axis_index("mp")
    other = x + 1 - 2 * rem(x, 2)
    kind = rem(x + z, 2)
    slot = rem(x, 2) * count + e

    def target(j, mine):
        return {"seq": z, "expert": rem(e + j, count), "mp": x if mine else other}

    barrier = pltpu.get_barrier_semaphore()
    for j in range(count):
        if j:
            pl.semaphore_signal(barrier, inc=1, device_id=target(j, True), device_id_type=MESH)
        pl.semaphore_signal(barrier, inc=1, device_id=target(j, False), device_id_type=MESH)
    pl.semaphore_wait(barrier, 2 * count - 1)

    local = pltpu.make_async_copy(send_ref.at[kind, e], recv_ref.at[slot], own_sem)
    local.start()
    copies = []
    for j in range(count):
        for mine in (True, False):
            if mine and j == 0:
                continue
            copy = pltpu.make_async_remote_copy(
                src_ref=send_ref.at[kind if mine else 1 - kind, rem(e + j, count)],
                dst_ref=recv_ref.at[slot],
                send_sem=send_sem.at[2 * j + (0 if mine else 1)],
                recv_sem=recv_sem.at[slot],
                device_id=target(j, mine),
                device_id_type=MESH,
            )
            copy.start()
            copies.append(copy)
    local.wait()
    for j in range(count):
        for mine in (True, False):
            if mine and j == 0:
                continue
            source = rem(x if mine else other, 2) * count + rem(e + j, count)
            pltpu.make_async_remote_copy(
                src_ref=recv_ref.at[source],
                dst_ref=recv_ref.at[source],
                send_sem=send_sem.at[2 * j + (0 if mine else 1)],
                recv_sem=recv_sem.at[source],
                device_id=target(j, mine),
                device_id_type=MESH,
            ).wait_recv()
    for copy in copies:
        copy.wait_send()


def dispatch(send, count):
    shape = send.shape[2:]
    return pl.pallas_call(
        functools.partial(dispatch_kernel, count),
        out_shape=jax.ShapeDtypeStruct((2 * count,) + shape, send.dtype),
        in_specs=[pl.BlockSpec(memory_space=pltpu.VMEM)],
        out_specs=pl.BlockSpec(memory_space=pltpu.VMEM),
        scratch_shapes=[
            pltpu.SemaphoreType.DMA((2 * count,)),
            pltpu.SemaphoreType.DMA((2 * count,)),
            pltpu.SemaphoreType.DMA,
        ],
        compiler_params=pltpu.CompilerParams(
            collective_id=0, has_side_effects=True, vmem_limit_bytes=16 << 20
        ),
        name="dispatch",
    )(send)


def giveback_kernel(count, send_ref, recv_ref, send_sem, recv_sem, own_sem):
    z, e, x = lax.axis_index("seq"), lax.axis_index("expert"), lax.axis_index("mp")
    other = x + 1 - 2 * rem(x, 2)
    kind = rem(x + z, 2)

    def target(j, mine):
        return {"seq": z, "expert": rem(e + j, count), "mp": x if mine else other}

    barrier = pltpu.get_barrier_semaphore()
    for j in range(count):
        if j:
            pl.semaphore_signal(barrier, inc=1, device_id=target(j, True), device_id_type=MESH)
        pl.semaphore_signal(barrier, inc=1, device_id=target(j, False), device_id_type=MESH)
    pl.semaphore_wait(barrier, 2 * count - 1)

    local = pltpu.make_async_copy(send_ref.at[rem(x, 2) * count + e], recv_ref.at[kind, e], own_sem)
    local.start()
    copies = []
    for j in range(count):
        for mine in (True, False):
            if mine and j == 0:
                continue
            copy = pltpu.make_async_remote_copy(
                src_ref=send_ref.at[rem(x if mine else other, 2) * count + rem(e + j, count)],
                dst_ref=recv_ref.at[kind, e],
                send_sem=send_sem.at[2 * j + (0 if mine else 1)],
                recv_sem=recv_sem.at[kind * count + e],
                device_id=target(j, mine),
                device_id_type=MESH,
            )
            copy.start()
            copies.append(copy)
    local.wait()
    for j in range(count):
        for mine in (True, False):
            if mine and j == 0:
                continue
            half = kind if mine else 1 - kind
            source = rem(e + j, count)
            pltpu.make_async_remote_copy(
                src_ref=recv_ref.at[half, source],
                dst_ref=recv_ref.at[half, source],
                send_sem=send_sem.at[2 * j + (0 if mine else 1)],
                recv_sem=recv_sem.at[half * count + source],
                device_id=target(j, mine),
                device_id_type=MESH,
            ).wait_recv()
    for copy in copies:
        copy.wait_send()


def giveback(send, count):
    shape = send.shape[1:]
    return pl.pallas_call(
        functools.partial(giveback_kernel, count),
        out_shape=jax.ShapeDtypeStruct((2, count) + shape, send.dtype),
        in_specs=[pl.BlockSpec(memory_space=pltpu.VMEM)],
        out_specs=pl.BlockSpec(memory_space=pltpu.VMEM),
        scratch_shapes=[
            pltpu.SemaphoreType.DMA((2 * count,)),
            pltpu.SemaphoreType.DMA((2 * count,)),
            pltpu.SemaphoreType.DMA,
        ],
        compiler_params=pltpu.CompilerParams(
            collective_id=1, has_side_effects=True, vmem_limit_bytes=16 << 20
        ),
        name="giveback",
    )(send)


def dot_nt(a, b, **kwargs):
    return lax.dot_general(a, b, (((1,), (1,)), ((), ())), preferred_element_type=F32, **kwargs)


def experts_kernel(
    own_ref, wg_hbm, wu_hbm, wd_hbm, out_ref, dot_ref,
    xs, running, first, local, acc_t, acc_g, grads, dots, dot_slots, wg, wu, wd,
    w_sem, ag_send, ag_recv, rs_send, rs_recv, dot_send, dot_recv,
):
    rows, quarter = own_ref.shape[1], own_ref.shape[2]
    hidden = wg.shape[1]
    part = quarter // 2
    half = 4 * part
    z, x = lax.axis_index("seq"), lax.axis_index("mp")
    spot = [place(c, z, x) for c in range(2)]
    after = [coords(c, rem(spot[c] + 1, RING)) for c in range(2)]
    before = [coords(c, rem(spot[c] + RING - 1, RING)) for c in range(2)]
    to = [peer(*after[0]), peer(*before[0]), peer(*after[1]), peer(*before[1])]

    loads = [
        pltpu.make_async_copy(wg_hbm.at[0], wg, w_sem.at[0]),
        pltpu.make_async_copy(wu_hbm.at[0], wu, w_sem.at[1]),
    ]
    for r in range(4):
        loads.append(pltpu.make_async_copy(wd_hbm.at[0, :, pl.ds(r * quarter, quarter)], wd.at[r], w_sem.at[2 + r]))

    barrier = pltpu.get_barrier_semaphore()
    for r in range(4):
        pl.semaphore_signal(barrier, inc=1, device_id=to[r], device_id_type=MESH)
    for r in range(4):
        xs[r, spot[r // 2]] = own_ref[r]
    pl.semaphore_wait(barrier, 4)

    def held(r, s):
        c = r // 2
        return rem(spot[c] + RING - s, RING) if r % 2 == 0 else rem(spot[c] + s, RING)

    def gather(r, s, slot_step):
        block = xs.at[r, held(r, slot_step)]
        return pltpu.make_async_remote_copy(
            src_ref=block, dst_ref=block, send_sem=ag_send.at[r, s], recv_sem=ag_recv.at[r, s],
            device_id=to[r], device_id_type=MESH,
        )

    for r in range(4):
        gather(r, 1, 0).start()
    for load in loads:
        load.start()
    acc_t[...] = jnp.zeros_like(acc_t)
    acc_g[...] = jnp.zeros_like(acc_g)
    for load in loads:
        load.wait()

    def forward_unit(unit):
        b = div(unit, 8)
        r = div(rem(unit, 8), 2)
        kind = rem(unit, 2)
        c, back = div(r, 2), rem(r, 2)
        p = spot[0] * (1 - c) + spot[1] * c
        begin = pl.multiple_of(r * quarter, quarter)

        @pl.when(kind == 0)
        def _():
            base = jnp.where(back == 0, div(p, 2) - GROUP * b - 3, div(p + 1, 2) + GROUP * b) + 32
            lhs = jnp.concatenate([xs[r, 2 * rem(base + i, 16)] for i in range(GROUP)], axis=0)
            gate = jnp.dot(lhs, wg[pl.ds(begin, quarter), :], preferred_element_type=F32)
            up = jnp.dot(lhs, wu[pl.ds(begin, quarter), :], preferred_element_type=F32)
            for i in range(GROUP):
                t = rem(base + i, 16)
                acc_t[c, t, :, :hidden] += gate[i * rows:(i + 1) * rows]
                acc_t[c, t, :, hidden:] += up[i * rows:(i + 1) * rows]

        @pl.when(kind == 1)
        def _():
            base = jnp.where(back == 0, div(p + 1, 2) - 1 - GROUP * b - 3, div(p, 2) + GROUP * b) + 32
            lhs = jnp.concatenate([xs[r, 2 * rem(base + i, 16) + 1] for i in range(GROUP)], axis=0)
            grad = dot_nt(lhs, wd[r])
            for i in range(GROUP):
                acc_g[c, rem(base + i, 16)] += grad[i * rows:(i + 1) * rows]

    def ag_step(s, carry):
        for r in range(4):
            gather(r, s, s).wait_recv()

            @pl.when(s < RING - 1)
            def _():
                gather(r, s + 1, s).start()

        @pl.when(s >= SPAN)
        def _():
            forward_unit(s - SPAN)

        return carry

    lax.fori_loop(1, RING, ag_step, 0)

    def tail_unit(u, carry):
        forward_unit(u + 3 * SPAN)
        return carry

    lax.fori_loop(0, SPAN, tail_unit, 0)

    ones = jnp.ones((8, 128), F32)
    for pair in range(16):
        pz, px = pair // 2, 2 * (pair % 2)
        holders = [(pz, px), (pz, px + 1)]
        if (px + pz) % 2:
            holders = holders[::-1]
        t = [place(c, *holders[0]) // 2 for c in range(2)]
        g = [place(c, *holders[1]) // 2 for c in range(2)]
        pre_gate = acc_t[0, t[0], :, :hidden] + acc_t[1, t[1], :, :hidden]
        pre_up = acc_t[0, t[0], :, hidden:] + acc_t[1, t[1], :, hidden:]
        grad_hidden = acc_g[0, g[0]] + acc_g[1, g[1]]
        sigma = jax.nn.sigmoid(pre_gate)
        act = pre_gate * sigma
        inner = grad_hidden * act * pre_up
        grad_gate = (grad_hidden * pre_up * sigma * (1.0 + pre_gate * (1.0 - sigma))).astype(BF)
        grad_up = (grad_hidden * act).astype(BF)
        for c in range(2):
            for q in (2 * t[c], 2 * g[c] + 1):
                grads[c, q, :, :hidden] = grad_gate
                grads[c, q, :, hidden:] = grad_up
        folded = inner[:, 0:128]
        for i in range(1, hidden // 128):
            folded = folded + inner[:, i * 128:(i + 1) * 128]
        sums = dot_nt(ones, folded, precision=lax.Precision.HIGHEST)
        for q in (2 * t[0], 2 * g[0] + 1):
            dots[q, :, :rows] = sums

    def backward_unit(unit):
        b = div(unit, 8)
        r = div(rem(unit, 8), 2)
        kind = rem(unit, 2)
        c, back = div(r, 2), rem(r, 2)
        p = spot[0] * (1 - c) + spot[1] * c
        j0 = rem(p + 1 + kind, 2)
        steps = [SPAN * b + j0 + 2 * i for i in range(GROUP)]
        where = [jnp.where(back == 0, rem(p + 2 * RING - 1 - s, RING), rem(p + 1 + s, RING)) for s in steps]
        lhs = jnp.concatenate([grads[c, q] for q in where], axis=0)
        begin = pl.multiple_of(kind * half + r * part, part)
        y = dot_nt(lhs[:, :hidden], wg[pl.ds(begin, part), :]) + dot_nt(lhs[:, hidden:], wu[pl.ds(begin, part), :])
        for i in range(GROUP):
            local[r, rem(steps[i], 2 * SPAN)] = y[i * rows:(i + 1) * rows].astype(local.dtype)

    def head_unit(u, carry):
        backward_unit(u)
        return carry

    lax.fori_loop(0, SPAN, head_unit, 0)

    def scatter(r, s, src):
        return pltpu.make_async_remote_copy(
            src_ref=src, dst_ref=running.at[r, s], send_sem=rs_send.at[r, s], recv_sem=rs_recv.at[r, s],
            device_id=to[r], device_id_type=MESH,
        )

    def dot_copy(s, src):
        return pltpu.make_async_remote_copy(
            src_ref=src, dst_ref=dot_slots.at[s], send_sem=dot_send.at[s], recv_sem=dot_recv.at[s],
            device_id=to[0], device_id_type=MESH,
        )

    def dest(s):
        return rem(spot[0] + 2 * RING - 1 - s, RING)

    for r in range(4):
        first[r] = local[r, 0].astype(BF)
        scatter(r, 0, first.at[r]).start()
    dot_copy(0, dots.at[dest(0)]).start()
    backward_unit(jnp.int32(SPAN))

    def rs_step(s, carry):
        for r in range(4):
            scatter(r, s - 1, running.at[r, s - 1]).wait_recv()
            total = running[r, s - 1].astype(F32) + local[r, rem(s, 2 * SPAN)].astype(F32)
            running[r, s - 1] = total.astype(BF)
            scatter(r, s, running.at[r, s - 1]).start()
        dot_copy(s - 1, dot_slots.at[s - 1]).wait_recv()
        dot_slots[s - 1] = dot_slots[s - 1] + dots[dest(s)]
        dot_copy(s, dot_slots.at[s - 1]).start()

        @pl.when(s < 3 * SPAN)
        def _():
            backward_unit(s + SPAN)

        return carry

    lax.fori_loop(1, RING - 1, rs_step, 0)
    last = RING - 2
    for r in range(4):
        scatter(r, last, running.at[r, last]).wait_recv()
        out_ref[r] = (running[r, last].astype(F32) + local[r, (RING - 1) % (2 * SPAN)].astype(F32)).astype(BF)
    dot_copy(last, dot_slots.at[last]).wait_recv()
    dot_ref[...] = dot_slots[last] + dots[dest(RING - 1)]

    def drain(s, carry):
        for r in range(4):
            gather(r, s + 1, s).wait_send()
            scatter(r, s, running.at[r, s]).wait_send()
        dot_copy(s, dot_slots.at[s]).wait_send()
        return carry

    lax.fori_loop(0, RING - 1, drain, 0)


def run_experts(own, gate_weight, up_weight, down_weight):
    rows, quarter = own.shape[1:]
    width, hidden = gate_weight.shape[1:]
    part = quarter // 2
    vmem = pl.BlockSpec(memory_space=pltpu.VMEM)
    hbm = pl.BlockSpec(memory_space=pl.ANY)
    return pl.pallas_call(
        experts_kernel,
        out_shape=(
            jax.ShapeDtypeStruct((4, rows, part), BF),
            jax.ShapeDtypeStruct((8, 128), F32),
        ),
        in_specs=[vmem, hbm, hbm, hbm],
        out_specs=(vmem, vmem),
        scratch_shapes=[
            pltpu.VMEM((4, RING, rows, quarter), BF),
            pltpu.VMEM((4, RING - 1, rows, part), BF),
            pltpu.VMEM((4, rows, part), BF),
            pltpu.VMEM((4, 2 * SPAN, rows, part), BF),
            pltpu.VMEM((2, 16, rows, 2 * hidden), F32),
            pltpu.VMEM((2, 16, rows, hidden), F32),
            pltpu.VMEM((2, RING, rows, 2 * hidden), BF),
            pltpu.VMEM((RING, 8, 128), F32),
            pltpu.VMEM((RING, 8, 128), F32),
            pltpu.VMEM((width, hidden), BF),
            pltpu.VMEM((width, hidden), BF),
            pltpu.VMEM((4, hidden, quarter), BF),
            pltpu.SemaphoreType.DMA((6,)),
            pltpu.SemaphoreType.DMA((4, RING)),
            pltpu.SemaphoreType.DMA((4, RING)),
            pltpu.SemaphoreType.DMA((4, RING)),
            pltpu.SemaphoreType.DMA((4, RING)),
            pltpu.SemaphoreType.DMA((RING,)),
            pltpu.SemaphoreType.DMA((RING,)),
        ],
        compiler_params=pltpu.CompilerParams(
            collective_id=2, has_side_effects=True, vmem_limit_bytes=62 << 20
        ),
        name="experts",
    )(own, gate_weight, up_weight, down_weight)


def on_device(tokens, out_grad, kept_mask, routes, router, gate_weight, up_weight, down_weight):
    row_count, width = tokens.shape
    count = lax.axis_size("expert")
    capacity = 3 * row_count // 8
    columns = lax.broadcasted_iota(jnp.int32, (row_count, count), 1)
    first_hot = (routes[:, 0:1] == columns).astype(F32)
    second_hot = (routes[:, 1:2] == columns).astype(F32)
    keep_rows = kept_mask.astype(F32)
    chosen = ((first_hot + second_hot) * keep_rows[:, None]).astype(jnp.int32)
    position = jnp.cumsum(chosen, axis=0) - 1
    slot_iota = lax.broadcasted_iota(jnp.int32, (row_count, count, capacity), 2)
    select_mask = (chosen[:, :, None] == 1) & (position[:, :, None] == slot_iota)
    select_bf = select_mask.astype(BF)
    select_full = select_mask.astype(F32)
    both = jnp.stack([tokens, out_grad])
    send = jnp.einsum("tec,ktd->kecd", select_bf, both, preferred_element_type=F32).astype(BF)
    got = dispatch(send, count)
    own = got.reshape(2 * count * capacity, 4, width // 4).transpose(1, 0, 2)
    sums, dot_sums = run_experts(own, gate_weight, up_weight, down_weight)
    sums = sums.transpose(1, 0, 2).reshape(2 * count, capacity, width // 2)

    dot_rows = dot_sums[0, : 2 * count * capacity].reshape(2 * count, capacity, 1)
    top = lax.reduce_precision(dot_rows, 8, 7)
    middle = lax.reduce_precision(dot_rows - top, 8, 7)
    low = lax.reduce_precision(dot_rows - top - middle, 8, 7)
    extra = jnp.concatenate([top, middle, low], axis=2).astype(BF)
    extra = jnp.pad(extra, ((0, 0), (0, 0), (0, 125)))
    back = giveback(jnp.concatenate([sums, extra], axis=2), count)

    logits = jnp.dot(tokens, router, preferred_element_type=F32)
    first_logit = jnp.sum(logits * first_hot, axis=1)
    second_logit = jnp.sum(logits * second_hot, axis=1)
    gate_first = jax.nn.sigmoid(first_logit - second_logit)
    gate_second = jax.nn.sigmoid(second_logit - first_logit)
    gate_table = (first_hot * gate_first[:, None] + second_hot * gate_second[:, None]).astype(BF)
    weigh = select_bf * gate_table[:, :, None]
    expert_sum = jnp.einsum("tec,kecd->tkd", weigh, back[..., : width // 2], preferred_element_type=F32)
    expert_sum = expert_sum.reshape(row_count, width)
    dot_parts = back[0, :, :, width // 2 : width // 2 + 3].astype(F32)
    dot_back = dot_parts[..., 0] + dot_parts[..., 1] + dot_parts[..., 2]
    dot_table = jnp.sum(select_full * dot_back[None], axis=2)
    dot_first = jnp.sum(dot_table * first_hot, axis=1)
    dot_second = jnp.sum(dot_table * second_hot, axis=1)
    product = gate_first * gate_second * keep_rows
    grad_first = product * (dot_first - dot_second)
    grad_second = product * (dot_second - dot_first)
    logit_grad = first_hot * grad_first[:, None] + second_hot * grad_second[:, None]
    router_term = jnp.dot(logit_grad, router.astype(F32).T, precision=lax.Precision.HIGHEST)
    d_tokens = ((expert_sum + router_term) * keep_rows[:, None]).astype(BF)
    gate_grad = jnp.stack([grad_first, grad_second], axis=1)
    return (d_tokens, gate_grad)


def solution(mesh):
    return jax.shard_map(
        on_device,
        mesh=mesh,
        in_specs=(
            P(("seq", "expert", "mp"), None),
            P(("seq", "expert", "mp"), None),
            P(("seq", "expert", "mp")),
            P(("seq", "expert", "mp"), None),
            P(),
            P("expert", None, ("seq", "mp")),
            P("expert", None, ("seq", "mp")),
            P("expert", ("seq", "mp"), None),
        ),
        out_specs=(P(("seq", "expert", "mp"), None), P(("seq", "expert", "mp"), None)),
        check_vma=False,
    )
```

```python
import functools

import jax
import jax.numpy as jnp
from jax import lax
from jax.experimental import pallas as pl
from jax.experimental.pallas import tpu as pltpu
from jax.sharding import PartitionSpec as P

MESH = pl.DeviceIdType.MESH
BF = jnp.bfloat16
F32 = jnp.float32
RING = 32
HOPS = 16
GROUP = 4
CHUNK = 16


def div(a, b):
    return a // b if isinstance(a, int) else lax.div(a, jnp.int32(b))


def rem(a, b):
    return a % b if isinstance(a, int) else lax.rem(a, jnp.int32(b))


def place(cycle, z, x):
    if cycle == 0:
        return 4 * z + rem(x + z, 4)
    turn = rem(z + 5 * x, 8)
    return 4 * x + 16 * div(turn, 4) + rem(turn, 4)


def coords(cycle, q):
    a, b = div(q, 4), rem(q, 4)
    if cycle == 0:
        return a, rem(b - a + 8, 4)
    return rem(3 * a + b, 8), rem(a, 4)


def peer(z, x):
    return {"seq": z, "mp": x}


def dispatch_kernel(count, send_ref, recv_ref, send_sem, recv_sem, own_sem):
    z, e, x = lax.axis_index("seq"), lax.axis_index("expert"), lax.axis_index("mp")
    other = x + 1 - 2 * rem(x, 2)
    kind = rem(x + z, 2)
    slot = rem(x, 2) * count + e

    def target(j, mine):
        return {"seq": z, "expert": rem(e + j, count), "mp": x if mine else other}

    barrier = pltpu.get_barrier_semaphore()
    for j in range(count):
        if j:
            pl.semaphore_signal(barrier, inc=1, device_id=target(j, True), device_id_type=MESH)
        pl.semaphore_signal(barrier, inc=1, device_id=target(j, False), device_id_type=MESH)
    pl.semaphore_wait(barrier, 2 * count - 1)

    local = pltpu.make_async_copy(send_ref.at[kind, e], recv_ref.at[slot], own_sem)
    local.start()
    copies = []
    for j in range(count):
        for mine in (True, False):
            if mine and j == 0:
                continue
            copy = pltpu.make_async_remote_copy(
                src_ref=send_ref.at[kind if mine else 1 - kind, rem(e + j, count)],
                dst_ref=recv_ref.at[slot],
                send_sem=send_sem.at[2 * j + (0 if mine else 1)],
                recv_sem=recv_sem.at[slot],
                device_id=target(j, mine),
                device_id_type=MESH,
            )
            copy.start()
            copies.append(copy)
    local.wait()
    for j in range(count):
        for mine in (True, False):
            if mine and j == 0:
                continue
            source = rem(x if mine else other, 2) * count + rem(e + j, count)
            pltpu.make_async_remote_copy(
                src_ref=recv_ref.at[source],
                dst_ref=recv_ref.at[source],
                send_sem=send_sem.at[2 * j + (0 if mine else 1)],
                recv_sem=recv_sem.at[source],
                device_id=target(j, mine),
                device_id_type=MESH,
            ).wait_recv()
    for copy in copies:
        copy.wait_send()


def dispatch(send, count):
    shape = send.shape[2:]
    return pl.pallas_call(
        functools.partial(dispatch_kernel, count),
        out_shape=jax.ShapeDtypeStruct((2 * count,) + shape, send.dtype),
        in_specs=[pl.BlockSpec(memory_space=pltpu.VMEM)],
        out_specs=pl.BlockSpec(memory_space=pltpu.VMEM),
        scratch_shapes=[
            pltpu.SemaphoreType.DMA((2 * count,)),
            pltpu.SemaphoreType.DMA((2 * count,)),
            pltpu.SemaphoreType.DMA,
        ],
        compiler_params=pltpu.CompilerParams(
            collective_id=0, has_side_effects=True, vmem_limit_bytes=16 << 20
        ),
        name="dispatch",
    )(send)


def giveback_kernel(count, send_ref, recv_ref, send_sem, recv_sem, own_sem):
    z, e, x = lax.axis_index("seq"), lax.axis_index("expert"), lax.axis_index("mp")
    other = x + 1 - 2 * rem(x, 2)
    kind = rem(x + z, 2)

    def target(j, mine):
        return {"seq": z, "expert": rem(e + j, count), "mp": x if mine else other}

    barrier = pltpu.get_barrier_semaphore()
    for j in range(count):
        if j:
            pl.semaphore_signal(barrier, inc=1, device_id=target(j, True), device_id_type=MESH)
        pl.semaphore_signal(barrier, inc=1, device_id=target(j, False), device_id_type=MESH)
    pl.semaphore_wait(barrier, 2 * count - 1)

    local = pltpu.make_async_copy(send_ref.at[rem(x, 2) * count + e], recv_ref.at[kind, e], own_sem)
    local.start()
    copies = []
    for j in range(count):
        for mine in (True, False):
            if mine and j == 0:
                continue
            copy = pltpu.make_async_remote_copy(
                src_ref=send_ref.at[rem(x if mine else other, 2) * count + rem(e + j, count)],
                dst_ref=recv_ref.at[kind, e],
                send_sem=send_sem.at[2 * j + (0 if mine else 1)],
                recv_sem=recv_sem.at[kind * count + e],
                device_id=target(j, mine),
                device_id_type=MESH,
            )
            copy.start()
            copies.append(copy)
    local.wait()
    for j in range(count):
        for mine in (True, False):
            if mine and j == 0:
                continue
            half = kind if mine else 1 - kind
            source = rem(e + j, count)
            pltpu.make_async_remote_copy(
                src_ref=recv_ref.at[half, source],
                dst_ref=recv_ref.at[half, source],
                send_sem=send_sem.at[2 * j + (0 if mine else 1)],
                recv_sem=recv_sem.at[half * count + source],
                device_id=target(j, mine),
                device_id_type=MESH,
            ).wait_recv()
    for copy in copies:
        copy.wait_send()


def giveback(send, count):
    shape = send.shape[1:]
    return pl.pallas_call(
        functools.partial(giveback_kernel, count),
        out_shape=jax.ShapeDtypeStruct((2, count) + shape, send.dtype),
        in_specs=[pl.BlockSpec(memory_space=pltpu.VMEM)],
        out_specs=pl.BlockSpec(memory_space=pltpu.VMEM),
        scratch_shapes=[
            pltpu.SemaphoreType.DMA((2 * count,)),
            pltpu.SemaphoreType.DMA((2 * count,)),
            pltpu.SemaphoreType.DMA,
        ],
        compiler_params=pltpu.CompilerParams(
            collective_id=1, has_side_effects=True, vmem_limit_bytes=16 << 20
        ),
        name="giveback",
    )(send)


def dot_nt(a, b, **kwargs):
    return lax.dot_general(a, b, (((1,), (1,)), ((), ())), preferred_element_type=F32, **kwargs)


def experts_kernel(
    own_ref, wg_hbm, wu_hbm, wd_hbm, out_ref, dot_ref,
    xs, running, local, acc_t, acc_g, grads, dots, dot_slots, wg, wu, wd,
    w_sem, ag_send, ag_recv, rs_send, rs_recv, dot_send, dot_recv,
):
    rows, share = own_ref.shape[1], own_ref.shape[2]
    hidden = wg.shape[1]
    part = share // 2
    half = 2 * part
    z, x = lax.axis_index("seq"), lax.axis_index("mp")
    spot = [place(c, z, x) for c in range(2)]
    after = [coords(c, rem(spot[c] + 1, RING)) for c in range(2)]
    before = [coords(c, rem(spot[c] + RING - 1, RING)) for c in range(2)]
    to = [peer(*after[0]), peer(*before[0]), peer(*after[1]), peer(*before[1])]

    loads = [
        pltpu.make_async_copy(wg_hbm.at[0], wg, w_sem.at[0]),
        pltpu.make_async_copy(wu_hbm.at[0], wu, w_sem.at[1]),
    ]
    for c in range(2):
        loads.append(pltpu.make_async_copy(wd_hbm.at[0, :, pl.ds(c * share, share)], wd.at[c], w_sem.at[2 + c]))

    barrier = pltpu.get_barrier_semaphore()
    for r in range(4):
        pl.semaphore_signal(barrier, inc=1, device_id=to[r], device_id_type=MESH)
    for c in range(2):
        xs[c, spot[c]] = own_ref[c]
    pl.semaphore_wait(barrier, 4)

    def held(r, s):
        c = r // 2
        return rem(spot[c] + RING - s, RING) if r % 2 == 0 else rem(spot[c] + s, RING)

    def gather(r, s, k, where, halved=False):
        lanes = pl.ds((r % 2) * part, part) if halved else slice(None)
        block = xs.at[r // 2, where, pl.ds(k * CHUNK, CHUNK), lanes]
        return pltpu.make_async_remote_copy(
            src_ref=block, dst_ref=block, send_sem=ag_send.at[r, s, k], recv_sem=ag_recv.at[r, s, k],
            device_id=to[r], device_id_type=MESH,
        )

    chunks = rows // CHUNK
    for k in range(chunks):
        for r in range(4):
            gather(r, 1, k, spot[r // 2]).start()
    for load in loads:
        load.start()
    for load in loads:
        load.wait()

    def forward_unit(unit):
        b = div(unit, 4)
        c = div(rem(unit, 4), 2)
        kind = rem(unit, 2)
        p = spot[0] * (1 - c) + spot[1] * c
        begin = pl.multiple_of(c * share, share)

        def positions(parity):
            low = p - GROUP * (b + 1)
            low = low + rem(low + parity + 2 * RING, 2) + RING
            high = p + GROUP * b
            high = high + rem(high + parity, 2)
            return [div(rem(q, RING), 2) for q in (low, low + 2, high, high + 2)]

        @pl.when(kind == 0)
        def _():
            where = positions(0)
            lhs = jnp.concatenate([xs[c, 2 * t] for t in where], axis=0)
            gate = jnp.dot(lhs, wg[pl.ds(begin, share), :], preferred_element_type=F32)
            up = jnp.dot(lhs, wu[pl.ds(begin, share), :], preferred_element_type=F32)
            for i, t in enumerate(where):
                acc_t[c, t, :, :hidden] = gate[i * rows:(i + 1) * rows]
                acc_t[c, t, :, hidden:] = up[i * rows:(i + 1) * rows]

        @pl.when(kind == 1)
        def _():
            where = positions(1)
            lhs = jnp.concatenate([xs[c, 2 * t + 1] for t in where], axis=0)
            grad = dot_nt(lhs, wd[c])
            for i, t in enumerate(where):
                acc_g[c, t] = grad[i * rows:(i + 1) * rows]

    def ag_step(s, carry):
        for k in range(chunks):
            for r in range(4):
                gather(r, s, k, held(r, s)).wait_recv()

                @pl.when(s < HOPS - 1)
                def _():
                    gather(r, s + 1, k, held(r, s)).start()

                @pl.when(s == HOPS - 1)
                def _():
                    gather(r, s + 1, k, held(r, s), True).start()

        @pl.when(s >= GROUP)
        def _():
            forward_unit(s - GROUP)

        return carry

    lax.fori_loop(1, HOPS, ag_step, 0)
    for k in range(chunks):
        for r in range(4):
            gather(r, HOPS, k, held(r, HOPS), True).wait_recv()

    def tail_unit(u, carry):
        forward_unit(u)
        return carry

    lax.fori_loop(HOPS - GROUP, HOPS, tail_unit, 0)

    ones = jnp.ones((8, 128), F32)
    for pair in range(16):
        pz, px = pair // 2, 2 * (pair % 2)
        holders = [(pz, px), (pz, px + 1)]
        if (px + pz) % 2:
            holders = holders[::-1]
        t = [place(c, *holders[0]) // 2 for c in range(2)]
        g = [place(c, *holders[1]) // 2 for c in range(2)]
        pre_gate = acc_t[0, t[0], :, :hidden] + acc_t[1, t[1], :, :hidden]
        pre_up = acc_t[0, t[0], :, hidden:] + acc_t[1, t[1], :, hidden:]
        grad_hidden = acc_g[0, g[0]] + acc_g[1, g[1]]
        sigma = jax.nn.sigmoid(pre_gate)
        act = pre_gate * sigma
        inner = grad_hidden * act * pre_up
        grad_gate = (grad_hidden * pre_up * sigma * (1.0 + pre_gate * (1.0 - sigma))).astype(BF)
        grad_up = (grad_hidden * act).astype(BF)
        for c in range(2):
            for q in (2 * t[c], 2 * g[c] + 1):
                grads[c, q, :, :hidden] = grad_gate
                grads[c, q, :, hidden:] = grad_up
        folded = inner[:, 0:128]
        for i in range(1, hidden // 128):
            folded = folded + inner[:, i * 128:(i + 1) * 128]
        sums = dot_nt(ones, folded, precision=lax.Precision.HIGHEST)
        for q in (2 * t[0], 2 * g[0] + 1):
            dots[q, :, :rows] = sums

    def dest(r, s):
        c = r // 2
        return rem(spot[c] + HOPS + RING - s, RING) if r % 2 == 0 else rem(spot[c] + HOPS + s, RING)

    def backward_unit(unit):
        b = div(unit, 4)
        c = div(rem(unit, 4), 2)
        kind = rem(unit, 2)
        p = spot[0] * (1 - c) + spot[1] * c
        low = p + HOPS + RING - GROUP * b - (GROUP - 1)
        low = low + rem(low + kind, 2)
        high = p + HOPS + GROUP * b + 1
        high = high + rem(high + kind, 2)
        where = [2 * div(rem(q, RING), 2) + kind for q in (low, low + 2, high, high + 2)]
        lhs = jnp.concatenate([grads[c, q] for q in where], axis=0)
        begin = pl.multiple_of(kind * half + c * part, part)
        y = dot_nt(lhs[:, :hidden], wg[pl.ds(begin, part), :]) + dot_nt(lhs[:, hidden:], wu[pl.ds(begin, part), :])
        for i in range(GROUP):
            local[c, where[i]] = y[i * rows:(i + 1) * rows].astype(local.dtype)

    def head_unit(u, carry):
        backward_unit(u)
        return carry

    lax.fori_loop(0, GROUP, head_unit, 0)

    def scatter(r, s, k):
        cut = pl.ds(k * CHUNK, CHUNK)
        return pltpu.make_async_remote_copy(
            src_ref=running.at[r, s - 1, cut], dst_ref=running.at[r, s, cut],
            send_sem=rs_send.at[r, s, k], recv_sem=rs_recv.at[r, s, k],
            device_id=to[r], device_id_type=MESH,
        )

    def scatter_first(r, k):
        cut, lanes = pl.ds(k * CHUNK, CHUNK), pl.ds((r % 2) * (part // 2), part // 2)
        return pltpu.make_async_remote_copy(
            src_ref=local.at[r // 2, dest(r, 0), cut, lanes], dst_ref=running.at[r, 0, cut, lanes],
            send_sem=rs_send.at[r, 0, k], recv_sem=rs_recv.at[r, 0, k],
            device_id=to[r], device_id_type=MESH,
        )

    def dot_copy(d, s, src):
        return pltpu.make_async_remote_copy(
            src_ref=src, dst_ref=dot_slots.at[d, s], send_sem=dot_send.at[d, s], recv_sem=dot_recv.at[d, s],
            device_id=to[d], device_id_type=MESH,
        )

    for k in range(chunks):
        for r in range(4):
            scatter_first(r, k).start()
    dot_copy(0, 0, dots.at[dest(0, 0)]).start()
    backward_unit(jnp.int32(GROUP))

    for k in range(chunks):
        cut = slice(k * CHUNK, (k + 1) * CHUNK)
        for r in range(4):
            mine = slice((r % 2) * (part // 2), (r % 2 + 1) * (part // 2))
            rest = slice((1 - r % 2) * (part // 2), (2 - r % 2) * (part // 2))
            scatter_first(r, k).wait_recv()
            total = running[r, 0, cut, mine].astype(F32) + local[r // 2, dest(r, 1), cut, mine].astype(F32)
            running[r, 0, cut, mine] = total.astype(BF)
            running[r, 0, cut, rest] = local[r // 2, dest(r, 1), cut, rest]
            scatter(r, 1, k).start()
    dot_copy(0, 0, dot_slots.at[0, 0]).wait_recv()
    dot_slots[0, 0] = dot_slots[0, 0] + dots[dest(0, 1)]
    dot_copy(0, 1, dot_slots.at[0, 0]).start()
    dot_copy(1, 1, dots.at[dest(1, 1)]).start()
    backward_unit(jnp.int32(GROUP + 1))

    def rs_step(s, carry):
        for k in range(chunks):
            cut = slice(k * CHUNK, (k + 1) * CHUNK)
            for r in range(4):
                scatter(r, s - 1, k).wait_recv()
                total = running[r, s - 1, cut].astype(F32) + local[r // 2, dest(r, s), cut].astype(F32)
                running[r, s - 1, cut] = total.astype(BF)
                scatter(r, s, k).start()
        for d in range(2):
            dot_copy(d, s - 1, dot_slots.at[d, s - 1]).wait_recv()
            dot_slots[d, s - 1] = dot_slots[d, s - 1] + dots[dest(d, s)]
            dot_copy(d, s, dot_slots.at[d, s - 1]).start()

        @pl.when(s < HOPS - GROUP)
        def _():
            backward_unit(s + GROUP)

        return carry

    lax.fori_loop(2, HOPS, rs_step, 0)
    last = HOPS - 1
    for k in range(chunks):
        cut = slice(k * CHUNK, (k + 1) * CHUNK)
        for c in range(2):
            scatter(2 * c, last, k).wait_recv()
            scatter(2 * c + 1, last, k).wait_recv()
            both = running[2 * c, last, cut].astype(F32) + running[2 * c + 1, last, cut].astype(F32)
            out_ref[c, cut] = (both + local[c, spot[c], cut].astype(F32)).astype(BF)
    for d in range(2):
        dot_copy(d, last, dot_slots.at[d, last]).wait_recv()
    dot_ref[...] = dot_slots[0, last] + dot_slots[1, last] + dots[spot[0]]

    for k in range(chunks):
        for r in range(4):
            gather(r, HOPS, k, held(r, HOPS - 1), True).wait_send()
            scatter_first(r, k).wait_send()
    dot_copy(0, 0, dots.at[dest(0, 0)]).wait_send()

    def drain(s, carry):
        for k in range(chunks):
            for r in range(4):
                gather(r, s, k, held(r, s - 1)).wait_send()
                scatter(r, s, k).wait_send()
        for d in range(2):
            dot_copy(d, s, dot_slots.at[d, s - 1]).wait_send()
        return carry

    lax.fori_loop(1, HOPS, drain, 0)


def run_experts(own, gate_weight, up_weight, down_weight):
    rows, share = own.shape[1:]
    width, hidden = gate_weight.shape[1:]
    part = share // 2
    chunks = rows // CHUNK
    vmem = pl.BlockSpec(memory_space=pltpu.VMEM)
    hbm = pl.BlockSpec(memory_space=pl.ANY)
    return pl.pallas_call(
        experts_kernel,
        out_shape=(
            jax.ShapeDtypeStruct((2, rows, part), BF),
            jax.ShapeDtypeStruct((8, 128), F32),
        ),
        in_specs=[vmem, hbm, hbm, hbm],
        out_specs=(vmem, vmem),
        scratch_shapes=[
            pltpu.VMEM((2, RING, rows, share), BF),
            pltpu.VMEM((4, HOPS, rows, part), BF),
            pltpu.VMEM((2, RING, rows, part), BF),
            pltpu.VMEM((2, 16, rows, 2 * hidden), F32),
            pltpu.VMEM((2, 16, rows, hidden), F32),
            pltpu.VMEM((2, RING, rows, 2 * hidden), BF),
            pltpu.VMEM((RING, 8, 128), F32),
            pltpu.VMEM((2, HOPS, 8, 128), F32),
            pltpu.VMEM((width, hidden), BF),
            pltpu.VMEM((width, hidden), BF),
            pltpu.VMEM((2, hidden, share), BF),
            pltpu.SemaphoreType.DMA((4,)),
            pltpu.SemaphoreType.DMA((4, HOPS + 1, chunks)),
            pltpu.SemaphoreType.DMA((4, HOPS + 1, chunks)),
            pltpu.SemaphoreType.DMA((4, HOPS, chunks)),
            pltpu.SemaphoreType.DMA((4, HOPS, chunks)),
            pltpu.SemaphoreType.DMA((2, HOPS)),
            pltpu.SemaphoreType.DMA((2, HOPS)),
        ],
        compiler_params=pltpu.CompilerParams(
            collective_id=2, has_side_effects=True, vmem_limit_bytes=62 << 20
        ),
        name="experts",
    )(own, gate_weight, up_weight, down_weight)


def on_device(tokens, out_grad, kept_mask, routes, router, gate_weight, up_weight, down_weight):
    row_count, width = tokens.shape
    count = lax.axis_size("expert")
    capacity = 3 * row_count // 8
    columns = lax.broadcasted_iota(jnp.int32, (row_count, count), 1)
    first_hot = (routes[:, 0:1] == columns).astype(F32)
    second_hot = (routes[:, 1:2] == columns).astype(F32)
    keep_rows = kept_mask.astype(F32)
    chosen = ((first_hot + second_hot) * keep_rows[:, None]).astype(jnp.int32)
    position = jnp.cumsum(chosen, axis=0) - 1
    slot_iota = lax.broadcasted_iota(jnp.int32, (row_count, count, capacity), 2)
    select_mask = (chosen[:, :, None] == 1) & (position[:, :, None] == slot_iota)
    select_bf = select_mask.astype(BF)
    select_full = select_mask.astype(F32)
    both = jnp.stack([tokens, out_grad])
    send = jnp.einsum("tec,ktd->kecd", select_bf, both, preferred_element_type=F32).astype(BF)
    got = dispatch(send, count)
    own = got.reshape(2 * count * capacity, 2, width // 2).transpose(1, 0, 2)
    sums, dot_sums = run_experts(own, gate_weight, up_weight, down_weight)
    sums = sums.transpose(1, 0, 2).reshape(2 * count, capacity, width // 2)

    dot_rows = dot_sums[0, : 2 * count * capacity].reshape(2 * count, capacity, 1)
    top = lax.reduce_precision(dot_rows, 8, 7)
    middle = lax.reduce_precision(dot_rows - top, 8, 7)
    low = lax.reduce_precision(dot_rows - top - middle, 8, 7)
    extra = jnp.concatenate([top, middle, low], axis=2).astype(BF)
    extra = jnp.pad(extra, ((0, 0), (0, 0), (0, 125)))
    back = giveback(jnp.concatenate([sums, extra], axis=2), count)

    logits = jnp.dot(tokens, router, preferred_element_type=F32)
    first_logit = jnp.sum(logits * first_hot, axis=1)
    second_logit = jnp.sum(logits * second_hot, axis=1)
    gate_first = jax.nn.sigmoid(first_logit - second_logit)
    gate_second = jax.nn.sigmoid(second_logit - first_logit)
    gate_table = (first_hot * gate_first[:, None] + second_hot * gate_second[:, None]).astype(BF)
    weigh = select_bf * gate_table[:, :, None]
    expert_sum = jnp.einsum("tec,kecd->tkd", weigh, back[..., : width // 2], preferred_element_type=F32)
    expert_sum = expert_sum.reshape(row_count, width)
    dot_parts = back[0, :, :, width // 2 : width // 2 + 3].astype(F32)
    dot_back = dot_parts[..., 0] + dot_parts[..., 1] + dot_parts[..., 2]
    dot_table = jnp.sum(select_full * dot_back[None], axis=2)
    dot_first = jnp.sum(dot_table * first_hot, axis=1)
    dot_second = jnp.sum(dot_table * second_hot, axis=1)
    product = gate_first * gate_second * keep_rows
    grad_first = product * (dot_first - dot_second)
    grad_second = product * (dot_second - dot_first)
    logit_grad = first_hot * grad_first[:, None] + second_hot * grad_second[:, None]
    router_term = jnp.dot(logit_grad, router.astype(F32).T, precision=lax.Precision.HIGHEST)
    d_tokens = ((expert_sum + router_term) * keep_rows[:, None]).astype(BF)
    gate_grad = jnp.stack([grad_first, grad_second], axis=1)
    return (d_tokens, gate_grad)


def solution(mesh):
    return jax.shard_map(
        on_device,
        mesh=mesh,
        in_specs=(
            P(("seq", "expert", "mp"), None),
            P(("seq", "expert", "mp"), None),
            P(("seq", "expert", "mp")),
            P(("seq", "expert", "mp"), None),
            P(),
            P("expert", None, ("seq", "mp")),
            P("expert", None, ("seq", "mp")),
            P("expert", ("seq", "mp"), None),
        ),
        out_specs=(P(("seq", "expert", "mp"), None), P(("seq", "expert", "mp"), None)),
        check_vma=False,
    )
```

```python
import functools

import jax
import jax.numpy as jnp
from jax import lax
from jax.experimental import pallas as pl
from jax.experimental.pallas import tpu as pltpu
from jax.sharding import PartitionSpec as P

MESH = pl.DeviceIdType.MESH
BF = jnp.bfloat16
F32 = jnp.float32
RING = 32
HOPS = 16
GROUP = 4


def div(a, b):
    return a // b if isinstance(a, int) else lax.div(a, jnp.int32(b))


def rem(a, b):
    return a % b if isinstance(a, int) else lax.rem(a, jnp.int32(b))


def place(cycle, z, x):
    if cycle == 0:
        return 4 * z + rem(x + z, 4)
    turn = rem(z + 5 * x, 8)
    return 4 * x + 16 * div(turn, 4) + rem(turn, 4)


def coords(cycle, q):
    a, b = div(q, 4), rem(q, 4)
    if cycle == 0:
        return a, rem(b - a + 8, 4)
    return rem(3 * a + b, 8), rem(a, 4)


def peer(z, x):
    return {"seq": z, "mp": x}


def dot_nt(a, b, **kwargs):
    return lax.dot_general(a, b, (((1,), (1,)), ((), ())), preferred_element_type=F32, **kwargs)


def experts_kernel(
    send_ref, wg_hbm, wu_hbm, wd_hbm, back_ref, back_dots,
    got, flat, leave, xs, running, local, acc_t, acc_g, grads, dots, dot_slots, dot_out, wg, wu, wd,
    w_sem, in_own, in_send, in_recv, ag_send, ag_recv, rs_send, rs_recv, dot_send, dot_recv,
    out_own, out_send, out_recv,
):
    count = send_ref.shape[1]
    rows, share = xs.shape[2], xs.shape[3]
    hidden = wg.shape[1]
    part = share // 2
    half = 2 * part
    z, e, x = lax.axis_index("seq"), lax.axis_index("expert"), lax.axis_index("mp")
    other = x + 1 - 2 * rem(x, 2)
    own_kind = rem(x + z, 2)
    spot = [place(c, z, x) for c in range(2)]
    after = [coords(c, rem(spot[c] + 1, RING)) for c in range(2)]
    before = [coords(c, rem(spot[c] + RING - 1, RING)) for c in range(2)]
    to = [peer(*after[0]), peer(*before[0]), peer(*after[1]), peer(*before[1])]

    mates = [(j, mine) for j in range(count) for mine in (True, False) if j or not mine]

    def mate(j, mine):
        return {"seq": z, "expert": rem(e + j, count), "mp": x if mine else other}

    def column_slot(j, mine):
        return rem(x if mine else other, 2) * count + rem(e + j, count)

    loads = [
        pltpu.make_async_copy(wg_hbm.at[0], wg, w_sem.at[0]),
        pltpu.make_async_copy(wu_hbm.at[0], wu, w_sem.at[1]),
    ]
    for c in range(2):
        loads.append(pltpu.make_async_copy(wd_hbm.at[0, :, pl.ds(c * share, share)], wd.at[c], w_sem.at[2 + c]))

    barrier = pltpu.get_barrier_semaphore()
    for j, mine in mates:
        pl.semaphore_signal(barrier, inc=1, device_id=mate(j, mine), device_id_type=MESH)
    for r in range(4):
        pl.semaphore_signal(barrier, inc=1, device_id=to[r], device_id_type=MESH)
    pl.semaphore_wait(barrier, len(mates) + 4)

    my_slot = column_slot(0, True)
    own_copies = [
        pltpu.make_async_copy(send_ref.at[own_kind, e, k], got.at[k, my_slot], in_own.at[k]) for k in range(2)
    ]

    def bring(k, j, mine):
        return pltpu.make_async_remote_copy(
            src_ref=send_ref.at[own_kind if mine else 1 - own_kind, rem(e + j, count), k],
            dst_ref=got.at[k, my_slot],
            send_sem=in_send.at[k, 2 * j + (0 if mine else 1)], recv_sem=in_recv.at[k, my_slot],
            device_id=mate(j, mine), device_id_type=MESH,
        )

    def brought(k, j, mine):
        slot = column_slot(j, mine)
        return pltpu.make_async_remote_copy(
            src_ref=got.at[k, slot], dst_ref=got.at[k, slot],
            send_sem=in_send.at[k, 2 * j + (0 if mine else 1)], recv_sem=in_recv.at[k, slot],
            device_id=mate(j, mine), device_id_type=MESH,
        )

    for k in range(2):
        own_copies[k].start()
        for j, mine in mates:
            bring(k, j, mine).start()
    for load in loads:
        load.start()

    def held(r, s):
        c = r // 2
        return rem(spot[c] + RING - s, RING) if r % 2 == 0 else rem(spot[c] + s, RING)

    def gather(r, s, k, where):
        block = xs.at[r // 2, where, :, pl.ds(k * part, part)]
        return pltpu.make_async_remote_copy(
            src_ref=block, dst_ref=block, send_sem=ag_send.at[r, s, k], recv_sem=ag_recv.at[r, s, k],
            device_id=to[r], device_id_type=MESH,
        )

    tiles = part // 128
    for k in range(2):
        own_copies[k].wait()
        for j, mine in mates:
            brought(k, j, mine).wait_recv()
        length = got.shape[2]
        for i in range(2 * count):
            flat[i * length:(i + 1) * length, :] = got[k, i].astype(F32)
        for c in range(2):
            for j in range(tiles):
                block = flat[pl.ds(c * tiles + j, rows, stride=2 * tiles), :]
                begin = k * part + j * 128
                xs[c, spot[c], :, begin:begin + 128] = block.astype(BF)
        for r in range(4):
            gather(r, 1, k, spot[r // 2]).start()
    for load in loads:
        load.wait()

    def forward_unit(unit):
        b = div(unit, 4)
        c = div(rem(unit, 4), 2)
        kind = rem(unit, 2)
        p = spot[0] * (1 - c) + spot[1] * c
        begin = pl.multiple_of(c * share, share)

        def positions(parity):
            low = p - GROUP * (b + 1)
            low = low + rem(low + parity + 2 * RING, 2) + RING
            high = p + GROUP * b
            high = high + rem(high + parity, 2)
            return [div(rem(q, RING), 2) for q in (low, low + 2, high, high + 2)]

        @pl.when(kind == 0)
        def _():
            where = positions(0)
            lhs = jnp.concatenate([xs[c, 2 * t] for t in where], axis=0)
            gate = jnp.dot(lhs, wg[pl.ds(begin, share), :], preferred_element_type=F32)
            up = jnp.dot(lhs, wu[pl.ds(begin, share), :], preferred_element_type=F32)
            for i, t in enumerate(where):
                acc_t[c, t, :, :hidden] = gate[i * rows:(i + 1) * rows]
                acc_t[c, t, :, hidden:] = up[i * rows:(i + 1) * rows]

        @pl.when(kind == 1)
        def _():
            where = positions(1)
            lhs = jnp.concatenate([xs[c, 2 * t + 1] for t in where], axis=0)
            grad = dot_nt(lhs, wd[c])
            for i, t in enumerate(where):
                acc_g[c, t] = grad[i * rows:(i + 1) * rows]

    def ag_step(s, carry):
        for k in range(2):
            for r in range(4):
                gather(r, s, k, held(r, s)).wait_recv()
                if r % 2 == k:
                    gather(r, s + 1, k, held(r, s)).start()
                else:
                    @pl.when(s < HOPS - 1)
                    def _():
                        gather(r, s + 1, k, held(r, s)).start()

        @pl.when(s >= GROUP)
        def _():
            forward_unit(s - GROUP)

        return carry

    lax.fori_loop(1, HOPS, ag_step, 0)
    for r in range(4):
        gather(r, HOPS, r % 2, held(r, HOPS)).wait_recv()

    def tail_unit(u, carry):
        forward_unit(u)
        return carry

    lax.fori_loop(HOPS - GROUP, HOPS, tail_unit, 0)

    ones = jnp.ones((8, 128), F32)
    for pair in range(16):
        pz, px = pair // 2, 2 * (pair % 2)
        holders = [(pz, px), (pz, px + 1)]
        if (px + pz) % 2:
            holders = holders[::-1]
        t = [place(c, *holders[0]) // 2 for c in range(2)]
        g = [place(c, *holders[1]) // 2 for c in range(2)]
        pre_gate = acc_t[0, t[0], :, :hidden] + acc_t[1, t[1], :, :hidden]
        pre_up = acc_t[0, t[0], :, hidden:] + acc_t[1, t[1], :, hidden:]
        grad_hidden = acc_g[0, g[0]] + acc_g[1, g[1]]
        sigma = jax.nn.sigmoid(pre_gate)
        act = pre_gate * sigma
        inner = grad_hidden * act * pre_up
        grad_gate = (grad_hidden * pre_up * sigma * (1.0 + pre_gate * (1.0 - sigma))).astype(BF)
        grad_up = (grad_hidden * act).astype(BF)
        for c in range(2):
            for q in (2 * t[c], 2 * g[c] + 1):
                grads[c, q, :, :hidden] = grad_gate
                grads[c, q, :, hidden:] = grad_up
        folded = inner[:, 0:128]
        for i in range(1, hidden // 128):
            folded = folded + inner[:, i * 128:(i + 1) * 128]
        sums = dot_nt(ones, folded, precision=lax.Precision.HIGHEST)
        for q in (2 * t[0], 2 * g[0] + 1):
            dots[q, :, :rows] = sums

    def dest(r, s):
        c = r // 2
        return rem(spot[c] + HOPS + RING - s, RING) if r % 2 == 0 else rem(spot[c] + HOPS + s, RING)

    def backward_unit(unit):
        b = div(unit, 4)
        c = div(rem(unit, 4), 2)
        kind = rem(unit, 2)
        p = spot[0] * (1 - c) + spot[1] * c
        low = p + HOPS + RING - GROUP * b - (GROUP - 1)
        low = low + rem(low + kind, 2)
        high = p + HOPS + GROUP * b + 1
        high = high + rem(high + kind, 2)
        where = [2 * div(rem(q, RING), 2) + kind for q in (low, low + 2, high, high + 2)]
        lhs = jnp.concatenate([grads[c, q] for q in where], axis=0)
        begin = pl.multiple_of(kind * half + c * part, part)
        y = dot_nt(lhs[:, :hidden], wg[pl.ds(begin, part), :]) + dot_nt(lhs[:, hidden:], wu[pl.ds(begin, part), :])
        for i in range(GROUP):
            local[c, where[i]] = y[i * rows:(i + 1) * rows].astype(local.dtype)

    def head_unit(u, carry):
        backward_unit(u)
        return carry

    lax.fori_loop(0, GROUP, head_unit, 0)

    def scatter(r, s, k, src=None):
        lanes = pl.ds(k * (part // 2), part // 2)
        return pltpu.make_async_remote_copy(
            src_ref=running.at[r, s - 1, :, lanes] if src is None else src, dst_ref=running.at[r, s, :, lanes],
            send_sem=rs_send.at[r, s, k], recv_sem=rs_recv.at[r, s, k],
            device_id=to[r], device_id_type=MESH,
        )

    def scatter_local(r, s, k):
        return scatter(r, s, k, local.at[r // 2, dest(r, s), :, pl.ds(k * (part // 2), part // 2)])

    def add_local(r, s, k):
        lanes = slice(k * (part // 2), (k + 1) * (part // 2))
        total = running[r, s - 1, :, lanes].astype(F32) + local[r // 2, dest(r, s), :, lanes].astype(F32)
        running[r, s - 1, :, lanes] = total.astype(BF)

    def dot_copy(d, s, src):
        return pltpu.make_async_remote_copy(
            src_ref=src, dst_ref=dot_slots.at[d, s], send_sem=dot_send.at[d, s], recv_sem=dot_recv.at[d, s],
            device_id=to[d], device_id_type=MESH,
        )

    for r in range(4):
        scatter_local(r, 0, r % 2).start()
    for r in range(4):
        scatter_local(r, 1, 1 - r % 2).start()
    dot_copy(0, 0, dots.at[dest(0, 0)]).start()
    dot_copy(1, 1, dots.at[dest(1, 1)]).start()
    backward_unit(jnp.int32(GROUP))

    for r in range(4):
        scatter_local(r, 0, r % 2).wait_recv()
        add_local(r, 1, r % 2)
        scatter(r, 1, r % 2).start()
    dot_copy(0, 0, dot_slots.at[0, 0]).wait_recv()
    dot_slots[0, 0] = dot_slots[0, 0] + dots[dest(0, 1)]
    dot_copy(0, 1, dot_slots.at[0, 0]).start()
    backward_unit(jnp.int32(GROUP + 1))

    def rs_step(s, carry):
        for turn in range(2):
            for r in range(4):
                k = (r + 1 + turn) % 2
                scatter(r, s - 1, k).wait_recv()
                add_local(r, s, k)
                scatter(r, s, k).start()
        for d in range(2):
            dot_copy(d, s - 1, dot_slots.at[d, s - 1]).wait_recv()
            dot_slots[d, s - 1] = dot_slots[d, s - 1] + dots[dest(d, s)]
            dot_copy(d, s, dot_slots.at[d, s - 1]).start()

        @pl.when(s < HOPS - GROUP)
        def _():
            backward_unit(s + GROUP)

        return carry

    lax.fori_loop(2, HOPS, rs_step, 0)
    last = HOPS - 1
    tiles = part // 128
    for c in range(2):
        for k in range(2):
            for d in range(2):
                scatter(2 * c + d, last, k).wait_recv()
            lanes = slice(k * (part // 2), (k + 1) * (part // 2))
            total = running[2 * c, last, :, lanes].astype(F32) + running[2 * c + 1, last, :, lanes].astype(F32)
            total = total + local[c, spot[c], :, lanes].astype(F32)
            for j in range(tiles // 2):
                row = c * tiles + k * (tiles // 2) + j
                flat[pl.ds(row, rows, stride=2 * tiles), :] = total[:, j * 128:(j + 1) * 128]
    length = leave.shape[1]
    for i in range(2 * count):
        leave[i] = flat[i * length:(i + 1) * length, :].astype(BF)
    for d in range(2):
        dot_copy(d, last, dot_slots.at[d, last]).wait_recv()
    dot_out[...] = dot_slots[0, last] + dot_slots[1, last] + dots[spot[0]]

    def giveback(i, j, mine, src, dst):
        return pltpu.make_async_remote_copy(
            src_ref=src, dst_ref=dst,
            send_sem=out_send.at[i, 2 * j + (0 if mine else 1)], recv_sem=out_recv.at[i, own_kind * count + e],
            device_id=mate(j, mine), device_id_type=MESH,
        )

    def returned(i, j, mine, ref):
        kind, source = own_kind if mine else 1 - own_kind, rem(e + j, count)
        return pltpu.make_async_remote_copy(
            src_ref=ref.at[kind, source], dst_ref=ref.at[kind, source],
            send_sem=out_send.at[i, 2 * j + (0 if mine else 1)], recv_sem=out_recv.at[i, kind * count + source],
            device_id=mate(j, mine), device_id_type=MESH,
        )

    finals = [
        pltpu.make_async_copy(leave.at[my_slot], back_ref.at[own_kind, e], out_own.at[0]),
        pltpu.make_async_copy(dot_out, back_dots.at[own_kind, e], out_own.at[1]),
    ]
    for final in finals:
        final.start()
    sent = []
    for j, mine in mates:
        sent.append(giveback(0, j, mine, leave.at[column_slot(j, mine)], back_ref.at[own_kind, e]))
        sent.append(giveback(1, j, mine, dot_out, back_dots.at[own_kind, e]))
        sent[-2].start()
        sent[-1].start()

    for k in range(2):
        for j, mine in mates:
            bring(k, j, mine).wait_send()
    for r in range(4):
        gather(r, HOPS, r % 2, held(r, HOPS - 1)).wait_send()
        scatter_local(r, 0, r % 2).wait_send()
    dot_copy(0, 0, dots.at[dest(0, 0)]).wait_send()

    def drain(s, carry):
        for k in range(2):
            for r in range(4):
                gather(r, s, k, held(r, s - 1)).wait_send()
                scatter(r, s, k).wait_send()
        for d in range(2):
            dot_copy(d, s, dot_slots.at[d, s - 1]).wait_send()
        return carry

    lax.fori_loop(1, HOPS, drain, 0)
    for copy in sent:
        copy.wait_send()
    for final in finals:
        final.wait()
    for j, mine in mates:
        returned(0, j, mine, back_ref).wait_recv()
        returned(1, j, mine, back_dots).wait_recv()


def run_experts(send, gate_weight, up_weight, down_weight):
    count, length = send.shape[1], send.shape[3]
    width, hidden = gate_weight.shape[1:]
    share, part = width // 2, width // 4
    rows = 2 * count * length * 128 // (2 * part)
    vmem = pl.BlockSpec(memory_space=pltpu.VMEM)
    hbm = pl.BlockSpec(memory_space=pl.ANY)
    return pl.pallas_call(
        experts_kernel,
        out_shape=(
            jax.ShapeDtypeStruct((2, count, length, 128), BF),
            jax.ShapeDtypeStruct((2, count, 8, 128), F32),
        ),
        in_specs=[vmem, hbm, hbm, hbm],
        out_specs=(vmem, vmem),
        scratch_shapes=[
            pltpu.VMEM((2, 2 * count, length, 128), BF),
            pltpu.VMEM((2 * count * length, 128), F32),
            pltpu.VMEM((2 * count, length, 128), BF),
            pltpu.VMEM((2, RING, rows, share), BF),
            pltpu.VMEM((4, HOPS, rows, part), BF),
            pltpu.VMEM((2, RING, rows, part), BF),
            pltpu.VMEM((2, 16, rows, 2 * hidden), F32),
            pltpu.VMEM((2, 16, rows, hidden), F32),
            pltpu.VMEM((2, RING, rows, 2 * hidden), BF),
            pltpu.VMEM((RING, 8, 128), F32),
            pltpu.VMEM((2, HOPS, 8, 128), F32),
            pltpu.VMEM((8, 128), F32),
            pltpu.VMEM((width, hidden), BF),
            pltpu.VMEM((width, hidden), BF),
            pltpu.VMEM((2, hidden, share), BF),
            pltpu.SemaphoreType.DMA((4,)),
            pltpu.SemaphoreType.DMA((2,)),
            pltpu.SemaphoreType.DMA((2, 2 * count)),
            pltpu.SemaphoreType.DMA((2, 2 * count)),
            pltpu.SemaphoreType.DMA((4, HOPS + 1, 2)),
            pltpu.SemaphoreType.DMA((4, HOPS + 1, 2)),
            pltpu.SemaphoreType.DMA((4, HOPS, 2)),
            pltpu.SemaphoreType.DMA((4, HOPS, 2)),
            pltpu.SemaphoreType.DMA((2, HOPS)),
            pltpu.SemaphoreType.DMA((2, HOPS)),
            pltpu.SemaphoreType.DMA((2,)),
            pltpu.SemaphoreType.DMA((2, 2 * count)),
            pltpu.SemaphoreType.DMA((2, 2 * count)),
        ],
        compiler_params=pltpu.CompilerParams(
            collective_id=0, has_side_effects=True, vmem_limit_bytes=63 << 20
        ),
        name="experts",
    )(send, gate_weight, up_weight, down_weight)


def on_device(tokens, out_grad, kept_mask, routes, router, gate_weight, up_weight, down_weight):
    row_count, width = tokens.shape
    count = lax.axis_size("expert")
    capacity = 3 * row_count // 8
    columns = lax.broadcasted_iota(jnp.int32, (row_count, count), 1)
    first_hot = (routes[:, 0:1] == columns).astype(F32)
    second_hot = (routes[:, 1:2] == columns).astype(F32)
    keep_rows = kept_mask.astype(F32)
    chosen = ((first_hot + second_hot) * keep_rows[:, None]).astype(jnp.int32)
    position = jnp.cumsum(chosen, axis=0) - 1
    slot_iota = lax.broadcasted_iota(jnp.int32, (row_count, count, capacity), 2)
    select_mask = (chosen[:, :, None] == 1) & (position[:, :, None] == slot_iota)
    select_bf = select_mask.astype(BF)
    select_full = select_mask.astype(F32)
    both = jnp.stack([tokens, out_grad])
    send = jnp.einsum("tec,ktd->kecd", select_bf, both, preferred_element_type=F32).astype(BF)
    tiles = width // 512
    send = send.reshape(2, count, capacity, 2, 2, tiles, 128).transpose(0, 1, 4, 2, 3, 5, 6)
    send = send.reshape(2, count, 2, capacity * 2 * tiles, 128)
    back, back_dots = run_experts(send, gate_weight, up_weight, down_weight)
    back = back.reshape(2, count, capacity, width // 2)
    own_slot = rem(lax.axis_index("mp"), 2) * count + lax.axis_index("expert")
    dot_back = lax.dynamic_slice_in_dim(back_dots[0, :, 0, :], own_slot * capacity, capacity, 1)

    logits = jnp.dot(tokens, router, preferred_element_type=F32)
    first_logit = jnp.sum(logits * first_hot, axis=1)
    second_logit = jnp.sum(logits * second_hot, axis=1)
    gate_first = jax.nn.sigmoid(first_logit - second_logit)
    gate_second = jax.nn.sigmoid(second_logit - first_logit)
    gate_table = (first_hot * gate_first[:, None] + second_hot * gate_second[:, None]).astype(BF)
    weigh = select_bf * gate_table[:, :, None]
    expert_sum = jnp.einsum("tec,kecd->tkd", weigh, back, preferred_element_type=F32)
    expert_sum = expert_sum.reshape(row_count, width)
    dot_table = jnp.sum(select_full * dot_back[None], axis=2)
    dot_first = jnp.sum(dot_table * first_hot, axis=1)
    dot_second = jnp.sum(dot_table * second_hot, axis=1)
    product = gate_first * gate_second * keep_rows
    grad_first = product * (dot_first - dot_second)
    grad_second = product * (dot_second - dot_first)
    logit_grad = first_hot * grad_first[:, None] + second_hot * grad_second[:, None]
    router_term = jnp.dot(logit_grad, router.astype(F32).T, precision=lax.Precision.HIGHEST)
    d_tokens = ((expert_sum + router_term) * keep_rows[:, None]).astype(BF)
    gate_grad = jnp.stack([grad_first, grad_second], axis=1)
    return (d_tokens, gate_grad)


def solution(mesh):
    return jax.shard_map(
        on_device,
        mesh=mesh,
        in_specs=(
            P(("seq", "expert", "mp"), None),
            P(("seq", "expert", "mp"), None),
            P(("seq", "expert", "mp")),
            P(("seq", "expert", "mp"), None),
            P(),
            P("expert", None, ("seq", "mp")),
            P("expert", None, ("seq", "mp")),
            P("expert", ("seq", "mp"), None),
        ),
        out_specs=(P(("seq", "expert", "mp"), None), P(("seq", "expert", "mp"), None)),
        check_vma=False,
    )
```

```python
import functools

import jax
import jax.numpy as jnp
from jax import lax
from jax.experimental import pallas as pl
from jax.experimental.pallas import tpu as pltpu
from jax.sharding import PartitionSpec as P

MESH = pl.DeviceIdType.MESH
BF = jnp.bfloat16
F32 = jnp.float32
RING = 32
HOPS = 16
GROUP = 4
CUTS = 4


def div(a, b):
    return a // b if isinstance(a, int) else lax.div(a, jnp.int32(b))


def rem(a, b):
    return a % b if isinstance(a, int) else lax.rem(a, jnp.int32(b))


def place(cycle, z, x):
    if cycle == 0:
        return 4 * z + rem(x + z, 4)
    turn = rem(z + 5 * x, 8)
    return 4 * x + 16 * div(turn, 4) + rem(turn, 4)


def coords(cycle, q):
    a, b = div(q, 4), rem(q, 4)
    if cycle == 0:
        return a, rem(b - a + 8, 4)
    return rem(3 * a + b, 8), rem(a, 4)


def peer(z, x):
    return {"seq": z, "mp": x}


def dot_nt(a, b, **kwargs):
    return lax.dot_general(a, b, (((1,), (1,)), ((), ())), preferred_element_type=F32, **kwargs)


def experts_kernel(
    plan_ref, tok_ref, grad_ref, wg_hbm, wu_hbm, wd_hbm, back_ref, back_dots,
    send_ref, got, flat, leave, xs, running, local, acc_t, acc_g, grads, dots, dot_slots, dot_out, wg, wu, wd,
    w_sem, in_own, in_send, in_recv, ag_send, ag_recv, rs_send, rs_recv, dot_send, dot_recv,
    out_own, out_send, out_recv,
):
    count = send_ref.shape[2]
    capacity = 3 * tok_ref.shape[0] // 8
    rows, share = xs.shape[2], xs.shape[3]
    hidden = wg.shape[1]
    part = share // 2
    half = 2 * part
    z, e, x = lax.axis_index("seq"), lax.axis_index("expert"), lax.axis_index("mp")
    other = x + 1 - 2 * rem(x, 2)
    own_kind = rem(x + z, 2)
    spot = [place(c, z, x) for c in range(2)]
    after = [coords(c, rem(spot[c] + 1, RING)) for c in range(2)]
    before = [coords(c, rem(spot[c] + RING - 1, RING)) for c in range(2)]
    to = [peer(*after[0]), peer(*before[0]), peer(*after[1]), peer(*before[1])]

    mates = [(j, mine) for j in range(count) for mine in (True, False) if j or not mine]

    def mate(j, mine):
        return {"seq": z, "expert": rem(e + j, count), "mp": x if mine else other}

    def column_slot(j, mine):
        return rem(x if mine else other, 2) * count + rem(e + j, count)

    loads = [
        pltpu.make_async_copy(wg_hbm.at[0], wg, w_sem.at[0]),
        pltpu.make_async_copy(wu_hbm.at[0], wu, w_sem.at[1]),
    ]
    for c in range(2):
        loads.append(pltpu.make_async_copy(wd_hbm.at[0, :, pl.ds(c * share, share)], wd.at[c], w_sem.at[2 + c]))

    barrier = pltpu.get_barrier_semaphore()
    for j, mine in mates:
        pl.semaphore_signal(barrier, inc=1, device_id=mate(j, mine), device_id_type=MESH)
    for r in range(4):
        pl.semaphore_signal(barrier, inc=1, device_id=to[r], device_id_type=MESH)
    tiles = part // 128
    row = lax.broadcasted_iota(jnp.int32, (count * capacity, 128), 0)
    expert = jnp.zeros((count * capacity, 128), jnp.int32)
    for m in range(1, count):
        expert = expert + (row >= m * capacity).astype(jnp.int32)
    place_in = (row - capacity * expert + 1).astype(F32)
    expert = expert.astype(F32)
    named = (plan_ref[0:1, :] == expert) | (plan_ref[1:2, :] == expert)
    chosen = jnp.where(named, plan_ref[2:3, :], 0.0)
    upto = lax.broadcasted_iota(jnp.int32, (128, 128), 0) <= lax.broadcasted_iota(jnp.int32, (128, 128), 1)
    nth = jnp.dot(chosen.astype(BF), upto.astype(F32).astype(BF), preferred_element_type=F32)
    pick = jnp.where(nth == place_in, chosen, 0.0).astype(BF)[:, : tok_ref.shape[0]]
    length = send_ref.shape[3]
    for kind, source in enumerate((tok_ref, grad_ref)):
        for c in range(2):
            for k in range(2):
                begin = c * share + k * part
                picked = jnp.dot(pick, source[:, begin:begin + part], preferred_element_type=F32)
                for j in range(tiles):
                    where = k * count * length + c * tiles + j
                    flat[pl.ds(where, count * capacity, stride=2 * tiles), :] = picked[:, j * 128:(j + 1) * 128]
        for k in range(2):
            for i in range(count):
                begin = (k * count + i) * length
                send_ref[kind, k, i] = flat[begin:begin + length, :].astype(BF)

    pl.semaphore_wait(barrier, len(mates) + 4)

    my_slot = column_slot(0, True)
    own_copies = [
        pltpu.make_async_copy(send_ref.at[own_kind, k, e], got.at[k, my_slot], in_own.at[k]) for k in range(2)
    ]

    def bring(k, j, mine):
        return pltpu.make_async_remote_copy(
            src_ref=send_ref.at[own_kind if mine else 1 - own_kind, k, rem(e + j, count)],
            dst_ref=got.at[k, my_slot],
            send_sem=in_send.at[k, 2 * j + (0 if mine else 1)], recv_sem=in_recv.at[k, my_slot],
            device_id=mate(j, mine), device_id_type=MESH,
        )

    def brought(k, j, mine):
        slot = column_slot(j, mine)
        return pltpu.make_async_remote_copy(
            src_ref=got.at[k, slot], dst_ref=got.at[k, slot],
            send_sem=in_send.at[k, 2 * j + (0 if mine else 1)], recv_sem=in_recv.at[k, slot],
            device_id=mate(j, mine), device_id_type=MESH,
        )

    for k in range(2):
        own_copies[k].start()
        for j, mine in mates:
            bring(k, j, mine).start()
    for load in loads:
        load.start()

    def held(r, s):
        c = r // 2
        return rem(spot[c] + RING - s, RING) if r % 2 == 0 else rem(spot[c] + s, RING)

    def gather(r, s, k, where):
        block = xs.at[r // 2, where, :, pl.ds(k * part, part)]
        return pltpu.make_async_remote_copy(
            src_ref=block, dst_ref=block, send_sem=ag_send.at[r, s, k], recv_sem=ag_recv.at[r, s, k],
            device_id=to[r], device_id_type=MESH,
        )

    for k in range(2):
        own_copies[k].wait()
        for j, mine in mates:
            brought(k, j, mine).wait_recv()
        length = got.shape[2]
        for i in range(2 * count):
            flat[i * length:(i + 1) * length, :] = got[k, i].astype(F32)
        for c in range(2):
            for j in range(tiles):
                block = flat[pl.ds(c * tiles + j, rows, stride=2 * tiles), :]
                begin = k * part + j * 128
                xs[c, spot[c], :, begin:begin + 128] = block.astype(BF)
        for r in range(4):
            gather(r, 1, k, spot[r // 2]).start()
    for load in loads:
        load.wait()

    def forward_unit(unit):
        b = div(unit, 4)
        c = div(rem(unit, 4), 2)
        kind = rem(unit, 2)
        p = spot[0] * (1 - c) + spot[1] * c
        begin = pl.multiple_of(c * share, share)

        def positions(parity):
            low = p - GROUP * (b + 1)
            low = low + rem(low + parity + 2 * RING, 2) + RING
            high = p + GROUP * b
            high = high + rem(high + parity, 2)
            return [div(rem(q, RING), 2) for q in (low, low + 2, high, high + 2)]

        @pl.when(kind == 0)
        def _():
            where = positions(0)
            lhs = jnp.concatenate([xs[c, 2 * t] for t in where], axis=0)
            gate = jnp.dot(lhs, wg[pl.ds(begin, share), :], preferred_element_type=F32)
            up = jnp.dot(lhs, wu[pl.ds(begin, share), :], preferred_element_type=F32)
            for i, t in enumerate(where):
                acc_t[c, t, :, :hidden] = gate[i * rows:(i + 1) * rows]
                acc_t[c, t, :, hidden:] = up[i * rows:(i + 1) * rows]

        @pl.when(kind == 1)
        def _():
            where = positions(1)
            lhs = jnp.concatenate([xs[c, 2 * t + 1] for t in where], axis=0)
            grad = dot_nt(lhs, wd[c])
            for i, t in enumerate(where):
                acc_g[c, t] = grad[i * rows:(i + 1) * rows]

    def ag_step(s, carry):
        for k in range(2):
            for r in range(4):
                gather(r, s, k, held(r, s)).wait_recv()
                if r % 2 == k:
                    gather(r, s + 1, k, held(r, s)).start()
                else:
                    @pl.when(s < HOPS - 1)
                    def _():
                        gather(r, s + 1, k, held(r, s)).start()

        @pl.when(s >= GROUP)
        def _():
            forward_unit(s - GROUP)

        return carry

    lax.fori_loop(1, HOPS, ag_step, 0)
    for r in range(4):
        gather(r, HOPS, r % 2, held(r, HOPS)).wait_recv()

    def tail_unit(u, carry):
        forward_unit(u)
        return carry

    lax.fori_loop(HOPS - GROUP, HOPS, tail_unit, 0)

    ones = jnp.ones((8, 128), F32)
    for pair in range(16):
        pz, px = pair // 2, 2 * (pair % 2)
        holders = [(pz, px), (pz, px + 1)]
        if (px + pz) % 2:
            holders = holders[::-1]
        t = [place(c, *holders[0]) // 2 for c in range(2)]
        g = [place(c, *holders[1]) // 2 for c in range(2)]
        pre_gate = acc_t[0, t[0], :, :hidden] + acc_t[1, t[1], :, :hidden]
        pre_up = acc_t[0, t[0], :, hidden:] + acc_t[1, t[1], :, hidden:]
        grad_hidden = acc_g[0, g[0]] + acc_g[1, g[1]]
        sigma = jax.nn.sigmoid(pre_gate)
        act = pre_gate * sigma
        inner = grad_hidden * act * pre_up
        grad_gate = (grad_hidden * pre_up * sigma * (1.0 + pre_gate * (1.0 - sigma))).astype(BF)
        grad_up = (grad_hidden * act).astype(BF)
        for c in range(2):
            for q in (2 * t[c], 2 * g[c] + 1):
                grads[c, q, :, :hidden] = grad_gate
                grads[c, q, :, hidden:] = grad_up
        folded = inner[:, 0:128]
        for i in range(1, hidden // 128):
            folded = folded + inner[:, i * 128:(i + 1) * 128]
        sums = dot_nt(ones, folded, precision=lax.Precision.HIGHEST)
        for q in (2 * t[0], 2 * g[0] + 1):
            dots[q, :, :rows] = sums

    def dest(r, s):
        c = r // 2
        return rem(spot[c] + HOPS + RING - s, RING) if r % 2 == 0 else rem(spot[c] + HOPS + s, RING)

    def backward_unit(unit):
        b = div(unit, 4)
        c = div(rem(unit, 4), 2)
        kind = rem(unit, 2)
        p = spot[0] * (1 - c) + spot[1] * c
        low = p + HOPS + RING - GROUP * b - (GROUP - 1)
        low = low + rem(low + kind, 2)
        high = p + HOPS + GROUP * b + 1
        high = high + rem(high + kind, 2)
        where = [2 * div(rem(q, RING), 2) + kind for q in (low, low + 2, high, high + 2)]
        lhs = jnp.concatenate([grads[c, q] for q in where], axis=0)
        begin = pl.multiple_of(kind * half + c * part, part)
        y = dot_nt(lhs[:, :hidden], wg[pl.ds(begin, part), :]) + dot_nt(lhs[:, hidden:], wu[pl.ds(begin, part), :])
        for i in range(GROUP):
            local[c, where[i]] = y[i * rows:(i + 1) * rows].astype(local.dtype)

    cut = part // CUTS
    mine_of = [[d * (CUTS // 2) + i for i in range(CUTS // 2)] for d in range(2)]

    def scatter(r, s, k, src=None):
        lanes = pl.ds(k * cut, cut)
        return pltpu.make_async_remote_copy(
            src_ref=running.at[r, s - 1, :, lanes] if src is None else src, dst_ref=running.at[r, s, :, lanes],
            send_sem=rs_send.at[r, s, k], recv_sem=rs_recv.at[r, s, k],
            device_id=to[r], device_id_type=MESH,
        )

    def scatter_local(r, s, k):
        return scatter(r, s, k, local.at[r // 2, dest(r, s), :, pl.ds(k * cut, cut)])

    def add_local(r, s, k):
        lanes = slice(k * cut, (k + 1) * cut)
        total = running[r, s - 1, :, lanes].astype(F32) + local[r // 2, dest(r, s), :, lanes].astype(F32)
        running[r, s - 1, :, lanes] = total.astype(BF)

    def dot_copy(d, s, src):
        return pltpu.make_async_remote_copy(
            src_ref=src, dst_ref=dot_slots.at[d, s], send_sem=dot_send.at[d, s], recv_sem=dot_recv.at[d, s],
            device_id=to[d], device_id_type=MESH,
        )

    def head_unit(u, carry):
        backward_unit(u)
        return carry

    for c in range(2):
        lax.fori_loop(2 * c, 2 * c + 2, head_unit, 0)
        for r in (2 * c, 2 * c + 1):
            for k in mine_of[r % 2]:
                scatter_local(r, 0, k).start()
        for r in (2 * c, 2 * c + 1):
            for k in mine_of[1 - r % 2]:
                scatter_local(r, 1, k).start()
    dot_copy(0, 0, dots.at[dest(0, 0)]).start()
    dot_copy(1, 1, dots.at[dest(1, 1)]).start()
    backward_unit(jnp.int32(GROUP))

    for i in range(CUTS // 2):
        for r in range(4):
            k = mine_of[r % 2][i]
            scatter_local(r, 0, k).wait_recv()
            add_local(r, 1, k)
            scatter(r, 1, k).start()
    dot_copy(0, 0, dot_slots.at[0, 0]).wait_recv()
    dot_slots[0, 0] = dot_slots[0, 0] + dots[dest(0, 1)]
    dot_copy(0, 1, dot_slots.at[0, 0]).start()
    backward_unit(jnp.int32(GROUP + 1))

    def rs_step(s, carry):
        for turn in range(CUTS):
            for r in range(4):
                k = (mine_of[1 - r % 2] + mine_of[r % 2])[turn]
                scatter(r, s - 1, k).wait_recv()
                add_local(r, s, k)
                scatter(r, s, k).start()
        for d in range(2):
            dot_copy(d, s - 1, dot_slots.at[d, s - 1]).wait_recv()
            dot_slots[d, s - 1] = dot_slots[d, s - 1] + dots[dest(d, s)]
            dot_copy(d, s, dot_slots.at[d, s - 1]).start()

        @pl.when(s < HOPS - GROUP)
        def _():
            backward_unit(s + GROUP)

        return carry

    lax.fori_loop(2, HOPS, rs_step, 0)
    last = HOPS - 1
    tiles = part // 128
    for c in range(2):
        for k in range(CUTS):
            for d in range(2):
                scatter(2 * c + d, last, k).wait_recv()
            lanes = slice(k * cut, (k + 1) * cut)
            total = running[2 * c, last, :, lanes].astype(F32) + running[2 * c + 1, last, :, lanes].astype(F32)
            total = total + local[c, spot[c], :, lanes].astype(F32)
            for j in range(tiles // CUTS):
                line = c * tiles + k * (tiles // CUTS) + j
                flat[pl.ds(line, rows, stride=2 * tiles), :] = total[:, j * 128:(j + 1) * 128]
    length = leave.shape[1]
    for i in range(2 * count):
        leave[i] = flat[i * length:(i + 1) * length, :].astype(BF)
    for d in range(2):
        dot_copy(d, last, dot_slots.at[d, last]).wait_recv()
    dot_out[...] = dot_slots[0, last] + dot_slots[1, last] + dots[spot[0]]

    def giveback(i, j, mine, src, dst):
        return pltpu.make_async_remote_copy(
            src_ref=src, dst_ref=dst,
            send_sem=out_send.at[i, 2 * j + (0 if mine else 1)], recv_sem=out_recv.at[i, own_kind * count + e],
            device_id=mate(j, mine), device_id_type=MESH,
        )

    def returned(i, j, mine, ref):
        kind, source = own_kind if mine else 1 - own_kind, rem(e + j, count)
        return pltpu.make_async_remote_copy(
            src_ref=ref.at[kind, source], dst_ref=ref.at[kind, source],
            send_sem=out_send.at[i, 2 * j + (0 if mine else 1)], recv_sem=out_recv.at[i, kind * count + source],
            device_id=mate(j, mine), device_id_type=MESH,
        )

    finals = [
        pltpu.make_async_copy(leave.at[my_slot], back_ref.at[own_kind, e], out_own.at[0]),
        pltpu.make_async_copy(dot_out, back_dots.at[own_kind, e], out_own.at[1]),
    ]
    for final in finals:
        final.start()
    sent = []
    for j, mine in mates:
        sent.append(giveback(0, j, mine, leave.at[column_slot(j, mine)], back_ref.at[own_kind, e]))
        sent.append(giveback(1, j, mine, dot_out, back_dots.at[own_kind, e]))
        sent[-2].start()
        sent[-1].start()

    for k in range(2):
        for j, mine in mates:
            bring(k, j, mine).wait_send()
    for r in range(4):
        gather(r, HOPS, r % 2, held(r, HOPS - 1)).wait_send()
        for k in mine_of[r % 2]:
            scatter_local(r, 0, k).wait_send()
    dot_copy(0, 0, dots.at[dest(0, 0)]).wait_send()

    def drain(s, carry):
        for k in range(2):
            for r in range(4):
                gather(r, s, k, held(r, s - 1)).wait_send()
        for k in range(CUTS):
            for r in range(4):
                scatter(r, s, k).wait_send()
        for d in range(2):
            dot_copy(d, s, dot_slots.at[d, s - 1]).wait_send()
        return carry

    lax.fori_loop(1, HOPS, drain, 0)
    for copy in sent:
        copy.wait_send()
    for final in finals:
        final.wait()
    for j, mine in mates:
        returned(0, j, mine, back_ref).wait_recv()
        returned(1, j, mine, back_dots).wait_recv()


def run_experts(count, plan, tokens, out_grad, gate_weight, up_weight, down_weight):
    width, hidden = gate_weight.shape[1:]
    share, part = width // 2, width // 4
    capacity = 3 * tokens.shape[0] // 8
    length = capacity * 2 * part // 128
    rows = 2 * count * capacity
    vmem = pl.BlockSpec(memory_space=pltpu.VMEM)
    hbm = pl.BlockSpec(memory_space=pl.ANY)
    return pl.pallas_call(
        experts_kernel,
        out_shape=(
            jax.ShapeDtypeStruct((2, count, length, 128), BF),
            jax.ShapeDtypeStruct((2, count, 8, 128), F32),
        ),
        in_specs=[vmem, vmem, vmem, hbm, hbm, hbm],
        out_specs=(vmem, vmem),
        scratch_shapes=[
            pltpu.VMEM((2, 2, count, length, 128), BF),
            pltpu.VMEM((2, 2 * count, length, 128), BF),
            pltpu.VMEM((2 * count * length, 128), F32),
            pltpu.VMEM((2 * count, length, 128), BF),
            pltpu.VMEM((2, RING, rows, share), BF),
            pltpu.VMEM((4, HOPS, rows, part), BF),
            pltpu.VMEM((2, RING, rows, part), BF),
            pltpu.VMEM((2, 16, rows, 2 * hidden), F32),
            pltpu.VMEM((2, 16, rows, hidden), F32),
            pltpu.VMEM((2, RING, rows, 2 * hidden), BF),
            pltpu.VMEM((RING, 8, 128), F32),
            pltpu.VMEM((2, HOPS, 8, 128), F32),
            pltpu.VMEM((8, 128), F32),
            pltpu.VMEM((width, hidden), BF),
            pltpu.VMEM((width, hidden), BF),
            pltpu.VMEM((2, hidden, share), BF),
            pltpu.SemaphoreType.DMA((4,)),
            pltpu.SemaphoreType.DMA((2,)),
            pltpu.SemaphoreType.DMA((2, 2 * count)),
            pltpu.SemaphoreType.DMA((2, 2 * count)),
            pltpu.SemaphoreType.DMA((4, HOPS + 1, 2)),
            pltpu.SemaphoreType.DMA((4, HOPS + 1, 2)),
            pltpu.SemaphoreType.DMA((4, HOPS, CUTS)),
            pltpu.SemaphoreType.DMA((4, HOPS, CUTS)),
            pltpu.SemaphoreType.DMA((2, HOPS)),
            pltpu.SemaphoreType.DMA((2, HOPS)),
            pltpu.SemaphoreType.DMA((2,)),
            pltpu.SemaphoreType.DMA((2, 2 * count)),
            pltpu.SemaphoreType.DMA((2, 2 * count)),
        ],
        compiler_params=pltpu.CompilerParams(
            collective_id=0, has_side_effects=True, vmem_limit_bytes=63 << 20
        ),
        name="experts",
    )(plan, tokens, out_grad, gate_weight, up_weight, down_weight)


def on_device(tokens, out_grad, kept_mask, routes, router, gate_weight, up_weight, down_weight):
    row_count, width = tokens.shape
    count = lax.axis_size("expert")
    capacity = 3 * row_count // 8
    columns = lax.broadcasted_iota(jnp.int32, (row_count, count), 1)
    first_hot = (routes[:, 0:1] == columns).astype(F32)
    second_hot = (routes[:, 1:2] == columns).astype(F32)
    keep_rows = kept_mask.astype(F32)
    chosen = ((first_hot + second_hot) * keep_rows[:, None]).astype(jnp.int32)
    position = jnp.cumsum(chosen, axis=0) - 1
    slot_iota = lax.broadcasted_iota(jnp.int32, (row_count, count, capacity), 2)
    select_mask = (chosen[:, :, None] == 1) & (position[:, :, None] == slot_iota)
    select_bf = select_mask.astype(BF)
    select_full = select_mask.astype(F32)
    plan = jnp.concatenate([routes.astype(F32).T, keep_rows[None]], axis=0)
    plan = jnp.pad(plan, ((0, 5), (0, 128 - row_count)))
    back, back_dots = run_experts(count, plan, tokens, out_grad, gate_weight, up_weight, down_weight)
    back = back.reshape(2, count, capacity, width // 2)
    own_slot = rem(lax.axis_index("mp"), 2) * count + lax.axis_index("expert")
    dot_back = lax.dynamic_slice_in_dim(back_dots[0, :, 0, :], own_slot * capacity, capacity, 1)

    logits = jnp.dot(tokens, router, preferred_element_type=F32)
    first_logit = jnp.sum(logits * first_hot, axis=1)
    second_logit = jnp.sum(logits * second_hot, axis=1)
    gate_first = jax.nn.sigmoid(first_logit - second_logit)
    gate_second = jax.nn.sigmoid(second_logit - first_logit)
    gate_table = (first_hot * gate_first[:, None] + second_hot * gate_second[:, None]).astype(BF)
    weigh = select_bf * gate_table[:, :, None]
    expert_sum = jnp.einsum("tec,kecd->tkd", weigh, back, preferred_element_type=F32)
    expert_sum = expert_sum.reshape(row_count, width)
    dot_table = jnp.sum(select_full * dot_back[None], axis=2)
    dot_first = jnp.sum(dot_table * first_hot, axis=1)
    dot_second = jnp.sum(dot_table * second_hot, axis=1)
    product = gate_first * gate_second * keep_rows
    grad_first = product * (dot_first - dot_second)
    grad_second = product * (dot_second - dot_first)
    logit_grad = first_hot * grad_first[:, None] + second_hot * grad_second[:, None]
    router_term = jnp.dot(logit_grad, router.astype(F32).T, precision=lax.Precision.HIGHEST)
    d_tokens = ((expert_sum + router_term) * keep_rows[:, None]).astype(BF)
    gate_grad = jnp.stack([grad_first, grad_second], axis=1)
    return (d_tokens, gate_grad)


def solution(mesh):
    return jax.shard_map(
        on_device,
        mesh=mesh,
        in_specs=(
            P(("seq", "expert", "mp"), None),
            P(("seq", "expert", "mp"), None),
            P(("seq", "expert", "mp")),
            P(("seq", "expert", "mp"), None),
            P(),
            P("expert", None, ("seq", "mp")),
            P("expert", None, ("seq", "mp")),
            P("expert", ("seq", "mp"), None),
        ),
        out_specs=(P(("seq", "expert", "mp"), None), P(("seq", "expert", "mp"), None)),
        check_vma=False,
    )
```

```python
import functools

import jax
import jax.numpy as jnp
from jax import lax
from jax.experimental import pallas as pl
from jax.experimental.pallas import tpu as pltpu
from jax.sharding import PartitionSpec as P

MESH = pl.DeviceIdType.MESH
BF = jnp.bfloat16
F32 = jnp.float32
RING = 32
HOPS = 16
GROUP = 4
CUTS = 4


def div(a, b):
    return a // b if isinstance(a, int) else lax.div(a, jnp.int32(b))


def rem(a, b):
    return a % b if isinstance(a, int) else lax.rem(a, jnp.int32(b))


def place(cycle, z, x):
    if cycle == 0:
        return 4 * z + rem(x + z, 4)
    turn = rem(z + 5 * x, 8)
    return 4 * x + 16 * div(turn, 4) + rem(turn, 4)


def coords(cycle, q):
    a, b = div(q, 4), rem(q, 4)
    if cycle == 0:
        return a, rem(b - a + 8, 4)
    return rem(3 * a + b, 8), rem(a, 4)


def peer(z, x):
    return {"seq": z, "mp": x}


def dot_nt(a, b, **kwargs):
    return lax.dot_general(a, b, (((1,), (1,)), ((), ())), preferred_element_type=F32, **kwargs)


def experts_kernel(
    plan_ref, tok_ref, grad_ref, wg_hbm, wu_hbm, wd_hbm, back_ref, back_dots,
    send_ref, got, flat, leave, xs, running, local, acc_t, acc_g, grads, dots, dot_slots, dot_out, wg, wu, wd,
    w_sem, in_own, in_send, in_recv, ag_send, ag_recv, rs_first, rs_send, rs_recv, dot_send, dot_recv,
    out_own, out_send, out_recv,
):
    count = send_ref.shape[2]
    capacity = 3 * tok_ref.shape[0] // 8
    rows, share = xs.shape[2], xs.shape[3]
    hidden = wg.shape[1]
    part = share // 2
    half = 2 * part
    z, e, x = lax.axis_index("seq"), lax.axis_index("expert"), lax.axis_index("mp")
    other = x + 1 - 2 * rem(x, 2)
    own_kind = rem(x + z, 2)
    spot = [place(c, z, x) for c in range(2)]
    after = [coords(c, rem(spot[c] + 1, RING)) for c in range(2)]
    before = [coords(c, rem(spot[c] + RING - 1, RING)) for c in range(2)]
    to = [peer(*after[0]), peer(*before[0]), peer(*after[1]), peer(*before[1])]

    mates = [(j, mine) for j in range(count) for mine in (True, False) if j or not mine]

    def mate(j, mine):
        return {"seq": z, "expert": rem(e + j, count), "mp": x if mine else other}

    def column_slot(j, mine):
        return rem(x if mine else other, 2) * count + rem(e + j, count)

    loads = [
        pltpu.make_async_copy(wg_hbm.at[0], wg, w_sem.at[0]),
        pltpu.make_async_copy(wu_hbm.at[0], wu, w_sem.at[1]),
    ]
    for c in range(2):
        loads.append(pltpu.make_async_copy(wd_hbm.at[0, :, pl.ds(c * share, share)], wd.at[c], w_sem.at[2 + c]))

    barrier = pltpu.get_barrier_semaphore()
    for j, mine in mates:
        pl.semaphore_signal(barrier, inc=1, device_id=mate(j, mine), device_id_type=MESH)
    for r in range(4):
        pl.semaphore_signal(barrier, inc=1, device_id=to[r], device_id_type=MESH)
    tiles = part // 128
    row = lax.broadcasted_iota(jnp.int32, (count * capacity, 128), 0)
    expert = jnp.zeros((count * capacity, 128), jnp.int32)
    for m in range(1, count):
        expert = expert + (row >= m * capacity).astype(jnp.int32)
    place_in = (row - capacity * expert + 1).astype(F32)
    expert = expert.astype(F32)
    named = (plan_ref[0:1, :] == expert) | (plan_ref[1:2, :] == expert)
    chosen = jnp.where(named, plan_ref[2:3, :], 0.0)
    upto = lax.broadcasted_iota(jnp.int32, (128, 128), 0) <= lax.broadcasted_iota(jnp.int32, (128, 128), 1)
    nth = jnp.dot(chosen.astype(BF), upto.astype(F32).astype(BF), preferred_element_type=F32)
    pick = jnp.where(nth == place_in, chosen, 0.0).astype(BF)[:, : tok_ref.shape[0]]
    length = send_ref.shape[3]
    for kind, source in enumerate((tok_ref, grad_ref)):
        for c in range(2):
            for k in range(2):
                begin = c * share + k * part
                picked = jnp.dot(pick, source[:, begin:begin + part], preferred_element_type=F32)
                for j in range(tiles):
                    where = k * count * length + c * tiles + j
                    flat[pl.ds(where, count * capacity, stride=2 * tiles), :] = picked[:, j * 128:(j + 1) * 128]
        for k in range(2):
            for i in range(count):
                begin = (k * count + i) * length
                send_ref[kind, k, i] = flat[begin:begin + length, :].astype(BF)

    pl.semaphore_wait(barrier, len(mates) + 4)

    my_slot = column_slot(0, True)
    own_copies = [
        pltpu.make_async_copy(send_ref.at[own_kind, k, e], got.at[k, my_slot], in_own.at[k]) for k in range(2)
    ]

    def bring(k, j, mine):
        return pltpu.make_async_remote_copy(
            src_ref=send_ref.at[own_kind if mine else 1 - own_kind, k, rem(e + j, count)],
            dst_ref=got.at[k, my_slot],
            send_sem=in_send.at[k], recv_sem=in_recv.at[k],
            device_id=mate(j, mine), device_id_type=MESH,
        )

    def bulk(ref, send_sem, recv_sem):
        return pltpu.make_async_remote_copy(
            src_ref=ref, dst_ref=ref, send_sem=send_sem, recv_sem=recv_sem, device_id=to[0], device_id_type=MESH
        )

    def brought(k):
        return bulk(got.at[k, pl.ds(0, len(mates))], in_send.at[k], in_recv.at[k])

    for k in range(2):
        own_copies[k].start()
        for j, mine in mates:
            bring(k, j, mine).start()
    for load in loads:
        load.start()

    def held(r, s):
        c = r // 2
        return rem(spot[c] + RING - s, RING) if r % 2 == 0 else rem(spot[c] + s, RING)

    def gather(r, s, k, where):
        block = xs.at[r // 2, where, :, pl.ds(k * part, part)]
        return pltpu.make_async_remote_copy(
            src_ref=block, dst_ref=block, send_sem=ag_send.at[r], recv_sem=ag_recv.at[r % 2, s, k],
            device_id=to[r], device_id_type=MESH,
        )

    for k in range(2):
        own_copies[k].wait()
        brought(k).wait_recv()
        length = got.shape[2]
        for i in range(2 * count):
            flat[i * length:(i + 1) * length, :] = got[k, i].astype(F32)
        for c in range(2):
            for j in range(tiles):
                block = flat[pl.ds(c * tiles + j, rows, stride=2 * tiles), :]
                begin = k * part + j * 128
                xs[c, spot[c], :, begin:begin + 128] = block.astype(BF)
        for r in range(4):
            gather(r, 1, k, spot[r // 2]).start()
    for load in loads:
        load.wait()

    def forward_unit(unit):
        b = div(unit, 4)
        c = div(rem(unit, 4), 2)
        kind = rem(unit, 2)
        p = spot[0] * (1 - c) + spot[1] * c
        begin = pl.multiple_of(c * share, share)

        def positions(parity):
            low = p - GROUP * (b + 1)
            low = low + rem(low + parity + 2 * RING, 2) + RING
            high = p + GROUP * b
            high = high + rem(high + parity, 2)
            return [div(rem(q, RING), 2) for q in (low, low + 2, high, high + 2)]

        @pl.when(kind == 0)
        def _():
            where = positions(0)
            lhs = jnp.concatenate([xs[c, 2 * t] for t in where], axis=0)
            gate = jnp.dot(lhs, wg[pl.ds(begin, share), :], preferred_element_type=F32)
            up = jnp.dot(lhs, wu[pl.ds(begin, share), :], preferred_element_type=F32)
            for i, t in enumerate(where):
                acc_t[c, t, :, :hidden] = gate[i * rows:(i + 1) * rows]
                acc_t[c, t, :, hidden:] = up[i * rows:(i + 1) * rows]

        @pl.when(kind == 1)
        def _():
            where = positions(1)
            lhs = jnp.concatenate([xs[c, 2 * t + 1] for t in where], axis=0)
            grad = dot_nt(lhs, wd[c])
            for i, t in enumerate(where):
                acc_g[c, t] = grad[i * rows:(i + 1) * rows]

    def gathered(d, s, k):
        return bulk(local.at[0, pl.ds(0, 2)], ag_send.at[d], ag_recv.at[d, s, k])

    def ag_step(s, carry):
        for k in range(2):
            for d in range(2):
                gathered(d, s, k).wait_recv()
                for r in (d, d + 2):
                    if d == k:
                        gather(r, s + 1, k, held(r, s)).start()
                    else:
                        @pl.when(s < HOPS - 1)
                        def _():
                            gather(r, s + 1, k, held(r, s)).start()

        @pl.when(s >= GROUP)
        def _():
            forward_unit(s - GROUP)

        return carry

    lax.fori_loop(1, HOPS, ag_step, 0)
    for d in range(2):
        gathered(d, HOPS, d).wait_recv()

    def tail_unit(u, carry):
        forward_unit(u)
        return carry

    lax.fori_loop(HOPS - GROUP, HOPS, tail_unit, 0)

    ones = jnp.ones((8, 128), F32)
    for pair in range(16):
        pz, px = pair // 2, 2 * (pair % 2)
        holders = [(pz, px), (pz, px + 1)]
        if (px + pz) % 2:
            holders = holders[::-1]
        t = [place(c, *holders[0]) // 2 for c in range(2)]
        g = [place(c, *holders[1]) // 2 for c in range(2)]
        pre_gate = acc_t[0, t[0], :, :hidden] + acc_t[1, t[1], :, :hidden]
        pre_up = acc_t[0, t[0], :, hidden:] + acc_t[1, t[1], :, hidden:]
        grad_hidden = acc_g[0, g[0]] + acc_g[1, g[1]]
        sigma = jax.nn.sigmoid(pre_gate)
        act = pre_gate * sigma
        inner = grad_hidden * act * pre_up
        grad_gate = (grad_hidden * pre_up * sigma * (1.0 + pre_gate * (1.0 - sigma))).astype(BF)
        grad_up = (grad_hidden * act).astype(BF)
        for c in range(2):
            for q in (2 * t[c], 2 * g[c] + 1):
                grads[c, q, :, :hidden] = grad_gate
                grads[c, q, :, hidden:] = grad_up
        folded = inner[:, 0:128]
        for i in range(1, hidden // 128):
            folded = folded + inner[:, i * 128:(i + 1) * 128]
        sums = dot_nt(ones, folded, precision=lax.Precision.HIGHEST)
        for q in (2 * t[0], 2 * g[0] + 1):
            dots[q, :, :rows] = sums

    def dest(r, s):
        c = r // 2
        return rem(spot[c] + HOPS + RING - s, RING) if r % 2 == 0 else rem(spot[c] + HOPS + s, RING)

    def backward_unit(unit):
        b = div(unit, 4)
        c = div(rem(unit, 4), 2)
        kind = rem(unit, 2)
        p = spot[0] * (1 - c) + spot[1] * c
        low = p + HOPS + RING - GROUP * b - (GROUP - 1)
        low = low + rem(low + kind, 2)
        high = p + HOPS + GROUP * b + 1
        high = high + rem(high + kind, 2)
        where = [2 * div(rem(q, RING), 2) + kind for q in (low, low + 2, high, high + 2)]
        lhs = jnp.concatenate([grads[c, q] for q in where], axis=0)
        begin = pl.multiple_of(kind * half + c * part, part)
        y = dot_nt(lhs[:, :hidden], wg[pl.ds(begin, part), :]) + dot_nt(lhs[:, hidden:], wu[pl.ds(begin, part), :])
        for i in range(GROUP):
            local[c, where[i]] = y[i * rows:(i + 1) * rows].astype(local.dtype)

    cut = part // CUTS
    mine_of = [[d * (CUTS // 2) + i for i in range(CUTS // 2)] for d in range(2)]

    def scatter(r, s, k, src=None, first=False):
        lanes = pl.ds(k * cut, cut)
        return pltpu.make_async_remote_copy(
            src_ref=running.at[r, s - 1, :, lanes] if src is None else src, dst_ref=running.at[r, s, :, lanes],
            send_sem=(rs_first if first else rs_send).at[r], recv_sem=rs_recv.at[r % 2, s, k],
            device_id=to[r], device_id_type=MESH,
        )

    def scatter_local(r, s, k):
        return scatter(r, s, k, local.at[r // 2, dest(r, s), :, pl.ds(k * cut, cut)], s == 0)

    def scattered(d, s, k):
        return bulk(running.at[pl.ds(0, 2), 0, :, pl.ds(0, cut)], rs_send.at[d], rs_recv.at[d, s, k])

    def add_local(r, s, k):
        lanes = slice(k * cut, (k + 1) * cut)
        total = running[r, s - 1, :, lanes].astype(F32) + local[r // 2, dest(r, s), :, lanes].astype(F32)
        running[r, s - 1, :, lanes] = total.astype(BF)

    def dot_copy(d, s, src):
        return pltpu.make_async_remote_copy(
            src_ref=src, dst_ref=dot_slots.at[d, s], send_sem=dot_send.at[d], recv_sem=dot_recv.at[s],
            device_id=to[d], device_id_type=MESH,
        )

    def dotted(s, copies):
        return bulk(dots.at[pl.ds(0, copies)], dot_send.at[0], dot_recv.at[s])

    def head_unit(u, carry):
        backward_unit(u)
        return carry

    for c in range(2):
        lax.fori_loop(2 * c, 2 * c + 2, head_unit, 0)
        for r in (2 * c, 2 * c + 1):
            for k in mine_of[r % 2]:
                scatter_local(r, 0, k).start()
        for r in (2 * c, 2 * c + 1):
            for k in mine_of[1 - r % 2]:
                scatter_local(r, 1, k).start()
    dot_copy(0, 0, dots.at[dest(0, 0)]).start()
    dot_copy(1, 1, dots.at[dest(1, 1)]).start()
    backward_unit(jnp.int32(GROUP))

    for i in range(CUTS // 2):
        for d in range(2):
            k = mine_of[d][i]
            scattered(d, 0, k).wait_recv()
            for r in (d, d + 2):
                add_local(r, 1, k)
                scatter(r, 1, k).start()
    dotted(0, 1).wait_recv()
    dot_slots[0, 0] = dot_slots[0, 0] + dots[dest(0, 1)]
    dot_copy(0, 1, dot_slots.at[0, 0]).start()
    backward_unit(jnp.int32(GROUP + 1))

    def rs_step(s, carry):
        for turn in range(CUTS):
            for d in range(2):
                k = (mine_of[1 - d] + mine_of[d])[turn]
                scattered(d, s - 1, k).wait_recv()
                for r in (d, d + 2):
                    add_local(r, s, k)
                    scatter(r, s, k).start()
        dotted(s - 1, 2).wait_recv()
        for d in range(2):
            dot_slots[d, s - 1] = dot_slots[d, s - 1] + dots[dest(d, s)]
            dot_copy(d, s, dot_slots.at[d, s - 1]).start()

        @pl.when(s < HOPS - GROUP)
        def _():
            backward_unit(s + GROUP)

        return carry

    lax.fori_loop(2, HOPS, rs_step, 0)
    last = HOPS - 1
    tiles = part // 128
    for k in range(CUTS):
        for d in range(2):
            scattered(d, last, k).wait_recv()
        for c in range(2):
            lanes = slice(k * cut, (k + 1) * cut)
            total = running[2 * c, last, :, lanes].astype(F32) + running[2 * c + 1, last, :, lanes].astype(F32)
            total = total + local[c, spot[c], :, lanes].astype(F32)
            for j in range(tiles // CUTS):
                line = c * tiles + k * (tiles // CUTS) + j
                flat[pl.ds(line, rows, stride=2 * tiles), :] = total[:, j * 128:(j + 1) * 128]
    length = leave.shape[1]
    for i in range(2 * count):
        leave[i] = flat[i * length:(i + 1) * length, :].astype(BF)
    dotted(last, 2).wait_recv()
    dot_out[...] = dot_slots[0, last] + dot_slots[1, last] + dots[spot[0]]

    def giveback(i, j, mine, src, dst):
        return pltpu.make_async_remote_copy(
            src_ref=src, dst_ref=dst,
            send_sem=out_send.at[i], recv_sem=out_recv.at[i],
            device_id=mate(j, mine), device_id_type=MESH,
        )

    returned = [
        bulk(ref.at[pl.ds(0, len(mates))], out_send.at[i], out_recv.at[i]) for i, ref in enumerate((leave, dots))
    ]
    finals = [
        pltpu.make_async_copy(leave.at[my_slot], back_ref.at[own_kind, e], out_own.at[0]),
        pltpu.make_async_copy(dot_out, back_dots.at[own_kind, e], out_own.at[1]),
    ]
    for final in finals:
        final.start()
    for j, mine in mates:
        giveback(0, j, mine, leave.at[column_slot(j, mine)], back_ref.at[own_kind, e]).start()
        giveback(1, j, mine, dot_out, back_dots.at[own_kind, e]).start()

    for k in range(2):
        brought(k).wait_send()
    for r in range(4):
        bulk(local.at[0, pl.ds(0, 2 * HOPS - 1)], ag_send.at[r], ag_recv.at[0, 0, 0]).wait_send()
        bulk(local.at[0, 0, :, pl.ds(0, part // 2)], rs_first.at[r], rs_recv.at[0, 0, 0]).wait_send()
        bulk(local.at[0, pl.ds(0, HOPS - 1)], rs_send.at[r], rs_recv.at[0, 0, 0]).wait_send()
    for d in range(2):
        bulk(dots.at[pl.ds(0, HOPS - d)], dot_send.at[d], dot_recv.at[0]).wait_send()
    for copy in returned:
        copy.wait_send()
    for final in finals:
        final.wait()
    for copy in returned:
        copy.wait_recv()


def run_experts(count, plan, tokens, out_grad, gate_weight, up_weight, down_weight):
    width, hidden = gate_weight.shape[1:]
    share, part = width // 2, width // 4
    capacity = 3 * tokens.shape[0] // 8
    length = capacity * 2 * part // 128
    rows = 2 * count * capacity
    vmem = pl.BlockSpec(memory_space=pltpu.VMEM)
    hbm = pl.BlockSpec(memory_space=pl.ANY)
    return pl.pallas_call(
        experts_kernel,
        out_shape=(
            jax.ShapeDtypeStruct((2, count, length, 128), BF),
            jax.ShapeDtypeStruct((2, count, 8, 128), F32),
        ),
        in_specs=[vmem, vmem, vmem, hbm, hbm, hbm],
        out_specs=(vmem, vmem),
        scratch_shapes=[
            pltpu.VMEM((2, 2, count, length, 128), BF),
            pltpu.VMEM((2, 2 * count, length, 128), BF),
            pltpu.VMEM((2 * count * length, 128), F32),
            pltpu.VMEM((2 * count, length, 128), BF),
            pltpu.VMEM((2, RING, rows, share), BF),
            pltpu.VMEM((4, HOPS, rows, part), BF),
            pltpu.VMEM((2, RING, rows, part), BF),
            pltpu.VMEM((2, 16, rows, 2 * hidden), F32),
            pltpu.VMEM((2, 16, rows, hidden), F32),
            pltpu.VMEM((2, RING, rows, 2 * hidden), BF),
            pltpu.VMEM((RING, 8, 128), F32),
            pltpu.VMEM((2, HOPS, 8, 128), F32),
            pltpu.VMEM((8, 128), F32),
            pltpu.VMEM((width, hidden), BF),
            pltpu.VMEM((width, hidden), BF),
            pltpu.VMEM((2, hidden, share), BF),
            pltpu.SemaphoreType.DMA((4,)),
            pltpu.SemaphoreType.DMA((2,)),
            pltpu.SemaphoreType.DMA((2,)),
            pltpu.SemaphoreType.DMA((2,)),
            pltpu.SemaphoreType.DMA((4,)),
            pltpu.SemaphoreType.DMA((2, HOPS + 1, 2)),
            pltpu.SemaphoreType.DMA((4,)),
            pltpu.SemaphoreType.DMA((4,)),
            pltpu.SemaphoreType.DMA((2, HOPS, CUTS)),
            pltpu.SemaphoreType.DMA((2,)),
            pltpu.SemaphoreType.DMA((HOPS,)),
            pltpu.SemaphoreType.DMA((2,)),
            pltpu.SemaphoreType.DMA((2,)),
            pltpu.SemaphoreType.DMA((2,)),
        ],
        compiler_params=pltpu.CompilerParams(
            collective_id=0, has_side_effects=True, vmem_limit_bytes=63 << 20
        ),
        name="experts",
    )(plan, tokens, out_grad, gate_weight, up_weight, down_weight)


def on_device(tokens, out_grad, kept_mask, routes, router, gate_weight, up_weight, down_weight):
    row_count, width = tokens.shape
    count = lax.axis_size("expert")
    capacity = 3 * row_count // 8
    columns = lax.broadcasted_iota(jnp.int32, (row_count, count), 1)
    first_hot = (routes[:, 0:1] == columns).astype(F32)
    second_hot = (routes[:, 1:2] == columns).astype(F32)
    keep_rows = kept_mask.astype(F32)
    chosen = ((first_hot + second_hot) * keep_rows[:, None]).astype(jnp.int32)
    position = jnp.cumsum(chosen, axis=0) - 1
    slot_iota = lax.broadcasted_iota(jnp.int32, (row_count, count, capacity), 2)
    select_mask = (chosen[:, :, None] == 1) & (position[:, :, None] == slot_iota)
    select_bf = select_mask.astype(BF)
    select_full = select_mask.astype(F32)
    plan = jnp.concatenate([routes.astype(F32).T, keep_rows[None]], axis=0)
    plan = jnp.pad(plan, ((0, 5), (0, 128 - row_count)))
    back, back_dots = run_experts(count, plan, tokens, out_grad, gate_weight, up_weight, down_weight)
    back = back.reshape(2, count, capacity, width // 2)
    own_slot = rem(lax.axis_index("mp"), 2) * count + lax.axis_index("expert")
    dot_back = lax.dynamic_slice_in_dim(back_dots[0, :, 0, :], own_slot * capacity, capacity, 1)

    logits = jnp.dot(tokens, router, preferred_element_type=F32)
    first_logit = jnp.sum(logits * first_hot, axis=1)
    second_logit = jnp.sum(logits * second_hot, axis=1)
    gate_first = jax.nn.sigmoid(first_logit - second_logit)
    gate_second = jax.nn.sigmoid(second_logit - first_logit)
    gate_table = (first_hot * gate_first[:, None] + second_hot * gate_second[:, None]).astype(BF)
    weigh = select_bf * gate_table[:, :, None]
    expert_sum = jnp.einsum("tec,kecd->tkd", weigh, back, preferred_element_type=F32)
    expert_sum = expert_sum.reshape(row_count, width)
    dot_table = jnp.sum(select_full * dot_back[None], axis=2)
    dot_first = jnp.sum(dot_table * first_hot, axis=1)
    dot_second = jnp.sum(dot_table * second_hot, axis=1)
    product = gate_first * gate_second * keep_rows
    grad_first = product * (dot_first - dot_second)
    grad_second = product * (dot_second - dot_first)
    logit_grad = first_hot * grad_first[:, None] + second_hot * grad_second[:, None]
    router_term = jnp.dot(logit_grad, router.astype(F32).T, precision=lax.Precision.HIGHEST)
    d_tokens = ((expert_sum + router_term) * keep_rows[:, None]).astype(BF)
    gate_grad = jnp.stack([grad_first, grad_second], axis=1)
    return (d_tokens, gate_grad)


def solution(mesh):
    return jax.shard_map(
        on_device,
        mesh=mesh,
        in_specs=(
            P(("seq", "expert", "mp"), None),
            P(("seq", "expert", "mp"), None),
            P(("seq", "expert", "mp")),
            P(("seq", "expert", "mp"), None),
            P(),
            P("expert", None, ("seq", "mp")),
            P("expert", None, ("seq", "mp")),
            P("expert", ("seq", "mp"), None),
        ),
        out_specs=(P(("seq", "expert", "mp"), None), P(("seq", "expert", "mp"), None)),
        check_vma=False,
    )
```

```python
import functools

import jax
import jax.numpy as jnp
from jax import lax
from jax.experimental import pallas as pl
from jax.experimental.pallas import tpu as pltpu
from jax.sharding import PartitionSpec as P

MESH = pl.DeviceIdType.MESH
BF = jnp.bfloat16
F32 = jnp.float32
RING = 32
HOPS = 16
GROUP = 4
CUTS = 4


def div(a, b):
    return a // b if isinstance(a, int) else lax.div(a, jnp.int32(b))


def rem(a, b):
    return a % b if isinstance(a, int) else lax.rem(a, jnp.int32(b))


def place(cycle, z, x):
    if cycle == 0:
        return 4 * z + rem(x + z, 4)
    turn = rem(z + 5 * x, 8)
    return 4 * x + 16 * div(turn, 4) + rem(turn, 4)


def coords(cycle, q):
    a, b = div(q, 4), rem(q, 4)
    if cycle == 0:
        return a, rem(b - a + 8, 4)
    return rem(3 * a + b, 8), rem(a, 4)


def peer(z, x):
    return {"seq": z, "mp": x}


def dot_nt(a, b, **kwargs):
    return lax.dot_general(a, b, (((1,), (1,)), ((), ())), preferred_element_type=F32, **kwargs)


def experts_kernel(
    routes_ref, kept_ref, router_ref, tok_ref, grad_ref, wg_hbm, wu_hbm, wd_hbm, out_ref, gate_grad_ref,
    back_ref, back_dots, send_ref, got, flat, leave, xs, running, local, acc_t, acc_g, grads, dots, dot_slots, dot_out, wg, wu, wd,
    w_sem, in_own, in_send, in_recv, ag_send, ag_recv, rs_first, rs_send, rs_recv, dot_send, dot_recv,
    out_own, out_send, out_recv,
):
    count = send_ref.shape[2]
    tokens = tok_ref.shape[0]
    capacity = 3 * tokens // 8
    rows, share = xs.shape[2], xs.shape[3]
    hidden = wg.shape[1]
    part = share // 2
    half = 2 * part
    z, e, x = lax.axis_index("seq"), lax.axis_index("expert"), lax.axis_index("mp")
    other = x + 1 - 2 * rem(x, 2)
    own_kind = rem(x + z, 2)
    spot = [place(c, z, x) for c in range(2)]
    after = [coords(c, rem(spot[c] + 1, RING)) for c in range(2)]
    before = [coords(c, rem(spot[c] + RING - 1, RING)) for c in range(2)]
    to = [peer(*after[0]), peer(*before[0]), peer(*after[1]), peer(*before[1])]

    mates = [(j, mine) for j in range(count) for mine in (True, False) if j or not mine]

    def mate(j, mine):
        return {"seq": z, "expert": rem(e + j, count), "mp": x if mine else other}

    def column_slot(j, mine):
        return rem(x if mine else other, 2) * count + rem(e + j, count)

    loads = [
        pltpu.make_async_copy(wg_hbm.at[0], wg, w_sem.at[0]),
        pltpu.make_async_copy(wu_hbm.at[0], wu, w_sem.at[1]),
    ]
    for c in range(2):
        loads.append(pltpu.make_async_copy(wd_hbm.at[0, :, pl.ds(c * share, share)], wd.at[c], w_sem.at[2 + c]))

    barrier = pltpu.get_barrier_semaphore()
    for j, mine in mates:
        pl.semaphore_signal(barrier, inc=1, device_id=mate(j, mine), device_id_type=MESH)
    for r in range(4):
        pl.semaphore_signal(barrier, inc=1, device_id=to[r], device_id_type=MESH)
    tiles = part // 128
    table = (count * capacity, tokens)
    row = lax.broadcasted_iota(jnp.int32, table, 0)
    expert = jnp.zeros(table, jnp.int32)
    for m in range(1, count):
        expert = expert + (row >= m * capacity).astype(jnp.int32)
    slot_of = row - capacity * expert
    kept = kept_ref[...].astype(F32)
    is_first = routes_ref[0:1, :] == expert
    is_second = routes_ref[1:2, :] == expert
    chosen = jnp.where(is_first | is_second, 1.0, 0.0) * kept
    square = (tokens, tokens)
    down, across = lax.broadcasted_iota(jnp.int32, square, 0), lax.broadcasted_iota(jnp.int32, square, 1)
    upto = jnp.where(down <= across, 1.0, 0.0).astype(BF)
    nth = jnp.dot(chosen.astype(BF), upto, preferred_element_type=F32)
    pick_full = jnp.where(nth == (slot_of + 1).astype(F32), chosen, 0.0)
    pick = pick_full.astype(BF)
    length = send_ref.shape[3]
    for kind, source in enumerate((tok_ref, grad_ref)):
        for c in range(2):
            for k in range(2):
                begin = c * share + k * part
                picked = jnp.dot(pick, source[:, begin:begin + part], preferred_element_type=F32)
                for j in range(tiles):
                    where = k * count * length + c * tiles + j
                    flat[pl.ds(where, count * capacity, stride=2 * tiles), :] = picked[:, j * 128:(j + 1) * 128]
        for k in range(2):
            for i in range(count):
                begin = (k * count + i) * length
                send_ref[kind, k, i] = flat[begin:begin + length, :].astype(BF)

    logits = dot_nt(router_ref[...], tok_ref[...])
    ids = lax.broadcasted_iota(jnp.int32, (count, tokens), 0)
    first_hot = jnp.where(routes_ref[0:1, :] == ids, 1.0, 0.0)
    second_hot = jnp.where(routes_ref[1:2, :] == ids, 1.0, 0.0)
    first_logit = jnp.sum(logits * first_hot, axis=0, keepdims=True)
    second_logit = jnp.sum(logits * second_hot, axis=0, keepdims=True)
    gate_first = jax.nn.sigmoid(first_logit - second_logit)
    gate_second = jax.nn.sigmoid(second_logit - first_logit)
    eye = jnp.where(down == across, 1.0, 0.0).astype(BF)
    gate_of = jnp.where(is_first, gate_first, gate_second)
    weigh = dot_nt(eye, (pick_full * gate_of).astype(BF)).astype(BF)
    keep_column = dot_nt(eye, jnp.broadcast_to(kept, (128, tokens)).astype(BF))[:, 0:1]

    pl.semaphore_wait(barrier, len(mates) + 4)

    my_slot = column_slot(0, True)
    own_copies = [
        pltpu.make_async_copy(send_ref.at[own_kind, k, e], got.at[k, my_slot], in_own.at[k]) for k in range(2)
    ]

    def bring(k, j, mine):
        return pltpu.make_async_remote_copy(
            src_ref=send_ref.at[own_kind if mine else 1 - own_kind, k, rem(e + j, count)],
            dst_ref=got.at[k, my_slot],
            send_sem=in_send.at[k], recv_sem=in_recv.at[k],
            device_id=mate(j, mine), device_id_type=MESH,
        )

    def bulk(ref, send_sem, recv_sem):
        return pltpu.make_async_remote_copy(
            src_ref=ref, dst_ref=ref, send_sem=send_sem, recv_sem=recv_sem, device_id=to[0], device_id_type=MESH
        )

    def brought(k):
        return bulk(got.at[k, pl.ds(0, len(mates))], in_send.at[k], in_recv.at[k])

    for k in range(2):
        own_copies[k].start()
        for j, mine in mates:
            bring(k, j, mine).start()
    for load in loads:
        load.start()

    def held(r, s):
        c = r // 2
        return rem(spot[c] + RING - s, RING) if r % 2 == 0 else rem(spot[c] + s, RING)

    def gather(r, s, k, where):
        block = xs.at[r // 2, where, :, pl.ds(k * part, part)]
        return pltpu.make_async_remote_copy(
            src_ref=block, dst_ref=block, send_sem=ag_send.at[r], recv_sem=ag_recv.at[r % 2, s, k],
            device_id=to[r], device_id_type=MESH,
        )

    for k in range(2):
        own_copies[k].wait()
        brought(k).wait_recv()
        length = got.shape[2]
        for i in range(2 * count):
            flat[i * length:(i + 1) * length, :] = got[k, i].astype(F32)
        for c in range(2):
            for j in range(tiles):
                block = flat[pl.ds(c * tiles + j, rows, stride=2 * tiles), :]
                begin = k * part + j * 128
                xs[c, spot[c], :, begin:begin + 128] = block.astype(BF)
        for r in range(4):
            gather(r, 1, k, spot[r // 2]).start()
    for load in loads:
        load.wait()

    def forward_unit(unit):
        b = div(unit, 4)
        c = div(rem(unit, 4), 2)
        kind = rem(unit, 2)
        p = spot[0] * (1 - c) + spot[1] * c
        begin = pl.multiple_of(c * share, share)

        def positions(parity):
            low = p - GROUP * (b + 1)
            low = low + rem(low + parity + 2 * RING, 2) + RING
            high = p + GROUP * b
            high = high + rem(high + parity, 2)
            return [div(rem(q, RING), 2) for q in (low, low + 2, high, high + 2)]

        @pl.when(kind == 0)
        def _():
            where = positions(0)
            lhs = jnp.concatenate([xs[c, 2 * t] for t in where], axis=0)
            gate = jnp.dot(lhs, wg[pl.ds(begin, share), :], preferred_element_type=F32)
            up = jnp.dot(lhs, wu[pl.ds(begin, share), :], preferred_element_type=F32)
            for i, t in enumerate(where):
                acc_t[c, t, :, :hidden] = gate[i * rows:(i + 1) * rows]
                acc_t[c, t, :, hidden:] = up[i * rows:(i + 1) * rows]

        @pl.when(kind == 1)
        def _():
            where = positions(1)
            lhs = jnp.concatenate([xs[c, 2 * t + 1] for t in where], axis=0)
            grad = dot_nt(lhs, wd[c])
            for i, t in enumerate(where):
                acc_g[c, t] = grad[i * rows:(i + 1) * rows]

    def gathered(d, s, k):
        return bulk(local.at[0, pl.ds(0, 2)], ag_send.at[d], ag_recv.at[d, s, k])

    def ag_step(s, carry):
        for k in range(2):
            for d in range(2):
                gathered(d, s, k).wait_recv()
                for r in (d, d + 2):
                    if d == k:
                        gather(r, s + 1, k, held(r, s)).start()
                    else:
                        @pl.when(s < HOPS - 1)
                        def _():
                            gather(r, s + 1, k, held(r, s)).start()

        @pl.when(s >= GROUP)
        def _():
            forward_unit(s - GROUP)

        return carry

    lax.fori_loop(1, HOPS, ag_step, 0)
    for d in range(2):
        gathered(d, HOPS, d).wait_recv()

    def tail_unit(u, carry):
        forward_unit(u)
        return carry

    lax.fori_loop(HOPS - GROUP, HOPS, tail_unit, 0)

    ones = jnp.ones((8, 128), F32)
    for pair in range(16):
        pz, px = pair // 2, 2 * (pair % 2)
        holders = [(pz, px), (pz, px + 1)]
        if (px + pz) % 2:
            holders = holders[::-1]
        t = [place(c, *holders[0]) // 2 for c in range(2)]
        g = [place(c, *holders[1]) // 2 for c in range(2)]
        pre_gate = acc_t[0, t[0], :, :hidden] + acc_t[1, t[1], :, :hidden]
        pre_up = acc_t[0, t[0], :, hidden:] + acc_t[1, t[1], :, hidden:]
        grad_hidden = acc_g[0, g[0]] + acc_g[1, g[1]]
        sigma = jax.nn.sigmoid(pre_gate)
        act = pre_gate * sigma
        inner = grad_hidden * act * pre_up
        grad_gate = (grad_hidden * pre_up * sigma * (1.0 + pre_gate * (1.0 - sigma))).astype(BF)
        grad_up = (grad_hidden * act).astype(BF)
        for c in range(2):
            for q in (2 * t[c], 2 * g[c] + 1):
                grads[c, q, :, :hidden] = grad_gate
                grads[c, q, :, hidden:] = grad_up
        folded = inner[:, 0:128]
        for i in range(1, hidden // 128):
            folded = folded + inner[:, i * 128:(i + 1) * 128]
        sums = dot_nt(ones, folded, precision=lax.Precision.HIGHEST)
        for q in (2 * t[0], 2 * g[0] + 1):
            dots[q, :, :rows] = sums

    def dest(r, s):
        c = r // 2
        return rem(spot[c] + HOPS + RING - s, RING) if r % 2 == 0 else rem(spot[c] + HOPS + s, RING)

    def backward_unit(unit):
        b = div(unit, 4)
        c = div(rem(unit, 4), 2)
        kind = rem(unit, 2)
        p = spot[0] * (1 - c) + spot[1] * c
        low = p + HOPS + RING - GROUP * b - (GROUP - 1)
        low = low + rem(low + kind, 2)
        high = p + HOPS + GROUP * b + 1
        high = high + rem(high + kind, 2)
        where = [2 * div(rem(q, RING), 2) + kind for q in (low, low + 2, high, high + 2)]
        lhs = jnp.concatenate([grads[c, q] for q in where], axis=0)
        begin = pl.multiple_of(kind * half + c * part, part)
        y = dot_nt(lhs[:, :hidden], wg[pl.ds(begin, part), :]) + dot_nt(lhs[:, hidden:], wu[pl.ds(begin, part), :])
        for i in range(GROUP):
            local[c, where[i]] = y[i * rows:(i + 1) * rows].astype(local.dtype)

    cut = part // CUTS
    mine_of = [[d * (CUTS // 2) + i for i in range(CUTS // 2)] for d in range(2)]

    def scatter(r, s, k, src=None, first=False):
        lanes = pl.ds(k * cut, cut)
        return pltpu.make_async_remote_copy(
            src_ref=running.at[r, s - 1, :, lanes] if src is None else src, dst_ref=running.at[r, s, :, lanes],
            send_sem=(rs_first if first else rs_send).at[r], recv_sem=rs_recv.at[r % 2, s, k],
            device_id=to[r], device_id_type=MESH,
        )

    def scatter_local(r, s, k):
        return scatter(r, s, k, local.at[r // 2, dest(r, s), :, pl.ds(k * cut, cut)], s == 0)

    def scattered(d, s, k):
        return bulk(running.at[pl.ds(0, 2), 0, :, pl.ds(0, cut)], rs_send.at[d], rs_recv.at[d, s, k])

    def add_local(r, s, k):
        lanes = slice(k * cut, (k + 1) * cut)
        total = running[r, s - 1, :, lanes].astype(F32) + local[r // 2, dest(r, s), :, lanes].astype(F32)
        running[r, s - 1, :, lanes] = total.astype(BF)

    def dot_copy(d, s, src):
        return pltpu.make_async_remote_copy(
            src_ref=src, dst_ref=dot_slots.at[d, s], send_sem=dot_send.at[d], recv_sem=dot_recv.at[s],
            device_id=to[d], device_id_type=MESH,
        )

    def dotted(s, copies):
        return bulk(dots.at[pl.ds(0, copies)], dot_send.at[0], dot_recv.at[s])

    def head_unit(u, carry):
        backward_unit(u)
        return carry

    for c in range(2):
        lax.fori_loop(2 * c, 2 * c + 2, head_unit, 0)
        for r in (2 * c, 2 * c + 1):
            for k in mine_of[r % 2]:
                scatter_local(r, 0, k).start()
        for r in (2 * c, 2 * c + 1):
            for k in mine_of[1 - r % 2]:
                scatter_local(r, 1, k).start()
    dot_copy(0, 0, dots.at[dest(0, 0)]).start()
    dot_copy(1, 1, dots.at[dest(1, 1)]).start()
    backward_unit(jnp.int32(GROUP))

    for i in range(CUTS // 2):
        for d in range(2):
            k = mine_of[d][i]
            scattered(d, 0, k).wait_recv()
            for r in (d, d + 2):
                add_local(r, 1, k)
                scatter(r, 1, k).start()
    dotted(0, 1).wait_recv()
    dot_slots[0, 0] = dot_slots[0, 0] + dots[dest(0, 1)]
    dot_copy(0, 1, dot_slots.at[0, 0]).start()
    backward_unit(jnp.int32(GROUP + 1))

    def rs_step(s, carry):
        for turn in range(CUTS):
            for d in range(2):
                k = (mine_of[1 - d] + mine_of[d])[turn]
                scattered(d, s - 1, k).wait_recv()
                for r in (d, d + 2):
                    add_local(r, s, k)
                    scatter(r, s, k).start()
        dotted(s - 1, 2).wait_recv()
        for d in range(2):
            dot_slots[d, s - 1] = dot_slots[d, s - 1] + dots[dest(d, s)]
            dot_copy(d, s, dot_slots.at[d, s - 1]).start()

        @pl.when(s < HOPS - GROUP)
        def _():
            backward_unit(s + GROUP)

        return carry

    lax.fori_loop(2, HOPS, rs_step, 0)
    last = HOPS - 1
    tiles = part // 128
    for k in range(CUTS):
        for d in range(2):
            scattered(d, last, k).wait_recv()
        for c in range(2):
            lanes = slice(k * cut, (k + 1) * cut)
            total = running[2 * c, last, :, lanes].astype(F32) + running[2 * c + 1, last, :, lanes].astype(F32)
            total = total + local[c, spot[c], :, lanes].astype(F32)
            for j in range(tiles // CUTS):
                line = c * tiles + k * (tiles // CUTS) + j
                flat[pl.ds(line, rows, stride=2 * tiles), :] = total[:, j * 128:(j + 1) * 128]
    length = leave.shape[1]
    for i in range(2 * count):
        leave[i] = flat[i * length:(i + 1) * length, :].astype(BF)
    dotted(last, 2).wait_recv()
    dot_out[...] = dot_slots[0, last] + dot_slots[1, last] + dots[spot[0]]

    def giveback(i, j, mine, src, dst):
        return pltpu.make_async_remote_copy(
            src_ref=src, dst_ref=dst,
            send_sem=out_send.at[i], recv_sem=out_recv.at[i],
            device_id=mate(j, mine), device_id_type=MESH,
        )

    returned = [
        bulk(ref.at[pl.ds(0, len(mates))], out_send.at[i], out_recv.at[i]) for i, ref in enumerate((leave, dots))
    ]
    finals = [
        pltpu.make_async_copy(leave.at[my_slot], back_ref.at[own_kind, e], out_own.at[0]),
        pltpu.make_async_copy(dot_out, back_dots.at[own_kind, e], out_own.at[1]),
    ]
    for final in finals:
        final.start()
    for j, mine in mates:
        giveback(0, j, mine, leave.at[column_slot(j, mine)], back_ref.at[own_kind, e]).start()
        giveback(1, j, mine, dot_out, back_dots.at[own_kind, e]).start()

    for k in range(2):
        brought(k).wait_send()
    for r in range(4):
        bulk(local.at[0, pl.ds(0, 2 * HOPS - 1)], ag_send.at[r], ag_recv.at[0, 0, 0]).wait_send()
        bulk(local.at[0, 0, :, pl.ds(0, part // 2)], rs_first.at[r], rs_recv.at[0, 0, 0]).wait_send()
        bulk(local.at[0, pl.ds(0, HOPS - 1)], rs_send.at[r], rs_recv.at[0, 0, 0]).wait_send()
    for d in range(2):
        bulk(dots.at[pl.ds(0, HOPS - d)], dot_send.at[d], dot_recv.at[0]).wait_send()
    for copy in returned:
        copy.wait_send()
    for final in finals:
        final.wait()
    for copy in returned:
        copy.wait_recv()

    for i in range(count):
        flat[i * capacity:(i + 1) * capacity, :] = back_dots[0, i, 0:capacity, :]
    lane = lax.broadcasted_iota(jnp.int32, (count * capacity, 128), 1)
    row = lax.broadcasted_iota(jnp.int32, (count * capacity, 128), 0)
    wanted = row + capacity * my_slot
    for m in range(1, count):
        wanted = wanted - capacity * (row >= m * capacity).astype(jnp.int32)
    dot_column = jnp.where(lane == wanted, flat[0:count * capacity, :], 0.0)
    dot_column = jnp.sum(dot_column, axis=1, keepdims=True)
    dot_first = jnp.sum(jnp.where(is_first, pick_full, 0.0) * dot_column, axis=0, keepdims=True)
    dot_second = jnp.sum(jnp.where(is_second, pick_full, 0.0) * dot_column, axis=0, keepdims=True)
    product = gate_first * gate_second * kept
    grad_first = product * (dot_first - dot_second)
    grad_second = product * (dot_second - dot_first)
    gate_grad_ref[0:1, :] = grad_first
    gate_grad_ref[1:2, :] = grad_second
    logit_grad = first_hot * grad_first + second_hot * grad_second
    high = logit_grad.astype(BF)
    low = (logit_grad - high.astype(F32)).astype(BF)
    pieces = jnp.concatenate([dot_nt(eye, high), dot_nt(eye, low)], axis=0).astype(BF)
    for kind in range(2):
        for i in range(count):
            flat[i * length:(i + 1) * length, :] = back_ref[kind, i].astype(F32)
        parts = [flat[pl.ds(i, count * capacity, stride=2 * tiles), :].astype(BF) for i in range(2 * tiles)]
        total = jnp.dot(weigh, jnp.concatenate(parts, axis=1), preferred_element_type=F32)
        lanes = slice(kind * half, (kind + 1) * half)
        term = jnp.dot(pieces, router_ref[:, lanes], preferred_element_type=F32)
        out_ref[:, lanes] = ((total + (term[:tokens] + term[tokens:])) * keep_column).astype(BF)


def run_experts(count, routes, kept, router, tokens, out_grad, gate_weight, up_weight, down_weight):
    width, hidden = gate_weight.shape[1:]
    share, part = width // 2, width // 4
    capacity = 3 * tokens.shape[0] // 8
    length = capacity * 2 * part // 128
    rows = 2 * count * capacity
    vmem = pl.BlockSpec(memory_space=pltpu.VMEM)
    hbm = pl.BlockSpec(memory_space=pl.ANY)
    return pl.pallas_call(
        experts_kernel,
        out_shape=(
            jax.ShapeDtypeStruct(tokens.shape, BF),
            jax.ShapeDtypeStruct(routes.shape, F32),
        ),
        in_specs=[vmem, vmem, vmem, vmem, vmem, hbm, hbm, hbm],
        out_specs=(vmem, vmem),
        scratch_shapes=[
            pltpu.VMEM((2, count, length, 128), BF),
            pltpu.VMEM((2, count, 8, 128), F32),
            pltpu.VMEM((2, 2, count, length, 128), BF),
            pltpu.VMEM((2, 2 * count, length, 128), BF),
            pltpu.VMEM((2 * count * length, 128), F32),
            pltpu.VMEM((2 * count, length, 128), BF),
            pltpu.VMEM((2, RING, rows, share), BF),
            pltpu.VMEM((4, HOPS, rows, part), BF),
            pltpu.VMEM((2, RING, rows, part), BF),
            pltpu.VMEM((2, 16, rows, 2 * hidden), F32),
            pltpu.VMEM((2, 16, rows, hidden), F32),
            pltpu.VMEM((2, RING, rows, 2 * hidden), BF),
            pltpu.VMEM((RING, 8, 128), F32),
            pltpu.VMEM((2, HOPS, 8, 128), F32),
            pltpu.VMEM((8, 128), F32),
            pltpu.VMEM((width, hidden), BF),
            pltpu.VMEM((width, hidden), BF),
            pltpu.VMEM((2, hidden, share), BF),
            pltpu.SemaphoreType.DMA((4,)),
            pltpu.SemaphoreType.DMA((2,)),
            pltpu.SemaphoreType.DMA((2,)),
            pltpu.SemaphoreType.DMA((2,)),
            pltpu.SemaphoreType.DMA((4,)),
            pltpu.SemaphoreType.DMA((2, HOPS + 1, 2)),
            pltpu.SemaphoreType.DMA((4,)),
            pltpu.SemaphoreType.DMA((4,)),
            pltpu.SemaphoreType.DMA((2, HOPS, CUTS)),
            pltpu.SemaphoreType.DMA((2,)),
            pltpu.SemaphoreType.DMA((HOPS,)),
            pltpu.SemaphoreType.DMA((2,)),
            pltpu.SemaphoreType.DMA((2,)),
            pltpu.SemaphoreType.DMA((2,)),
        ],
        compiler_params=pltpu.CompilerParams(
            collective_id=0, has_side_effects=True, vmem_limit_bytes=63 << 20
        ),
        name="experts",
    )(routes, kept, router, tokens, out_grad, gate_weight, up_weight, down_weight)


def on_device(tokens, out_grad, kept_mask, routes, router, gate_weight, up_weight, down_weight):
    d_tokens, gate_grad = run_experts(
        lax.axis_size("expert"), routes.T, kept_mask[None], router.T, tokens, out_grad,
        gate_weight, up_weight, down_weight,
    )
    return (d_tokens, gate_grad.T)


def solution(mesh):
    return jax.shard_map(
        on_device,
        mesh=mesh,
        in_specs=(
            P(("seq", "expert", "mp"), None),
            P(("seq", "expert", "mp"), None),
            P(("seq", "expert", "mp")),
            P(("seq", "expert", "mp"), None),
            P(),
            P("expert", None, ("seq", "mp")),
            P("expert", None, ("seq", "mp")),
            P("expert", ("seq", "mp"), None),
        ),
        out_specs=(P(("seq", "expert", "mp"), None), P(("seq", "expert", "mp"), None)),
        check_vma=False,
    )
```

```python
import functools

import jax
import jax.numpy as jnp
from jax import lax
from jax.experimental import pallas as pl
from jax.experimental.pallas import tpu as pltpu
from jax.sharding import PartitionSpec as P

MESH = pl.DeviceIdType.MESH
BF = jnp.bfloat16
F32 = jnp.float32
RING = 32
HOPS = 16
GROUP = 4
CUTS = 4


def div(a, b):
    return a // b if isinstance(a, int) else lax.div(a, jnp.int32(b))


def rem(a, b):
    return a % b if isinstance(a, int) else lax.rem(a, jnp.int32(b))


def place(cycle, z, x):
    if cycle == 0:
        return 4 * z + rem(x + z, 4)
    turn = rem(z + 5 * x, 8)
    return 4 * x + 16 * div(turn, 4) + rem(turn, 4)


def coords(cycle, q):
    a, b = div(q, 4), rem(q, 4)
    if cycle == 0:
        return a, rem(b - a + 8, 4)
    return rem(3 * a + b, 8), rem(a, 4)


def peer(z, x):
    return {"seq": z, "mp": x}


def dot_nt(a, b, **kwargs):
    return lax.dot_general(a, b, (((1,), (1,)), ((), ())), preferred_element_type=F32, **kwargs)


def experts_kernel(
    routes_ref, kept_ref, router_ref, tok_ref, grad_ref, wg_hbm, wu_hbm, wd_hbm, out_ref, gate_grad_ref,
    back_ref, back_dots, send_ref, got, flat, leave, xs, running, first, local, acc_t, acc_g, grads, dots, dot_slots, dot_out, wg, wu, wd,
    w_sem, in_own, in_send, in_recv, ag_send, ag_recv, rs_first, rs_send, rs_recv, dot_send, dot_recv,
    out_own, out_send, out_recv,
):
    count = send_ref.shape[2]
    tokens = tok_ref.shape[0]
    capacity = 3 * tokens // 8
    rows, share = xs.shape[2], xs.shape[3]
    hidden = wg.shape[1]
    part = share // 2
    half = 2 * part
    z, e, x = lax.axis_index("seq"), lax.axis_index("expert"), lax.axis_index("mp")
    other = x + 1 - 2 * rem(x, 2)
    own_kind = rem(x + z, 2)
    spot = [place(c, z, x) for c in range(2)]
    after = [coords(c, rem(spot[c] + 1, RING)) for c in range(2)]
    before = [coords(c, rem(spot[c] + RING - 1, RING)) for c in range(2)]
    to = [peer(*after[0]), peer(*before[0]), peer(*after[1]), peer(*before[1])]

    mates = [(j, mine) for j in range(count) for mine in (True, False) if j or not mine]

    def mate(j, mine):
        return {"seq": z, "expert": rem(e + j, count), "mp": x if mine else other}

    def column_slot(j, mine):
        return rem(x if mine else other, 2) * count + rem(e + j, count)

    loads = [
        pltpu.make_async_copy(wg_hbm.at[0], wg, w_sem.at[0]),
        pltpu.make_async_copy(wu_hbm.at[0], wu, w_sem.at[1]),
    ]
    for c in range(2):
        loads.append(pltpu.make_async_copy(wd_hbm.at[0, :, pl.ds(c * share, share)], wd.at[c], w_sem.at[2 + c]))

    barrier = pltpu.get_barrier_semaphore()
    for j, mine in mates:
        pl.semaphore_signal(barrier, inc=1, device_id=mate(j, mine), device_id_type=MESH)
    for r in range(4):
        pl.semaphore_signal(barrier, inc=1, device_id=to[r], device_id_type=MESH)
    tiles = part // 128
    table = (count * capacity, tokens)
    row = lax.broadcasted_iota(jnp.int32, table, 0)
    expert = jnp.zeros(table, jnp.int32)
    for m in range(1, count):
        expert = expert + (row >= m * capacity).astype(jnp.int32)
    slot_of = row - capacity * expert
    kept = kept_ref[...].astype(F32)
    is_first = routes_ref[0:1, :] == expert
    is_second = routes_ref[1:2, :] == expert
    chosen = jnp.where(is_first | is_second, 1.0, 0.0) * kept
    square = (tokens, tokens)
    down, across = lax.broadcasted_iota(jnp.int32, square, 0), lax.broadcasted_iota(jnp.int32, square, 1)
    upto = jnp.where(down <= across, 1.0, 0.0).astype(BF)
    nth = jnp.dot(chosen.astype(BF), upto, preferred_element_type=F32)
    pick_full = jnp.where(nth == (slot_of + 1).astype(F32), chosen, 0.0)
    pick = pick_full.astype(BF)
    length = send_ref.shape[3]
    for kind, source in enumerate((tok_ref, grad_ref)):
        for c in range(2):
            for k in range(2):
                begin = c * share + k * part
                picked = jnp.dot(pick, source[:, begin:begin + part], preferred_element_type=F32)
                for j in range(tiles):
                    where = k * count * length + c * tiles + j
                    flat[pl.ds(where, count * capacity, stride=2 * tiles), :] = picked[:, j * 128:(j + 1) * 128]
        for k in range(2):
            for i in range(count):
                begin = (k * count + i) * length
                send_ref[kind, k, i] = flat[begin:begin + length, :].astype(BF)

    logits = dot_nt(router_ref[...], tok_ref[...])
    ids = lax.broadcasted_iota(jnp.int32, (count, tokens), 0)
    first_hot = jnp.where(routes_ref[0:1, :] == ids, 1.0, 0.0)
    second_hot = jnp.where(routes_ref[1:2, :] == ids, 1.0, 0.0)
    first_logit = jnp.sum(logits * first_hot, axis=0, keepdims=True)
    second_logit = jnp.sum(logits * second_hot, axis=0, keepdims=True)
    gate_first = jax.nn.sigmoid(first_logit - second_logit)
    gate_second = jax.nn.sigmoid(second_logit - first_logit)
    eye = jnp.where(down == across, 1.0, 0.0).astype(BF)
    gate_of = jnp.where(is_first, gate_first, gate_second)
    weigh = dot_nt(eye, (pick_full * gate_of).astype(BF)).astype(BF)
    keep_column = dot_nt(eye, jnp.broadcast_to(kept, (128, tokens)).astype(BF))[:, 0:1]

    pl.semaphore_wait(barrier, len(mates) + 4)

    my_slot = column_slot(0, True)
    own_copies = [
        pltpu.make_async_copy(send_ref.at[own_kind, k, e], got.at[k, my_slot], in_own.at[k]) for k in range(2)
    ]

    def bring(k, j, mine):
        return pltpu.make_async_remote_copy(
            src_ref=send_ref.at[own_kind if mine else 1 - own_kind, k, rem(e + j, count)],
            dst_ref=got.at[k, my_slot],
            send_sem=in_send.at[k], recv_sem=in_recv.at[k],
            device_id=mate(j, mine), device_id_type=MESH,
        )

    def bulk(ref, send_sem, recv_sem):
        return pltpu.make_async_remote_copy(
            src_ref=ref, dst_ref=ref, send_sem=send_sem, recv_sem=recv_sem, device_id=to[0], device_id_type=MESH
        )

    def brought(k):
        return bulk(got.at[k, pl.ds(0, len(mates))], in_send.at[k], in_recv.at[k])

    for k in range(2):
        own_copies[k].start()
        for j, mine in mates:
            bring(k, j, mine).start()
    for load in loads:
        load.start()

    def held(r, s):
        c = r // 2
        return rem(spot[c] + RING - s, RING) if r % 2 == 0 else rem(spot[c] + s, RING)

    def gather(r, s, k, where):
        block = xs.at[r // 2, where, :, pl.ds(k * part, part)]
        return pltpu.make_async_remote_copy(
            src_ref=block, dst_ref=block, send_sem=ag_send.at[r], recv_sem=ag_recv.at[r % 2, s, k],
            device_id=to[r], device_id_type=MESH,
        )

    for k in range(2):
        own_copies[k].wait()
        brought(k).wait_recv()
        length = got.shape[2]
        for i in range(2 * count):
            flat[i * length:(i + 1) * length, :] = got[k, i].astype(F32)
        for c in range(2):
            for j in range(tiles):
                block = flat[pl.ds(c * tiles + j, rows, stride=2 * tiles), :]
                begin = k * part + j * 128
                xs[c, spot[c], :, begin:begin + 128] = block.astype(BF)
        for r in range(4):
            gather(r, 1, k, spot[r // 2]).start()
    for load in loads:
        load.wait()

    def forward(c, kind, low, high, each):
        begin = pl.multiple_of(c * share, share)

        def positions(parity):
            runs = [run + rem(run + parity, 2) for run in (low + 2 * RING, high + 2 * RING)]
            return [div(rem(run + 2 * i, RING), 2) for run in runs for i in range(each)]

        @pl.when(kind == 0)
        def _():
            where = positions(0)
            lhs = jnp.concatenate([xs[c, 2 * t] for t in where], axis=0)
            gate = jnp.dot(lhs, wg[pl.ds(begin, share), :], preferred_element_type=F32)
            up = jnp.dot(lhs, wu[pl.ds(begin, share), :], preferred_element_type=F32)
            for i, t in enumerate(where):
                acc_t[c, t, :, :hidden] = gate[i * rows:(i + 1) * rows]
                acc_t[c, t, :, hidden:] = up[i * rows:(i + 1) * rows]

        @pl.when(kind == 1)
        def _():
            where = positions(1)
            lhs = jnp.concatenate([xs[c, 2 * t + 1] for t in where], axis=0)
            grad = dot_nt(lhs, wd[c])
            for i, t in enumerate(where):
                acc_g[c, t] = grad[i * rows:(i + 1) * rows]

    def forward_unit(unit):
        b = div(unit, 4)
        c = div(rem(unit, 4), 2)
        p = spot[0] * (1 - c) + spot[1] * c
        forward(c, rem(unit, 2), p - GROUP * (b + 1), p + GROUP * b, 2)

    def forward_half(unit):
        h = div(unit, 4)
        c = div(rem(unit, 4), 2)
        p = spot[0] * (1 - c) + spot[1] * c
        forward(c, rem(unit, 2), p - (HOPS - 2) - 2 * h, p + HOPS - GROUP + 2 * h, 1)

    def half_units(begin, end):
        def body(u, carry):
            forward_half(u)
            return carry

        lax.fori_loop(begin, end, body, 0)

    def gathered(d, s, k):
        return bulk(local.at[0, pl.ds(0, 2)], ag_send.at[d], ag_recv.at[d, s, k])

    def ag_step(s, carry):
        for k in range(2):
            for d in range(2):
                gathered(d, s, k).wait_recv()
                for r in (d, d + 2):
                    if d == k:
                        gather(r, s + 1, k, held(r, s)).start()
                    else:
                        @pl.when(s < HOPS - 1)
                        def _():
                            gather(r, s + 1, k, held(r, s)).start()

        @pl.when(s >= GROUP)
        def _():
            forward_unit(s - GROUP)

        @pl.when(s >= HOPS - 2)
        def _():
            half_units(2 * (s - (HOPS - 2)), 2 * (s - (HOPS - 2)) + 2)

        return carry

    lax.fori_loop(1, HOPS, ag_step, 0)
    for d in range(2):
        gathered(d, HOPS, d).wait_recv()

    half_units(4, 8)

    ones = jnp.ones((8, 128), F32)
    for pair in range(16):
        pz, px = pair // 2, 2 * (pair % 2)
        holders = [(pz, px), (pz, px + 1)]
        if (px + pz) % 2:
            holders = holders[::-1]
        t = [place(c, *holders[0]) // 2 for c in range(2)]
        g = [place(c, *holders[1]) // 2 for c in range(2)]
        pre_gate = acc_t[0, t[0], :, :hidden] + acc_t[1, t[1], :, :hidden]
        pre_up = acc_t[0, t[0], :, hidden:] + acc_t[1, t[1], :, hidden:]
        grad_hidden = acc_g[0, g[0]] + acc_g[1, g[1]]
        sigma = jax.nn.sigmoid(pre_gate)
        act = pre_gate * sigma
        inner = grad_hidden * act * pre_up
        grad_gate = (grad_hidden * pre_up * sigma * (1.0 + pre_gate * (1.0 - sigma))).astype(BF)
        grad_up = (grad_hidden * act).astype(BF)
        for c in range(2):
            for q in (2 * t[c], 2 * g[c] + 1):
                grads[c, q, :, :hidden] = grad_gate
                grads[c, q, :, hidden:] = grad_up
        folded = inner[:, 0:128]
        for i in range(1, hidden // 128):
            folded = folded + inner[:, i * 128:(i + 1) * 128]
        sums = dot_nt(ones, folded, precision=lax.Precision.HIGHEST)
        for q in (2 * t[0], 2 * g[0] + 1):
            dots[q, :, :rows] = sums

    def dest(r, s):
        c = r // 2
        return rem(spot[c] + HOPS + RING - s, RING) if r % 2 == 0 else rem(spot[c] + HOPS + s, RING)

    def backward_unit(unit):
        b = div(unit, 4)
        c = div(rem(unit, 4), 2)
        kind = rem(unit, 2)
        p = spot[0] * (1 - c) + spot[1] * c
        low = p + HOPS + RING - GROUP * b - (GROUP - 1)
        low = low + rem(low + kind, 2)
        high = p + HOPS + GROUP * b + 1
        high = high + rem(high + kind, 2)
        where = [2 * div(rem(q, RING), 2) + kind for q in (low, low + 2, high, high + 2)]
        lhs = jnp.concatenate([grads[c, q] for q in where], axis=0)
        begin = pl.multiple_of(kind * half + c * part, part)
        y = dot_nt(lhs[:, :hidden], wg[pl.ds(begin, part), :]) + dot_nt(lhs[:, hidden:], wu[pl.ds(begin, part), :])
        for i in range(GROUP):
            local[c, where[i]] = y[i * rows:(i + 1) * rows].astype(local.dtype)

    cut = part // CUTS
    mine_of = [[d * (CUTS // 2) + i for i in range(CUTS // 2)] for d in range(2)]

    def scatter(r, s, k, src=None, opening=False):
        lanes = pl.ds(k * cut, cut)
        return pltpu.make_async_remote_copy(
            src_ref=running.at[r, s - 1, :, lanes] if src is None else src, dst_ref=running.at[r, s, :, lanes],
            send_sem=(rs_first if opening else rs_send).at[r], recv_sem=rs_recv.at[r % 2, s, k],
            device_id=to[r], device_id_type=MESH,
        )

    def scatter_local(r, s, k):
        lanes = pl.ds(k * cut, cut)
        src = first.at[r // 2, :, lanes] if s == 0 else local.at[r // 2, dest(r, s), :, lanes]
        return scatter(r, s, k, src, s == 0)

    def scattered(d, s, k):
        return bulk(running.at[pl.ds(0, 2), 0, :, pl.ds(0, cut)], rs_send.at[d], rs_recv.at[d, s, k])

    def add_local(r, s, k):
        lanes = slice(k * cut, (k + 1) * cut)
        total = running[r, s - 1, :, lanes].astype(F32) + local[r // 2, dest(r, s), :, lanes].astype(F32)
        running[r, s - 1, :, lanes] = total.astype(BF)

    def dot_copy(d, s, src):
        return pltpu.make_async_remote_copy(
            src_ref=src, dst_ref=dot_slots.at[d, s], send_sem=dot_send.at[d], recv_sem=dot_recv.at[s],
            device_id=to[d], device_id_type=MESH,
        )

    def dotted(s, copies):
        return bulk(dots.at[pl.ds(0, copies)], dot_send.at[0], dot_recv.at[s])

    def head_unit(u, carry):
        backward_unit(u)
        return carry

    for c in range(2):
        q = dest(2 * c, 0)
        begin = pl.multiple_of(rem(q, 2) * half + c * part, part)
        y = dot_nt(grads[c, q, :, :hidden], wg[pl.ds(begin, part), :])
        y = y + dot_nt(grads[c, q, :, hidden:], wu[pl.ds(begin, part), :])
        first[c] = y.astype(BF)
        for r in (2 * c, 2 * c + 1):
            for k in mine_of[r % 2]:
                scatter_local(r, 0, k).start()
    for c in range(2):
        lax.fori_loop(2 * c, 2 * c + 2, head_unit, 0)
        for r in (2 * c, 2 * c + 1):
            for k in mine_of[1 - r % 2]:
                scatter_local(r, 1, k).start()
    dot_copy(0, 0, dots.at[dest(0, 0)]).start()
    dot_copy(1, 1, dots.at[dest(1, 1)]).start()
    backward_unit(jnp.int32(GROUP))

    for i in range(CUTS // 2):
        for d in range(2):
            k = mine_of[d][i]
            scattered(d, 0, k).wait_recv()
            for r in (d, d + 2):
                add_local(r, 1, k)
                scatter(r, 1, k).start()
    dotted(0, 1).wait_recv()
    dot_slots[0, 0] = dot_slots[0, 0] + dots[dest(0, 1)]
    dot_copy(0, 1, dot_slots.at[0, 0]).start()
    backward_unit(jnp.int32(GROUP + 1))

    def rs_step(s, carry):
        for turn in range(CUTS):
            for d in range(2):
                k = (mine_of[1 - d] + mine_of[d])[turn]
                scattered(d, s - 1, k).wait_recv()
                for r in (d, d + 2):
                    add_local(r, s, k)
                    scatter(r, s, k).start()
        dotted(s - 1, 2).wait_recv()
        for d in range(2):
            dot_slots[d, s - 1] = dot_slots[d, s - 1] + dots[dest(d, s)]
            dot_copy(d, s, dot_slots.at[d, s - 1]).start()

        @pl.when(s < HOPS - GROUP)
        def _():
            backward_unit(s + GROUP)

        return carry

    lax.fori_loop(2, HOPS, rs_step, 0)
    def giveback(i, j, mine, src, dst):
        return pltpu.make_async_remote_copy(
            src_ref=src, dst_ref=dst,
            send_sem=out_send.at[i], recv_sem=out_recv.at[i],
            device_id=mate(j, mine), device_id_type=MESH,
        )

    returned = [
        bulk(ref.at[pl.ds(0, len(mates))], out_send.at[i], out_recv.at[i]) for i, ref in enumerate((leave, dots))
    ]
    finals = [
        pltpu.make_async_copy(leave.at[my_slot], back_ref.at[own_kind, e], out_own.at[0]),
        pltpu.make_async_copy(dot_out, back_dots.at[own_kind, e], out_own.at[1]),
    ]

    last = HOPS - 1
    tiles = part // 128
    for k in range(CUTS):
        for d in range(2):
            scattered(d, last, k).wait_recv()
        for c in range(2):
            lanes = slice(k * cut, (k + 1) * cut)
            total = running[2 * c, last, :, lanes].astype(F32) + running[2 * c + 1, last, :, lanes].astype(F32)
            total = total + local[c, spot[c], :, lanes].astype(F32)
            for j in range(tiles // CUTS):
                line = c * tiles + k * (tiles // CUTS) + j
                flat[pl.ds(line, rows, stride=2 * tiles), :] = total[:, j * 128:(j + 1) * 128]
    dotted(last, 2).wait_recv()
    dot_out[...] = dot_slots[0, last] + dot_slots[1, last] + dots[spot[0]]
    finals[1].start()
    for j, mine in mates:
        giveback(1, j, mine, dot_out, back_dots.at[own_kind, e]).start()
    length = leave.shape[1]
    for i in range(2 * count):
        leave[i] = flat[i * length:(i + 1) * length, :].astype(BF)
    finals[0].start()
    for j, mine in mates:
        giveback(0, j, mine, leave.at[column_slot(j, mine)], back_ref.at[own_kind, e]).start()

    for k in range(2):
        brought(k).wait_send()
    for r in range(4):
        bulk(local.at[0, pl.ds(0, 2 * HOPS - 1)], ag_send.at[r], ag_recv.at[0, 0, 0]).wait_send()
        bulk(local.at[0, 0, :, pl.ds(0, part // 2)], rs_first.at[r], rs_recv.at[0, 0, 0]).wait_send()
        bulk(local.at[0, pl.ds(0, HOPS - 1)], rs_send.at[r], rs_recv.at[0, 0, 0]).wait_send()
    for d in range(2):
        bulk(dots.at[pl.ds(0, HOPS - d)], dot_send.at[d], dot_recv.at[0]).wait_send()
    returned[1].wait_send()
    finals[1].wait()
    returned[1].wait_recv()
    for i in range(count):
        flat[i * capacity:(i + 1) * capacity, :] = back_dots[0, i, 0:capacity, :]
    lane = lax.broadcasted_iota(jnp.int32, (count * capacity, 128), 1)
    row = lax.broadcasted_iota(jnp.int32, (count * capacity, 128), 0)
    wanted = row + capacity * my_slot
    for m in range(1, count):
        wanted = wanted - capacity * (row >= m * capacity).astype(jnp.int32)
    dot_column = jnp.where(lane == wanted, flat[0:count * capacity, :], 0.0)
    dot_column = jnp.sum(dot_column, axis=1, keepdims=True)
    dot_first = jnp.sum(jnp.where(is_first, pick_full, 0.0) * dot_column, axis=0, keepdims=True)
    dot_second = jnp.sum(jnp.where(is_second, pick_full, 0.0) * dot_column, axis=0, keepdims=True)
    product = gate_first * gate_second * kept
    grad_first = product * (dot_first - dot_second)
    grad_second = product * (dot_second - dot_first)
    gate_grad_ref[0:1, :] = grad_first
    gate_grad_ref[1:2, :] = grad_second
    logit_grad = first_hot * grad_first + second_hot * grad_second
    high = logit_grad.astype(BF)
    low = (logit_grad - high.astype(F32)).astype(BF)
    pieces = jnp.concatenate([dot_nt(eye, high), dot_nt(eye, low)], axis=0).astype(BF)
    returned[0].wait_send()
    finals[0].wait()
    returned[0].wait_recv()
    for kind in range(2):
        for i in range(count):
            flat[i * length:(i + 1) * length, :] = back_ref[kind, i].astype(F32)
        parts = [flat[pl.ds(i, count * capacity, stride=2 * tiles), :].astype(BF) for i in range(2 * tiles)]
        total = jnp.dot(weigh, jnp.concatenate(parts, axis=1), preferred_element_type=F32)
        lanes = slice(kind * half, (kind + 1) * half)
        term = jnp.dot(pieces, router_ref[:, lanes], preferred_element_type=F32)
        out_ref[:, lanes] = ((total + (term[:tokens] + term[tokens:])) * keep_column).astype(BF)


def run_experts(count, routes, kept, router, tokens, out_grad, gate_weight, up_weight, down_weight):
    width, hidden = gate_weight.shape[1:]
    share, part = width // 2, width // 4
    capacity = 3 * tokens.shape[0] // 8
    length = capacity * 2 * part // 128
    rows = 2 * count * capacity
    vmem = pl.BlockSpec(memory_space=pltpu.VMEM)
    hbm = pl.BlockSpec(memory_space=pl.ANY)
    return pl.pallas_call(
        experts_kernel,
        out_shape=(
            jax.ShapeDtypeStruct(tokens.shape, BF),
            jax.ShapeDtypeStruct(routes.shape, F32),
        ),
        in_specs=[vmem, vmem, vmem, vmem, vmem, hbm, hbm, hbm],
        out_specs=(vmem, vmem),
        scratch_shapes=[
            pltpu.VMEM((2, count, length, 128), BF),
            pltpu.VMEM((2, count, 8, 128), F32),
            pltpu.VMEM((2, 2, count, length, 128), BF),
            pltpu.VMEM((2, 2 * count, length, 128), BF),
            pltpu.VMEM((2 * count * length, 128), F32),
            pltpu.VMEM((2 * count, length, 128), BF),
            pltpu.VMEM((2, RING, rows, share), BF),
            pltpu.VMEM((4, HOPS, rows, part), BF),
            pltpu.VMEM((2, rows, part), BF),
            pltpu.VMEM((2, RING, rows, part), BF),
            pltpu.VMEM((2, 16, rows, 2 * hidden), F32),
            pltpu.VMEM((2, 16, rows, hidden), F32),
            pltpu.VMEM((2, RING, rows, 2 * hidden), BF),
            pltpu.VMEM((RING, 8, 128), F32),
            pltpu.VMEM((2, HOPS, 8, 128), F32),
            pltpu.VMEM((8, 128), F32),
            pltpu.VMEM((width, hidden), BF),
            pltpu.VMEM((width, hidden), BF),
            pltpu.VMEM((2, hidden, share), BF),
            pltpu.SemaphoreType.DMA((4,)),
            pltpu.SemaphoreType.DMA((2,)),
            pltpu.SemaphoreType.DMA((2,)),
            pltpu.SemaphoreType.DMA((2,)),
            pltpu.SemaphoreType.DMA((4,)),
            pltpu.SemaphoreType.DMA((2, HOPS + 1, 2)),
            pltpu.SemaphoreType.DMA((4,)),
            pltpu.SemaphoreType.DMA((4,)),
            pltpu.SemaphoreType.DMA((2, HOPS, CUTS)),
            pltpu.SemaphoreType.DMA((2,)),
            pltpu.SemaphoreType.DMA((HOPS,)),
            pltpu.SemaphoreType.DMA((2,)),
            pltpu.SemaphoreType.DMA((2,)),
            pltpu.SemaphoreType.DMA((2,)),
        ],
        compiler_params=pltpu.CompilerParams(
            collective_id=0, has_side_effects=True, vmem_limit_bytes=63 << 20
        ),
        name="experts",
    )(routes, kept, router, tokens, out_grad, gate_weight, up_weight, down_weight)


def on_device(tokens, out_grad, kept_mask, routes, router, gate_weight, up_weight, down_weight):
    d_tokens, gate_grad = run_experts(
        lax.axis_size("expert"), routes.T, kept_mask[None], router.T, tokens, out_grad,
        gate_weight, up_weight, down_weight,
    )
    return (d_tokens, gate_grad.T)


def solution(mesh):
    return jax.shard_map(
        on_device,
        mesh=mesh,
        in_specs=(
            P(("seq", "expert", "mp"), None),
            P(("seq", "expert", "mp"), None),
            P(("seq", "expert", "mp")),
            P(("seq", "expert", "mp"), None),
            P(),
            P("expert", None, ("seq", "mp")),
            P("expert", None, ("seq", "mp")),
            P("expert", ("seq", "mp"), None),
        ),
        out_specs=(P(("seq", "expert", "mp"), None), P(("seq", "expert", "mp"), None)),
        check_vma=False,
    )
```

```python
import functools

import jax
import jax.numpy as jnp
from jax import lax
from jax.experimental import pallas as pl
from jax.experimental.pallas import tpu as pltpu
from jax.sharding import PartitionSpec as P

MESH = pl.DeviceIdType.MESH
BF = jnp.bfloat16
F32 = jnp.float32
RING = 32
HOPS = 16
GROUP = 4
CUTS = 6


def div(a, b):
    return a // b if isinstance(a, int) else lax.div(a, jnp.int32(b))


def rem(a, b):
    return a % b if isinstance(a, int) else lax.rem(a, jnp.int32(b))


def place(cycle, z, x):
    if cycle == 0:
        return 4 * z + rem(x + z, 4)
    turn = rem(z + 5 * x, 8)
    return 4 * x + 16 * div(turn, 4) + rem(turn, 4)


def coords(cycle, q):
    a, b = div(q, 4), rem(q, 4)
    if cycle == 0:
        return a, rem(b - a + 8, 4)
    return rem(3 * a + b, 8), rem(a, 4)


def peer(z, x):
    return {"seq": z, "mp": x}


def dot_nt(a, b, **kwargs):
    return lax.dot_general(a, b, (((1,), (1,)), ((), ())), preferred_element_type=F32, **kwargs)


def experts_kernel(
    routes_ref, kept_ref, router_ref, tok_ref, grad_ref, wg_hbm, wu_hbm, wd_hbm, out_ref, gate_grad_ref,
    back_ref, back_dots, send_ref, got, flat, leave, xs, running, first, local, acc_t, acc_g, grads, dots, dot_slots, dot_out, wg, wu, wd,
    w_sem, in_own, in_send, in_recv, ag_send, ag_recv, rs_first, rs_send, rs_recv, dot_send, dot_recv,
    out_own, out_send, out_recv,
):
    count = send_ref.shape[2]
    tokens = tok_ref.shape[0]
    capacity = 3 * tokens // 8
    rows, share = xs.shape[2], xs.shape[3]
    hidden = wg.shape[1]
    part = share // 2
    half = 2 * part
    z, e, x = lax.axis_index("seq"), lax.axis_index("expert"), lax.axis_index("mp")
    other = x + 1 - 2 * rem(x, 2)
    own_kind = rem(x + z, 2)
    spot = [place(c, z, x) for c in range(2)]
    after = [coords(c, rem(spot[c] + 1, RING)) for c in range(2)]
    before = [coords(c, rem(spot[c] + RING - 1, RING)) for c in range(2)]
    to = [peer(*after[0]), peer(*before[0]), peer(*after[1]), peer(*before[1])]

    mates = [(j, mine) for j in range(count) for mine in (True, False) if j or not mine]

    def mate(j, mine):
        return {"seq": z, "expert": rem(e + j, count), "mp": x if mine else other}

    def column_slot(j, mine):
        return rem(x if mine else other, 2) * count + rem(e + j, count)

    loads = [
        pltpu.make_async_copy(wg_hbm.at[0], wg, w_sem.at[0]),
        pltpu.make_async_copy(wu_hbm.at[0], wu, w_sem.at[1]),
    ]
    for c in range(2):
        loads.append(pltpu.make_async_copy(wd_hbm.at[0, :, pl.ds(c * share, share)], wd.at[c], w_sem.at[2 + c]))

    barrier = pltpu.get_barrier_semaphore()
    for j, mine in mates:
        pl.semaphore_signal(barrier, inc=1, device_id=mate(j, mine), device_id_type=MESH)
    for r in range(4):
        pl.semaphore_signal(barrier, inc=1, device_id=to[r], device_id_type=MESH)
    tiles = part // 128
    table = (count * capacity, tokens)
    row = lax.broadcasted_iota(jnp.int32, table, 0)
    expert = jnp.zeros(table, jnp.int32)
    for m in range(1, count):
        expert = expert + (row >= m * capacity).astype(jnp.int32)
    slot_of = row - capacity * expert
    kept = kept_ref[...].astype(F32)
    is_first = routes_ref[0:1, :] == expert
    is_second = routes_ref[1:2, :] == expert
    chosen = jnp.where(is_first | is_second, 1.0, 0.0) * kept
    square = (tokens, tokens)
    down, across = lax.broadcasted_iota(jnp.int32, square, 0), lax.broadcasted_iota(jnp.int32, square, 1)
    upto = jnp.where(down <= across, 1.0, 0.0).astype(BF)
    nth = jnp.dot(chosen.astype(BF), upto, preferred_element_type=F32)
    pick_full = jnp.where(nth == (slot_of + 1).astype(F32), chosen, 0.0)
    pick = pick_full.astype(BF)
    length = send_ref.shape[3]
    for kind, source in enumerate((tok_ref, grad_ref)):
        for c in range(2):
            for k in range(2):
                begin = c * share + k * part
                picked = jnp.dot(pick, source[:, begin:begin + part], preferred_element_type=F32)
                for j in range(tiles):
                    where = k * count * length + c * tiles + j
                    flat[pl.ds(where, count * capacity, stride=2 * tiles), :] = picked[:, j * 128:(j + 1) * 128]
        for k in range(2):
            for i in range(count):
                begin = (k * count + i) * length
                send_ref[kind, k, i] = flat[begin:begin + length, :].astype(BF)

    logits = dot_nt(router_ref[...], tok_ref[...])
    ids = lax.broadcasted_iota(jnp.int32, (count, tokens), 0)
    first_hot = jnp.where(routes_ref[0:1, :] == ids, 1.0, 0.0)
    second_hot = jnp.where(routes_ref[1:2, :] == ids, 1.0, 0.0)
    first_logit = jnp.sum(logits * first_hot, axis=0, keepdims=True)
    second_logit = jnp.sum(logits * second_hot, axis=0, keepdims=True)
    gate_first = jax.nn.sigmoid(first_logit - second_logit)
    gate_second = jax.nn.sigmoid(second_logit - first_logit)
    eye = jnp.where(down == across, 1.0, 0.0).astype(BF)
    gate_of = jnp.where(is_first, gate_first, gate_second)
    weigh = dot_nt(eye, (pick_full * gate_of).astype(BF)).astype(BF)
    keep_column = dot_nt(eye, jnp.broadcast_to(kept, (128, tokens)).astype(BF))[:, 0:1]

    pl.semaphore_wait(barrier, len(mates) + 4)

    my_slot = column_slot(0, True)
    own_copies = [
        pltpu.make_async_copy(send_ref.at[own_kind, k, e], got.at[k, my_slot], in_own.at[k]) for k in range(2)
    ]

    def bring(k, j, mine):
        return pltpu.make_async_remote_copy(
            src_ref=send_ref.at[own_kind if mine else 1 - own_kind, k, rem(e + j, count)],
            dst_ref=got.at[k, my_slot],
            send_sem=in_send.at[k], recv_sem=in_recv.at[k],
            device_id=mate(j, mine), device_id_type=MESH,
        )

    def bulk(ref, send_sem, recv_sem):
        return pltpu.make_async_remote_copy(
            src_ref=ref, dst_ref=ref, send_sem=send_sem, recv_sem=recv_sem, device_id=to[0], device_id_type=MESH
        )

    def brought(k):
        return bulk(got.at[k, pl.ds(0, len(mates))], in_send.at[k], in_recv.at[k])

    for k in range(2):
        own_copies[k].start()
        for j, mine in mates:
            bring(k, j, mine).start()
    for load in loads:
        load.start()

    def held(r, s):
        c = r // 2
        return rem(spot[c] + RING - s, RING) if r % 2 == 0 else rem(spot[c] + s, RING)

    def gather(r, s, k, where):
        block = xs.at[r // 2, where, :, pl.ds(k * part, part)]
        return pltpu.make_async_remote_copy(
            src_ref=block, dst_ref=block, send_sem=ag_send.at[r], recv_sem=ag_recv.at[r % 2, s, k],
            device_id=to[r], device_id_type=MESH,
        )

    for k in range(2):
        own_copies[k].wait()
        brought(k).wait_recv()
        length = got.shape[2]
        for i in range(2 * count):
            flat[i * length:(i + 1) * length, :] = got[k, i].astype(F32)
        for c in range(2):
            for j in range(tiles):
                block = flat[pl.ds(c * tiles + j, rows, stride=2 * tiles), :]
                begin = k * part + j * 128
                xs[c, spot[c], :, begin:begin + 128] = block.astype(BF)
        for r in range(4):
            gather(r, 1, k, spot[r // 2]).start()
    for load in loads:
        load.wait()

    def forward(c, kind, low, high, each):
        begin = pl.multiple_of(c * share, share)

        def positions(parity):
            runs = [run + rem(run + parity, 2) for run in (low + 2 * RING, high + 2 * RING)]
            return [div(rem(run + 2 * i, RING), 2) for run in runs for i in range(each)]

        @pl.when(kind == 0)
        def _():
            where = positions(0)
            lhs = jnp.concatenate([xs[c, 2 * t] for t in where], axis=0)
            gate = jnp.dot(lhs, wg[pl.ds(begin, share), :], preferred_element_type=F32)
            up = jnp.dot(lhs, wu[pl.ds(begin, share), :], preferred_element_type=F32)
            for i, t in enumerate(where):
                acc_t[c, t, :, :hidden] = gate[i * rows:(i + 1) * rows]
                acc_t[c, t, :, hidden:] = up[i * rows:(i + 1) * rows]

        @pl.when(kind == 1)
        def _():
            where = positions(1)
            lhs = jnp.concatenate([xs[c, 2 * t + 1] for t in where], axis=0)
            grad = dot_nt(lhs, wd[c])
            for i, t in enumerate(where):
                acc_g[c, t] = grad[i * rows:(i + 1) * rows]

    def forward_unit(unit):
        b = div(unit, 4)
        c = div(rem(unit, 4), 2)
        p = spot[0] * (1 - c) + spot[1] * c
        forward(c, rem(unit, 2), p - GROUP * (b + 1), p + GROUP * b, 2)

    def forward_half(unit):
        h = div(unit, 4)
        c = div(rem(unit, 4), 2)
        p = spot[0] * (1 - c) + spot[1] * c
        forward(c, rem(unit, 2), p - (HOPS - 2) - 2 * h, p + HOPS - GROUP + 2 * h, 1)

    def half_units(begin, end):
        def body(u, carry):
            forward_half(u)
            return carry

        lax.fori_loop(begin, end, body, 0)

    def gathered(d, s, k):
        return bulk(local.at[0, pl.ds(0, 2)], ag_send.at[d], ag_recv.at[d, s, k])

    def ag_step(s, carry):
        for k in range(2):
            for d in range(2):
                gathered(d, s, k).wait_recv()
                for r in (d, d + 2):
                    if d == k:
                        gather(r, s + 1, k, held(r, s)).start()
                    else:
                        @pl.when(s < HOPS - 1)
                        def _():
                            gather(r, s + 1, k, held(r, s)).start()

        @pl.when(s >= GROUP)
        def _():
            forward_unit(s - GROUP)

        @pl.when(s >= HOPS - 2)
        def _():
            half_units(2 * (s - (HOPS - 2)), 2 * (s - (HOPS - 2)) + 2)

        return carry

    lax.fori_loop(1, HOPS, ag_step, 0)
    for d in range(2):
        gathered(d, HOPS, d).wait_recv()

    half_units(4, 8)

    ones = jnp.ones((8, 128), F32)
    for pair in range(16):
        pz, px = pair // 2, 2 * (pair % 2)
        holders = [(pz, px), (pz, px + 1)]
        if (px + pz) % 2:
            holders = holders[::-1]
        t = [place(c, *holders[0]) // 2 for c in range(2)]
        g = [place(c, *holders[1]) // 2 for c in range(2)]
        pre_gate = acc_t[0, t[0], :, :hidden] + acc_t[1, t[1], :, :hidden]
        pre_up = acc_t[0, t[0], :, hidden:] + acc_t[1, t[1], :, hidden:]
        grad_hidden = acc_g[0, g[0]] + acc_g[1, g[1]]
        sigma = jax.nn.sigmoid(pre_gate)
        act = pre_gate * sigma
        inner = grad_hidden * act * pre_up
        grad_gate = (grad_hidden * pre_up * sigma * (1.0 + pre_gate * (1.0 - sigma))).astype(BF)
        grad_up = (grad_hidden * act).astype(BF)
        for c in range(2):
            for q in (2 * t[c], 2 * g[c] + 1):
                grads[c, q, :, :hidden] = grad_gate
                grads[c, q, :, hidden:] = grad_up
        folded = inner[:, 0:128]
        for i in range(1, hidden // 128):
            folded = folded + inner[:, i * 128:(i + 1) * 128]
        sums = dot_nt(ones, folded, precision=lax.Precision.HIGHEST)
        for q in (2 * t[0], 2 * g[0] + 1):
            dots[q, :, :rows] = sums

    def dest(r, s):
        c = r // 2
        return rem(spot[c] + HOPS + RING - s, RING) if r % 2 == 0 else rem(spot[c] + HOPS + s, RING)

    def backward_unit(unit):
        b = div(unit, 4)
        c = div(rem(unit, 4), 2)
        kind = rem(unit, 2)
        p = spot[0] * (1 - c) + spot[1] * c
        low = p + HOPS + RING - GROUP * b - (GROUP - 1)
        low = low + rem(low + kind, 2)
        high = p + HOPS + GROUP * b + 1
        high = high + rem(high + kind, 2)
        where = [2 * div(rem(q, RING), 2) + kind for q in (low, low + 2, high, high + 2)]
        lhs = jnp.concatenate([grads[c, q] for q in where], axis=0)
        begin = pl.multiple_of(kind * half + c * part, part)
        y = dot_nt(lhs[:, :hidden], wg[pl.ds(begin, part), :]) + dot_nt(lhs[:, hidden:], wu[pl.ds(begin, part), :])
        for i in range(GROUP):
            local[c, where[i]] = y[i * rows:(i + 1) * rows].astype(local.dtype)

    cut = part // CUTS
    mine_of = [[d * (CUTS // 2) + i for i in range(CUTS // 2)] for d in range(2)]

    def scatter(r, s, k, src=None, opening=False):
        lanes = pl.ds(k * cut, cut)
        return pltpu.make_async_remote_copy(
            src_ref=running.at[r, s - 1, :, lanes] if src is None else src, dst_ref=running.at[r, s, :, lanes],
            send_sem=(rs_first if opening else rs_send).at[r], recv_sem=rs_recv.at[r % 2, s, k],
            device_id=to[r], device_id_type=MESH,
        )

    def scatter_local(r, s, k):
        lanes = pl.ds(k * cut, cut)
        src = first.at[r // 2, :, lanes] if s == 0 else local.at[r // 2, dest(r, s), :, lanes]
        return scatter(r, s, k, src, s == 0)

    def scattered(d, s, k):
        return bulk(running.at[pl.ds(0, 2), 0, :, pl.ds(0, cut)], rs_send.at[d], rs_recv.at[d, s, k])

    def add_local(r, s, k):
        lanes = slice(k * cut, (k + 1) * cut)
        total = running[r, s - 1, :, lanes].astype(F32) + local[r // 2, dest(r, s), :, lanes].astype(F32)
        running[r, s - 1, :, lanes] = total.astype(BF)

    def dot_copy(d, s, src):
        return pltpu.make_async_remote_copy(
            src_ref=src, dst_ref=dot_slots.at[d, s], send_sem=dot_send.at[d], recv_sem=dot_recv.at[s],
            device_id=to[d], device_id_type=MESH,
        )

    def dotted(s, copies):
        return bulk(dots.at[pl.ds(0, copies)], dot_send.at[0], dot_recv.at[s])

    def head_unit(u, carry):
        backward_unit(u)
        return carry

    for c in range(2):
        q = dest(2 * c, 0)
        begin = pl.multiple_of(rem(q, 2) * half + c * part, part)
        y = dot_nt(grads[c, q, :, :hidden], wg[pl.ds(begin, part), :])
        y = y + dot_nt(grads[c, q, :, hidden:], wu[pl.ds(begin, part), :])
        first[c] = y.astype(BF)
        for r in (2 * c, 2 * c + 1):
            for k in mine_of[r % 2]:
                scatter_local(r, 0, k).start()
    for c in range(2):
        lax.fori_loop(2 * c, 2 * c + 2, head_unit, 0)
        for r in (2 * c, 2 * c + 1):
            for k in mine_of[1 - r % 2]:
                scatter_local(r, 1, k).start()
    dot_copy(0, 0, dots.at[dest(0, 0)]).start()
    dot_copy(1, 1, dots.at[dest(1, 1)]).start()
    backward_unit(jnp.int32(GROUP))

    for i in range(CUTS // 2):
        for d in range(2):
            k = mine_of[d][i]
            scattered(d, 0, k).wait_recv()
            for r in (d, d + 2):
                add_local(r, 1, k)
                scatter(r, 1, k).start()
    dotted(0, 1).wait_recv()
    dot_slots[0, 0] = dot_slots[0, 0] + dots[dest(0, 1)]
    dot_copy(0, 1, dot_slots.at[0, 0]).start()
    backward_unit(jnp.int32(GROUP + 1))

    def rs_step(s, carry):
        for turn in range(CUTS):
            for d in range(2):
                k = (mine_of[1 - d] + mine_of[d])[turn]
                scattered(d, s - 1, k).wait_recv()
                for r in (d, d + 2):
                    add_local(r, s, k)
                    scatter(r, s, k).start()
        dotted(s - 1, 2).wait_recv()
        for d in range(2):
            dot_slots[d, s - 1] = dot_slots[d, s - 1] + dots[dest(d, s)]
            dot_copy(d, s, dot_slots.at[d, s - 1]).start()

        @pl.when(s < HOPS - GROUP)
        def _():
            backward_unit(s + GROUP)

        return carry

    lax.fori_loop(2, HOPS, rs_step, 0)
    def giveback(i, j, mine, src, dst):
        return pltpu.make_async_remote_copy(
            src_ref=src, dst_ref=dst,
            send_sem=out_send.at[i], recv_sem=out_recv.at[i],
            device_id=mate(j, mine), device_id_type=MESH,
        )

    returned = [
        bulk(ref.at[pl.ds(0, len(mates))], out_send.at[i], out_recv.at[i]) for i, ref in enumerate((leave, dots))
    ]
    finals = [
        pltpu.make_async_copy(leave.at[my_slot], back_ref.at[own_kind, e], out_own.at[0]),
        pltpu.make_async_copy(dot_out, back_dots.at[own_kind, e], out_own.at[1]),
    ]

    last = HOPS - 1
    tiles = part // 128
    for k in range(CUTS):
        for d in range(2):
            scattered(d, last, k).wait_recv()
        for c in range(2):
            lanes = slice(k * cut, (k + 1) * cut)
            total = running[2 * c, last, :, lanes].astype(F32) + running[2 * c + 1, last, :, lanes].astype(F32)
            total = total + local[c, spot[c], :, lanes].astype(F32)
            for j in range(tiles // CUTS):
                line = c * tiles + k * (tiles // CUTS) + j
                flat[pl.ds(line, rows, stride=2 * tiles), :] = total[:, j * 128:(j + 1) * 128]
    dotted(last, 2).wait_recv()
    dot_out[...] = dot_slots[0, last] + dot_slots[1, last] + dots[spot[0]]
    finals[1].start()
    for j, mine in mates:
        giveback(1, j, mine, dot_out, back_dots.at[own_kind, e]).start()
    length = leave.shape[1]
    for i in range(2 * count):
        leave[i] = flat[i * length:(i + 1) * length, :].astype(BF)
    finals[0].start()
    for j, mine in mates:
        giveback(0, j, mine, leave.at[column_slot(j, mine)], back_ref.at[own_kind, e]).start()

    for k in range(2):
        brought(k).wait_send()
    for r in range(4):
        bulk(local.at[0, pl.ds(0, 2 * HOPS - 1)], ag_send.at[r], ag_recv.at[0, 0, 0]).wait_send()
        bulk(local.at[0, 0, :, pl.ds(0, part // 2)], rs_first.at[r], rs_recv.at[0, 0, 0]).wait_send()
        bulk(local.at[0, pl.ds(0, HOPS - 1)], rs_send.at[r], rs_recv.at[0, 0, 0]).wait_send()
    for d in range(2):
        bulk(dots.at[pl.ds(0, HOPS - d)], dot_send.at[d], dot_recv.at[0]).wait_send()
    returned[1].wait_send()
    finals[1].wait()
    returned[1].wait_recv()
    for i in range(count):
        flat[i * capacity:(i + 1) * capacity, :] = back_dots[0, i, 0:capacity, :]
    lane = lax.broadcasted_iota(jnp.int32, (count * capacity, 128), 1)
    row = lax.broadcasted_iota(jnp.int32, (count * capacity, 128), 0)
    wanted = row + capacity * my_slot
    for m in range(1, count):
        wanted = wanted - capacity * (row >= m * capacity).astype(jnp.int32)
    dot_column = jnp.where(lane == wanted, flat[0:count * capacity, :], 0.0)
    dot_column = jnp.sum(dot_column, axis=1, keepdims=True)
    dot_first = jnp.sum(jnp.where(is_first, pick_full, 0.0) * dot_column, axis=0, keepdims=True)
    dot_second = jnp.sum(jnp.where(is_second, pick_full, 0.0) * dot_column, axis=0, keepdims=True)
    product = gate_first * gate_second * kept
    grad_first = product * (dot_first - dot_second)
    grad_second = product * (dot_second - dot_first)
    gate_grad_ref[0:1, :] = grad_first
    gate_grad_ref[1:2, :] = grad_second
    logit_grad = first_hot * grad_first + second_hot * grad_second
    high = logit_grad.astype(BF)
    low = (logit_grad - high.astype(F32)).astype(BF)
    pieces = jnp.concatenate([dot_nt(eye, high), dot_nt(eye, low)], axis=0).astype(BF)
    returned[0].wait_send()
    finals[0].wait()
    returned[0].wait_recv()
    for kind in range(2):
        for i in range(count):
            flat[i * length:(i + 1) * length, :] = back_ref[kind, i].astype(F32)
        parts = [flat[pl.ds(i, count * capacity, stride=2 * tiles), :].astype(BF) for i in range(2 * tiles)]
        total = jnp.dot(weigh, jnp.concatenate(parts, axis=1), preferred_element_type=F32)
        lanes = slice(kind * half, (kind + 1) * half)
        term = jnp.dot(pieces, router_ref[:, lanes], preferred_element_type=F32)
        out_ref[:, lanes] = ((total + (term[:tokens] + term[tokens:])) * keep_column).astype(BF)


def run_experts(count, routes, kept, router, tokens, out_grad, gate_weight, up_weight, down_weight):
    width, hidden = gate_weight.shape[1:]
    share, part = width // 2, width // 4
    capacity = 3 * tokens.shape[0] // 8
    length = capacity * 2 * part // 128
    rows = 2 * count * capacity
    vmem = pl.BlockSpec(memory_space=pltpu.VMEM)
    hbm = pl.BlockSpec(memory_space=pl.ANY)
    return pl.pallas_call(
        experts_kernel,
        out_shape=(
            jax.ShapeDtypeStruct(tokens.shape, BF),
            jax.ShapeDtypeStruct(routes.shape, F32),
        ),
        in_specs=[vmem, vmem, vmem, vmem, vmem, hbm, hbm, hbm],
        out_specs=(vmem, vmem),
        scratch_shapes=[
            pltpu.VMEM((2, count, length, 128), BF),
            pltpu.VMEM((2, count, 8, 128), F32),
            pltpu.VMEM((2, 2, count, length, 128), BF),
            pltpu.VMEM((2, 2 * count, length, 128), BF),
            pltpu.VMEM((2 * count * length, 128), F32),
            pltpu.VMEM((2 * count, length, 128), BF),
            pltpu.VMEM((2, RING, rows, share), BF),
            pltpu.VMEM((4, HOPS, rows, part), BF),
            pltpu.VMEM((2, rows, part), BF),
            pltpu.VMEM((2, RING, rows, part), BF),
            pltpu.VMEM((2, 16, rows, 2 * hidden), F32),
            pltpu.VMEM((2, 16, rows, hidden), F32),
            pltpu.VMEM((2, RING, rows, 2 * hidden), BF),
            pltpu.VMEM((RING, 8, 128), F32),
            pltpu.VMEM((2, HOPS, 8, 128), F32),
            pltpu.VMEM((8, 128), F32),
            pltpu.VMEM((width, hidden), BF),
            pltpu.VMEM((width, hidden), BF),
            pltpu.VMEM((2, hidden, share), BF),
            pltpu.SemaphoreType.DMA((4,)),
            pltpu.SemaphoreType.DMA((2,)),
            pltpu.SemaphoreType.DMA((2,)),
            pltpu.SemaphoreType.DMA((2,)),
            pltpu.SemaphoreType.DMA((4,)),
            pltpu.SemaphoreType.DMA((2, HOPS + 1, 2)),
            pltpu.SemaphoreType.DMA((4,)),
            pltpu.SemaphoreType.DMA((4,)),
            pltpu.SemaphoreType.DMA((2, HOPS, CUTS)),
            pltpu.SemaphoreType.DMA((2,)),
            pltpu.SemaphoreType.DMA((HOPS,)),
            pltpu.SemaphoreType.DMA((2,)),
            pltpu.SemaphoreType.DMA((2,)),
            pltpu.SemaphoreType.DMA((2,)),
        ],
        compiler_params=pltpu.CompilerParams(
            collective_id=0, has_side_effects=True, vmem_limit_bytes=63 << 20
        ),
        name="experts",
    )(routes, kept, router, tokens, out_grad, gate_weight, up_weight, down_weight)


def on_device(tokens, out_grad, kept_mask, routes, router, gate_weight, up_weight, down_weight):
    d_tokens, gate_grad = run_experts(
        lax.axis_size("expert"), routes.T, kept_mask[None], router.T, tokens, out_grad,
        gate_weight, up_weight, down_weight,
    )
    return (d_tokens, gate_grad.T)


def solution(mesh):
    return jax.shard_map(
        on_device,
        mesh=mesh,
        in_specs=(
            P(("seq", "expert", "mp"), None),
            P(("seq", "expert", "mp"), None),
            P(("seq", "expert", "mp")),
            P(("seq", "expert", "mp"), None),
            P(),
            P("expert", None, ("seq", "mp")),
            P("expert", None, ("seq", "mp")),
            P("expert", ("seq", "mp"), None),
        ),
        out_specs=(P(("seq", "expert", "mp"), None), P(("seq", "expert", "mp"), None)),
        check_vma=False,
    )
```
